256 devices in a mesh: gx: 4 (over x), gy: 8 (over z), gz: 8 (over y, core).
Axes of the slice: x: 4, y: 4, z: 8, core: 2. Of those that a mesh axis runs over, the one named last changes fastest.
Arguments:
- solution_old: float32 [1024, 32, 1024], P(('gx', 'gy', 'gz')), may hold values from -6 to 6
- right_side: float32 [1024, 32, 1024], P(('gx', 'gy', 'gz')), may hold values from -6 to 6
- acoef: float32 [1024, 32, 1024], P(('gx', 'gy', 'gz')), may hold values from 0.05 to 1
- bcoef: float32 [1024, 32, 1024], P(('gx', 'gy', 'gz')), may hold values from 0.25 to 4
- corners: int32 [3, 1024], replicated, may hold values from 0 to 992, as said below
Outputs:
- solution: float32 [128, 256, 1024], P('gx', 'gy', 'gz')
- residual: float32 [128, 256, 1024], P('gx', 'gy', 'gz')
The draws below stay inside these ranges and needn't reach their ends.
Inputs may be any that keep to these rules, and one draw needn't show every extreme that they name: `corners`: each corner is a multiple of 32 in every dimension and the boxes tile the level one to one. The new owner of a box, the device whose block of 32 x 32 x 128 cells holds its corner, has the same gx and gz indices as the device that holds its row. At most one box moves from one device to any other device, and at most min(3, 7) boxes leave or reach one device; in each group of devices with one gx and one gz index, one device swaps a box with each of that many others, and every other device of the group passes one box on along a cycle through them.
All inputs are finite; a program needn't handle non-finite values.
Results may differ from the reference program's by a relative error of at most 0.00002.
Values sent between devices are 32-bit elements; how exact they have to be, the bound alone decides.
No kernel may reach another device: no remote copies, remote signals or barrier semaphores. Data moves between devices by JAX's collectives and lax.ppermute only.
A program may use at most 64 MiB of HBM per device.

```python
import math
import jax
import jax.numpy as jnp
from jax import lax

BOX = 32
BXB = 1
BYB = 1
BZB = 4
SWEEPS = 2
NB = 1024
NX = 128
NY = 256
NZ = 1024
N_GX = 4
N_GY = 8
N_GZ = 8


def draw_corners(key, part):
    group = N_GY
    groups_n = N_GX * N_GZ
    per_dev = BXB * BYB * BZB
    others_n = group - 1
    hot_n = min(per_dev - 1, others_n)
    key_hot, key_order, key_perm = jax.random.split(key, 3)
    hot_dev = jax.random.randint(key_hot, (groups_n,), 0, group).astype(jnp.int32)

    def ordered(one_key):
        return jax.random.permutation(one_key, others_n).astype(jnp.int32)

    def shuffled(one_key):
        return jax.random.permutation(one_key, per_dev).astype(jnp.int32)
    order = jax.vmap(ordered)(jax.random.split(key_order, groups_n))
    order_inv = jnp.argsort(order, axis=1).astype(jnp.int32)
    perms = jax.vmap(shuffled)(jax.random.split(key_perm, groups_n * group)).reshape(groups_n, group, per_dev)
    inverse = jnp.argsort(perms, axis=2).astype(jnp.int32)
    full_shape = (groups_n, group, per_dev)
    group_id = jnp.arange(groups_n, dtype=jnp.int32)[:, None, None]
    device = jnp.broadcast_to(jnp.arange(group, dtype=jnp.int32)[None, :, None], full_shape)
    position = jnp.broadcast_to(jnp.arange(per_dev, dtype=jnp.int32)[None, None, :], full_shape)
    group_full = jnp.broadcast_to(group_id, full_shape)
    hot_here = jnp.broadcast_to(hot_dev[:, None, None], full_shape)
    is_hot = device == hot_here
    rel = (device - hot_here - 1) % group
    cyc = order_inv[group_full, jnp.minimum(rel, others_n - 1)]
    rank = inverse
    src_dev = device
    src_slot = position
    in_set = jnp.logical_not(is_hot) & (cyc < hot_n)
    from_hot = in_set & (rank == 0)
    src_dev = jnp.where(from_hot, hot_here, src_dev)
    src_slot = jnp.where(from_hot, perms[group_full, hot_here, jnp.minimum(cyc, per_dev - 1)], src_slot)
    if others_n >= 2:
        pred_rel = order[group_full, (cyc - 1) % others_n]
        pred = (hot_here + 1 + pred_rel) % group
        by_cycle = jnp.logical_not(is_hot) & (rank == 1)
        src_dev = jnp.where(by_cycle, pred, src_dev)
        src_slot = jnp.where(by_cycle, perms[group_full, pred, 1], src_slot)
    to_hot = is_hot & (rank < hot_n)
    peer = (hot_here + 1 + order[group_full, jnp.minimum(rank, others_n - 1)]) % group
    src_dev = jnp.where(to_hot, peer, src_dev)
    src_slot = jnp.where(to_hot, perms[group_full, peer, 0], src_slot)
    index_x = group_full // N_GZ
    index_z = group_full % N_GZ
    old_index = ((index_x * N_GY + src_dev) * N_GZ + index_z) * per_dev + src_slot
    box_x = position // (BYB * BZB)
    box_y = position // BZB % BYB
    box_z = position % BZB
    corner_x = index_x * (BXB * BOX) + box_x * BOX
    corner_y = device * (BYB * BOX) + box_y * BOX
    corner_z = index_z * (BZB * BOX) + box_z * BOX
    stacked = jnp.stack([corner_x, corner_y, corner_z]).reshape(3, -1).astype(jnp.int32)
    total = groups_n * group * per_dev
    return jnp.zeros((3, total), jnp.int32).at[:, old_index.reshape(-1)].set(stacked)


def block_levels(stream_key, extent, shards, least, largest):
    def one(dim, blocks):
        draws = jax.random.uniform(jax.random.fold_in(jax.random.fold_in(stream_key, 6), dim), (blocks,), jnp.float32, least / len(shards), largest / len(shards))
        return jnp.repeat(jnp.exp(draws), extent[dim] // blocks).reshape((-1,) + (1,) * (len(extent) - dim - 1))

    loudness = one(*shards[0])
    for cut in shards[1:]:
        loudness = loudness * one(*cut)
    return loudness


def scatter_about(rng, shape, scale, most, pieces=(), held_as=jnp.bfloat16):
    factor_of = block_levels(rng, shape, pieces, -0.22, 0.18) if pieces else 1.0
    result = jax.random.normal(rng, shape, jnp.float32) * scale * factor_of
    return jnp.minimum(jnp.maximum(result, -most), most).astype(held_as)


def setup_inputs(seed: int = 0) -> dict:
    seeds = jax.random.split(jax.random.key(seed), 6)
    solution_old = scatter_about(seeds[0], (NB, BOX, BOX * BOX), 1.0, 6.0, ((0, 256),), jnp.float32)
    right_side = scatter_about(seeds[1], (NB, BOX, BOX * BOX), 1.0, 6.0, ((0, 256),), jnp.float32)
    acoef = jnp.clip(jnp.exp(math.log(1.0) - 2.9957323 * jax.random.uniform(seeds[2], (NB, BOX, BOX * BOX), jnp.float32) ** block_levels(seeds[2], (NB, BOX, BOX * BOX), ((0, 256),), -0.2, 0.2)), 0.05, 1.0)
    bcoef = jnp.clip(jnp.exp(math.log(4.0) - 2.7725887 * jax.random.uniform(seeds[3], (NB, BOX, BOX * BOX), jnp.float32) ** block_levels(seeds[3], (NB, BOX, BOX * BOX), ((0, 256),), -0.2, 0.2)), 0.25, 4.0)
    corners = draw_corners(jax.random.fold_in(seeds[5], 71), 0)
    return {"solution_old": solution_old, "right_side": right_side, "acoef": acoef, "bcoef": bcoef, "corners": corners}


def place_boxes(boxes, box_order):
    grouped = boxes[box_order].reshape(NX // BOX, NY // BOX, NZ // BOX, BOX, BOX, BOX)
    return grouped.transpose(0, 3, 1, 4, 2, 5).reshape(NX, NY, NZ)


def face_coefs(padded):
    face_x = 0.5 * (padded[1:, 1:-1, 1:-1] + padded[:-1, 1:-1, 1:-1])
    face_y = 0.5 * (padded[1:-1, 1:, 1:-1] + padded[1:-1, :-1, 1:-1])
    face_z = 0.5 * (padded[1:-1, 1:-1, 1:] + padded[1:-1, 1:-1, :-1])
    return face_x, face_y, face_z


def diag_of(absorb, face_set):
    face_x, face_y, face_z = face_set
    return absorb + (face_x[1:] + face_x[:-1]) + (face_y[:, 1:] + face_y[:, :-1]) + (face_z[:, :, 1:] + face_z[:, :, :-1])


def neighbors(padded, face_set):
    face_x, face_y, face_z = face_set
    summed = face_x[1:] * padded[2:, 1:-1, 1:-1] + face_x[:-1] * padded[:-2, 1:-1, 1:-1]
    summed = summed + face_y[:, 1:] * padded[1:-1, 2:, 1:-1] + face_y[:, :-1] * padded[1:-1, :-2, 1:-1]
    summed = summed + face_z[:, :, 1:] * padded[1:-1, 1:-1, 2:] + face_z[:, :, :-1] * padded[1:-1, 1:-1, :-2]
    return summed


def checker(grid_shape):
    return (lax.broadcasted_iota(jnp.int32, grid_shape, 0) + lax.broadcasted_iota(jnp.int32, grid_shape, 1) + lax.broadcasted_iota(jnp.int32, grid_shape, 2)) % 2


def reference(solution_old, right_side, acoef, bcoef, corners):
    box_cells = corners // BOX
    flat_index = (box_cells[0] * (NY // BOX) + box_cells[1]) * (NZ // BOX) + box_cells[2]
    box_order = jnp.zeros((NB,), jnp.int32).at[flat_index].set(jnp.arange(NB, dtype=jnp.int32))
    solution = place_boxes(solution_old, box_order)
    forcing = place_boxes(right_side, box_order)
    absorb = place_boxes(acoef, box_order)
    diffuse = place_boxes(bcoef, box_order)
    face_set = face_coefs(jnp.pad(diffuse, 1))
    diagonal = diag_of(absorb, face_set)
    parity = checker((NX, NY, NZ))
    for sweep_no in range(SWEEPS):
        for colour in (0, 1):
            updated = (forcing + neighbors(jnp.pad(solution, 1), face_set)) / diagonal
            solution = jnp.where(parity == colour, updated, solution)
    residual = forcing - (diagonal * solution - neighbors(jnp.pad(solution, 1), face_set))
    return solution, residual
```

```python
import functools
import itertools

import jax
import jax.numpy as jnp
from jax import lax
from jax.experimental import pallas as pl
from jax.experimental.pallas import tpu as pltpu
from jax.sharding import PartitionSpec as P

BOX = 32
N_GX, N_GY, N_GZ = 4, 8, 8
PER_DEV = 4
ROUNDS = 3
HALO = 5
XE = BOX + 2 * HALO
SWEEPS = 2
F32 = jnp.float32
VMEM_LIMIT = 56 * 1024 * 1024


def _colourings():
    table = {}
    for p1, p2 in itertools.combinations(range(1, 7), 2):
        spots = (0, p1, p2)
        for cyc in itertools.product(range(3), repeat=7):
            if any(cyc[p] == cyc[p - 1] for p in range(7)):
                continue
            star = [3 - cyc[p] - cyc[p - 1] for p in spots]
            if len(set(star)) == 3:
                code = sum(c << (2 * i) for i, c in enumerate(list(cyc) + star))
                table[p1 * 7 + p2] = code
                break
    return table


COLOURINGS = _colourings()


def _pick(flag, yes, no):
    return jnp.where(flag, jnp.int32(yes) if isinstance(yes, int) else yes, jnp.int32(no) if isinstance(no, int) else no)


def plan_kernel(corners, f0, f1, f2, f3, plan, pay0, pay1, pay2, own, succ, swap, spot, sems):
    gx, me, gz = lax.axis_index("gx"), lax.axis_index("gy"), lax.axis_index("gz")
    base = gx * (N_GY * N_GZ * PER_DEV) + gz * PER_DEV
    stride = N_GZ * PER_DEV

    def owner(g, s):
        return lax.shift_right_logical(corners[1, base + g * stride + s], 5)

    def inner(g, s):
        return lax.shift_right_logical(corners[2, base + g * stride + s], 5) & 3

    hot = jnp.int32(0)
    rows = []
    for g in range(N_GY):
        row = [owner(g, s) for s in range(PER_DEV)]
        rows.append(row)
        leaving = sum(_pick(o != g, 1, 0) for o in row)
        hot = hot + _pick(leaving == 3, g, 0)
        for s in range(PER_DEV):
            own[g * PER_DEV + s] = row[s]
    first = jnp.int32(0)
    for g in reversed(range(N_GY)):
        to_hot = jnp.int32(0)
        nxt = jnp.int32(0)
        for o in rows[g]:
            to_hot = to_hot + _pick(o == hot, 1, 0)
            nxt = nxt + _pick((o != g) & (o != hot), o, 0)
        is_swap = _pick(hot == g, 0, to_hot)
        succ[g] = nxt
        swap[g] = is_swap
        first = _pick(is_swap == 1, g, first)
    v = first
    p1 = jnp.int32(0)
    p2 = jnp.int32(0)
    mine = jnp.int32(-1)
    pred = jnp.int32(0)
    for p in range(7):
        spot[p] = v
        if p:
            sw = swap[v] == 1
            p2 = _pick(sw & (p1 != 0), p, p2)
            p1 = _pick(sw & (p1 == 0), p, p1)
        mine = _pick(v == me, p, mine)
        pred = _pick(succ[v] == me, v, pred)
        v = succ[v]
    key = p1 * 7 + p2
    code = jnp.int32(0)
    for k, c in COLOURINGS.items():
        code = _pick(key == k, c, code)

    def cycle_colour(p):
        return lax.shift_right_logical(code, 2 * p) & 3

    star = [lax.shift_right_logical(code, 14 + 2 * i) & 3 for i in range(3)]
    spots = [spot[0], spot[p1], spot[p2]]
    is_hot = me == hot
    at = jnp.maximum(mine, 0)
    out_colour = cycle_colour(at)
    in_colour = cycle_colour(_pick(at == 0, 6, at - 1))
    my_succ = succ[me]
    swaps_here = jnp.logical_not(is_hot) & (swap[me] == 1)
    swap_colour = _pick(swaps_here, _pick(at == 0, star[0], _pick(at == p1, star[1], star[2])), -1)
    partners, slots, places, arrives = [], [], [], []
    for k in range(ROUNDS):
        hot_partner = sum(_pick(star[i] == k, spots[i], 0) for i in range(3))
        kind = _pick(swap_colour == k, 3, _pick(out_colour == k, 1, _pick(in_colour == k, 2, 0)))
        partner = _pick(swap_colour == k, hot, _pick(out_colour == k, my_succ, pred))
        kind = _pick(is_hot, 3, kind)
        partner = _pick(is_hot, hot_partner, partner)
        way = me ^ partner
        up = ((kind == 1) & (me < partner)) | ((kind == 2) & (partner < me))
        branch = _pick(kind == 0, 0, _pick(kind == 3, way, _pick(up, 7 + way, 14 + way)))
        plan[k] = branch
        slot = jnp.int32(0)
        place = jnp.int32(0)
        for s in range(PER_DEV):
            slot = slot + _pick(own[me * PER_DEV + s] == partner, s, 0)
            place = place + _pick(own[partner * PER_DEV + s] == me, inner(partner, s), 0)
        slot = jnp.minimum(slot, PER_DEV - 1)
        slots.append(slot)
        places.append(place)
        arrives.append((kind == 2) | (kind == 3))
    fields = (f0, f1, f2, f3)
    pays = (pay0, pay1, pay2)
    copies = [
        pltpu.make_async_copy(fields[f].at[slots[k]], pays[k].at[f], sems.at[k, f])
        for k in range(ROUNDS)
        for f in range(4)
    ]
    for copy in copies:
        copy.start()
    for q in range(PER_DEV):
        source = jnp.int32(0)
        for s in range(PER_DEV):
            source = source + _pick((own[me * PER_DEV + s] == me) & (inner(me, s) == q), s, 0)
        for k in range(ROUNDS):
            source = source + _pick(arrives[k] & (places[k] == q), 4 + k, 0)
        plan[4 + q] = source
    plan[3] = jnp.int32(0)
    for copy in copies:
        copy.wait()


def plan_and_pack(corners, fields):
    any_spec = pl.BlockSpec(memory_space=pl.ANY)
    smem = pl.BlockSpec(memory_space=pltpu.SMEM)
    pay = jax.ShapeDtypeStruct((4,) + fields[0].shape[1:], F32)
    return pl.pallas_call(
        plan_kernel,
        out_shape=(jax.ShapeDtypeStruct((8,), jnp.int32), pay, pay, pay),
        in_specs=[smem] + [any_spec] * 4,
        out_specs=(smem, any_spec, any_spec, any_spec),
        scratch_shapes=[
            pltpu.SMEM((32,), jnp.int32),
            pltpu.SMEM((8,), jnp.int32),
            pltpu.SMEM((8,), jnp.int32),
            pltpu.SMEM((8,), jnp.int32),
            pltpu.SemaphoreType.DMA((ROUNDS, 4)),
        ],
        name="plan",
    )(corners, *fields)


def swap_round(branch, pay):
    def stay(x):
        return x

    def move(pairs, x):
        return lax.ppermute(x, "gy", pairs)

    branches = [stay]
    for r in range(1, 8):
        branches.append(functools.partial(move, [(i, i ^ r) for i in range(8)]))
    for r in range(1, 8):
        branches.append(functools.partial(move, [(i, i ^ r) for i in range(8) if i < i ^ r]))
    for r in range(1, 8):
        branches.append(functools.partial(move, [(i, i ^ r) for i in range(8) if i > i ^ r]))
    return lax.switch(branch, branches, pay)


def iota(dim):
    return lax.broadcasted_iota(jnp.int32, (8, 128), dim)


def lroll(v, shift):
    shift %= 128
    return pltpu.roll(v, shift, 1) if shift else v


def sroll(v, shift):
    shift %= 8
    return pltpu.roll(v, shift, 0) if shift else v


def assemble_kernel(plan, f0, f1, f2, f3, r0, r1, r2, home, even, odd, raw, tmp, sems):
    fields = (f0, f1, f2, f3)
    gots = (r0, r1, r2)
    for q in range(PER_DEV):
        source = plan[4 + q]

        @pl.when(source < 4)
        def _():
            for f in range(4):
                pltpu.make_async_copy(fields[f].at[jnp.minimum(source, 3)], raw.at[f, q], sems.at[f, q]).start()

        for k in range(ROUNDS):

            @pl.when(source == 4 + k)
            def _():
                for f in range(4):
                    pltpu.make_async_copy(gots[k].at[f], raw.at[f, q], sems.at[f, q]).start()

    for q in range(PER_DEV):
        for f in range(4):
            pltpu.make_async_copy(f0.at[0], raw.at[f, q], sems.at[f, q]).wait()

    lane = iota(1)
    m64 = (lane & 64) != 0
    m32 = (lane & 32) != 0

    def step(i, carry):
        f = i // 4
        xt = pl.multiple_of((i % 4) * 8, 8)
        for t in range(4):
            for jj in range(2):
                j = 2 * t + jj
                a = [raw[f, k, pl.ds(xt, 8), j * 128 : (j + 1) * 128] for k in range(4)]
                n0 = jnp.where(m64, lroll(a[2], 64), a[0])
                n2 = jnp.where(m64, a[2], lroll(a[0], 64))
                n1 = jnp.where(m64, lroll(a[3], 64), a[1])
                n3 = jnp.where(m64, a[3], lroll(a[1], 64))
                b = [
                    jnp.where(m32, lroll(n1, 32), n0),
                    jnp.where(m32, n1, lroll(n0, 96)),
                    jnp.where(m32, lroll(n3, 32), n2),
                    jnp.where(m32, n3, lroll(n2, 96)),
                ]
                for q in range(4):
                    y = jj * 4 + q
                    tmp[t, y * 8 : y * 8 + 8, :] = b[q]
            for x in range(8):
                home[f, xt + x, t * 8 : t * 8 + 8, :] = tmp[t, pl.ds(x, 8, stride=8), :]
        return carry

    lax.fori_loop(0, 16, step, 0)

    low = (lax.axis_index("gx") & 1) == 1
    base = iota(0) + lane
    for t in range(4):
        ys = slice(t * 8, t * 8 + 8)

        def put(n, lo, hi):
            even[n, ys, :] = jnp.where(low, lo, hi)
            odd[n, ys, :] = jnp.where(low, hi, lo)

        for n in range(3):
            pair = []
            for x in (n, 27 + n):
                here = home[0, x, ys, :]
                if n < 2:
                    here = jnp.where(((base + x) & 1) == 1, here, home[0, x + 3, ys, :])
                pair.append(here)
            put(n, *pair)
        for n in range(5):
            put(3 + n, home[3, n, ys, :], home[3, 27 + n, ys, :])
        for n in range(4):
            put(8 + n, home[1, n, ys, :], home[1, 28 + n, ys, :])
            put(12 + n, home[2, n, ys, :], home[2, 28 + n, ys, :])


def assemble(plan, fields, gots):
    any_spec = pl.BlockSpec(memory_space=pl.ANY)
    vmem = pl.BlockSpec(memory_space=pltpu.VMEM)
    face = jax.ShapeDtypeStruct((16, BOX, 128), F32)
    return pl.pallas_call(
        assemble_kernel,
        out_shape=(jax.ShapeDtypeStruct((4, BOX, BOX, 128), F32), face, face),
        in_specs=[pl.BlockSpec(memory_space=pltpu.SMEM)] + [any_spec] * 7,
        out_specs=(vmem, vmem, vmem),
        scratch_shapes=[
            pltpu.VMEM((4, PER_DEV, BOX, BOX * BOX), F32),
            pltpu.VMEM((4, 64, 128), F32),
            pltpu.SemaphoreType.DMA((4, PER_DEV)),
        ],
        compiler_params=pltpu.CompilerParams(vmem_limit_bytes=VMEM_LIMIT),
        name="assemble",
    )(plan, *fields, *gots)


def sides(axis, count):
    i = lax.axis_index(axis)
    return (i & 1) == 1, i > 0, i < count - 1


def halo_of(axis, count, even, odd):
    low_first, has_low, has_high = sides(axis, count)
    low = jnp.where(has_low, jnp.where(low_first, even, odd), 0.0)
    high = jnp.where(has_high, jnp.where(low_first, odd, even), 0.0)
    return low, high


def x_halo_tiles(even, odd, t):
    ys = slice(t * 8, t * 8 + 8)
    layers = [halo_of("gx", N_GX, even[n, ys, :], odd[n, ys, :]) for n in range(16)]
    planes = {}
    for side in range(2):
        part = [layer[side] for layer in layers]
        for i in range(HALO):
            j = i - 1 if side == 0 else i
            inside = 0 <= j < 4
            u = part[i % 3]
            planes[i if side == 0 else HALO + BOX + i] = (
                u,
                part[8 + j] if inside else None,
                part[12 + j] if inside else None,
                part[3 + i],
            )
    return planes


def pack_y(u, f, a, b, colour1, high):
    sub = iota(0)
    pair = jnp.where(colour1, u, sroll(u, -3))
    if high:
        first = jnp.where(sub < 3, sroll(pair, -3), b)
        second = jnp.where(sub < 4, sroll(f, -4), a)
    else:
        first = jnp.where(sub < 3, pair, sroll(b, 3))
        second = jnp.where(sub < 4, f, sroll(a, 4))
    return first, second


def pack_y_kernel(home, x_even, x_odd, even, odd):
    low = (lax.axis_index("gy") & 1) == 1
    base = iota(0) + iota(1)

    def put(e, tiles, colour1):
        lo = pack_y(*tiles[0], colour1, False)
        hi = pack_y(*tiles[1], colour1, True)
        for n in range(2):
            even[e, n * 8 : n * 8 + 8, :] = jnp.where(low, lo[n], hi[n])
            odd[e, n * 8 : n * 8 + 8, :] = jnp.where(low, hi[n], lo[n])

    def step(x, carry):
        colour1 = ((base + x) & 1) == 1
        put(x + HALO, [[home[f, x, t * 8 : t * 8 + 8, :] for f in range(4)] for t in (0, 3)], colour1)
        return carry

    lax.fori_loop(0, BOX, step, 0)
    near, far = x_halo_tiles(x_even, x_odd, 0), x_halo_tiles(x_even, x_odd, 3)
    zero = jnp.zeros((8, 128), F32)
    for e in near:
        colour1 = ((base + e + 1) & 1) == 1
        put(e, [[zero if v is None else v for v in tiles[e]] for tiles in (near, far)], colour1)


def build_main(home, x_even, x_odd, y_even, y_odd, ub, fa):
    def step(x, carry):
        ub[0, x + HALO, 16:48, :] = home[0, x]
        ub[1, x + HALO, 16:48, :] = home[3, x]
        fa[0, x + HALO, 8:40, :] = home[1, x]
        fa[1, x + HALO, 8:40, :] = home[2, x]
        return carry

    lax.fori_loop(0, BOX, step, 0)
    zero = jnp.zeros((8, 128), F32)
    for t in range(4):
        for e, (u, f, a, b) in x_halo_tiles(x_even, x_odd, t).items():
            ub[0, e, 16 + t * 8 : 24 + t * 8, :] = u
            ub[1, e, 16 + t * 8 : 24 + t * 8, :] = b
            fa[0, e, 8 + t * 8 : 16 + t * 8, :] = zero if f is None else f
            fa[1, e, 8 + t * 8 : 16 + t * 8, :] = zero if a is None else a
    sub = iota(0)

    def halo(e, carry):
        l0, h0 = halo_of("gy", N_GY, y_even[e, 0:8, :], y_odd[e, 0:8, :])
        l1, h1 = halo_of("gy", N_GY, y_even[e, 8:16, :], y_odd[e, 8:16, :])
        ub[0, e, 0:8, :] = zero
        ub[1, e, 0:8, :] = zero
        ub[0, e, 8:16, :] = jnp.where(sub < 6, sroll(l0, 3), sroll(l0, 6))
        ub[1, e, 8:16, :] = l0
        fa[0, e, 0:8, :] = sroll(l1, 4)
        fa[1, e, 0:8, :] = l1
        ub[0, e, 48:56, :] = jnp.where(sub < 3, h0, sroll(h0, 3))
        ub[1, e, 48:56, :] = sroll(h0, -3)
        fa[0, e, 40:48, :] = h1
        fa[1, e, 40:48, :] = sroll(h1, 4)
        ub[0, e, 56:64, :] = zero
        ub[1, e, 56:64, :] = zero
        return carry

    lax.fori_loop(0, XE, halo, 0)


def pack_z_kernel(home, x_even, x_odd, y_even, y_odd, ub, fa, even, odd):
    build_main(home, x_even, x_odd, y_even, y_odd, ub, fa)
    low = (lax.axis_index("gz") & 1) == 1
    lane = iota(1)
    base = iota(0) + lane
    place = lane & 15
    group = lax.shift_right_logical(lane, 4)

    def step(e, carry):
        colour1 = ((base + e + 1) & 1) == 1
        lo = jnp.zeros((8, 128), F32)
        hi = lo
        for t in range(6):
            u = ub[0, e, 8 + t * 8 : 16 + t * 8, :]
            b = ub[1, e, 8 + t * 8 : 16 + t * 8, :]
            f = fa[0, e, t * 8 : 8 + t * 8, :]
            a = fa[1, e, t * 8 : 8 + t * 8, :]
            pair = jnp.where(colour1, u, lroll(u, -3))
            o = 16 * t

            def join(p, bb, ff, aa):
                return jnp.where(place < 3, p, jnp.where(place < 8, bb, jnp.where(place < 12, ff, aa)))

            g = join(lroll(pair, o), lroll(b, o + 3), lroll(f, o + 8), lroll(a, o + 12))
            lo = jnp.where(group == t, g, lo)
            g = join(lroll(pair, o + 5), lroll(b, o + 8), lroll(f, o + 12), lroll(a, o + 16))
            hi = jnp.where(group == t, g, hi)
        even[e] = jnp.where(low, lo, hi)
        odd[e] = jnp.where(low, hi, lo)
        return carry

    lax.fori_loop(0, XE, step, 0)


def shifted_z(main, aux, lane, first, last):
    m, a = lroll(main, 1), lroll(aux, 1)
    below = (jnp.where(first, a, m), jnp.where(first, m, a))
    m, a = lroll(main, 127), lroll(aux, 127)
    above = (jnp.where(last, a, m), jnp.where(last, m, a))
    return below, above


def sweep_kernel(ub, fa, z_even, z_odd, sol, res, u, b, fx, co, dg):
    lane = iota(1)
    first, last = lane == 0, lane == 127
    base = iota(0) + lane
    zero = jnp.zeros((8, 128), F32)

    def unpack(e, carry):
        lo, hi = halo_of("gz", N_GZ, z_even[e], z_odd[e])
        for w in (0, 56):
            u[1, e, w : w + 8, :] = zero
            b[1, e, w : w + 8, :] = zero
        u[0, e] = ub[0, e]
        b[0, e] = ub[1, e]
        for t in range(6):
            o = 16 * t
            rows = slice(8 + t * 8, 16 + t * 8)
            part = jnp.where(lane < 3, lroll(hi, -o), lroll(hi, 3 - o))
            part = jnp.where(lane < 64, part, jnp.where(lane < 126, lroll(lo, 123 - o), lroll(lo, 126 - o)))
            u[1, e, rows, :] = part
            b[1, e, rows, :] = jnp.where(lane < 64, lroll(hi, -3 - o), lroll(lo, 120 - o))
            rows = slice(t * 8, 8 + t * 8)
            fx[0, e, rows, :] = jnp.where(lane < 64, lroll(hi, -8 - o), lroll(lo, 116 - o))
            fx[1, e, rows, :] = jnp.where(lane < 64, lroll(hi, -12 - o), lroll(lo, 112 - o))
        return carry

    lax.fori_loop(0, XE, unpack, 0)

    def coefs(e, carry):
        for t in range(6):
            r = 8 + t * 8
            rows = slice(t * 8, 8 + t * 8)
            mid = [b[s, e, r : r + 8, :] for s in range(2)]
            below, above = shifted_z(mid[0], mid[1], lane, first, last)
            for s in range(2):
                near = (
                    b[s, e - 1, r : r + 8, :],
                    b[s, e + 1, r : r + 8, :],
                    b[s, e, r - 1 : r + 7, :],
                    b[s, e, r + 1 : r + 9, :],
                    below[s],
                    above[s],
                )
                faces = [0.5 * (mid[s] + v) for v in near]
                f, a = (fa, fx)[s][0, e, rows, :], (fa, fx)[s][1, e, rows, :]
                diag = a + (faces[1] + faces[0]) + (faces[3] + faces[2]) + (faces[5] + faces[4])
                inverse = jnp.where(mid[s] > 0, 1.0 / diag, 0.0)
                for n in range(6):
                    co[s, n, e - 1, rows, :] = faces[n] * inverse
                co[s, 6, e - 1, rows, :] = f * inverse
                if s == 0 and 1 <= t <= 4:
                    dg[e - 1, (t - 1) * 8 : t * 8, :] = diag
        return carry

    lax.fori_loop(1, XE - 1, coefs, 0)

    def update(e, t, spans):
        r = 8 + t * 8
        rows = slice(t * 8, 8 + t * 8)
        mid = [u[s, e, r : r + 8, :] for s in range(2)]
        below, above = shifted_z(mid[0], mid[1], lane, first, last)
        new = []
        for s in spans:
            c = [co[s, n, e - 1, rows, :] for n in range(7)]
            x = c[0] * u[s, e - 1, r : r + 8, :] + c[1] * u[s, e + 1, r : r + 8, :]
            y = c[2] * u[s, e, r - 1 : r + 7, :] + c[3] * u[s, e, r + 1 : r + 9, :]
            z = c[4] * below[s] + c[5] * above[s]
            new.append(c[6] + ((x + y) + z))
        return mid, new

    for half in range(2 * SWEEPS):
        colour = half % 2

        def sweep(e, carry):
            hit = ((base + e + 1) & 1) == colour
            for t in range(6):
                r = 8 + t * 8
                mid, new = update(e, t, (0, 1))
                for s in range(2):
                    u[s, e, r : r + 8, :] = jnp.where(hit, new[s], mid[s])
            return carry

        lax.fori_loop(1 + half, XE - 1 - half, sweep, 0)

    def finish(e, carry):
        for t in range(1, 5):
            mid, new = update(e, t, (0,))
            rows = slice((t - 1) * 8, t * 8)
            sol[e - HALO, rows, :] = mid[0]
            res[e - HALO, rows, :] = dg[e - 1, rows, :] * (new[0] - mid[0])
        return carry

    lax.fori_loop(HALO, HALO + BOX, finish, 0)


def on_vmem(kernel, out_shape, scratch, name, *args):
    vmem = pl.BlockSpec(memory_space=pltpu.VMEM)
    return pl.pallas_call(
        kernel,
        out_shape=out_shape,
        in_specs=[vmem] * len(args),
        out_specs=tuple([vmem] * len(out_shape)),
        scratch_shapes=scratch,
        compiler_params=pltpu.CompilerParams(vmem_limit_bytes=VMEM_LIMIT),
        name=name,
    )(*args)


def exchange(axis, count, even, odd):
    pairs = []
    for start in (0, 1):
        step = []
        for i in range(start, count, 2):
            j = (i + 1) % count
            step += [(i, j), (j, i)]
        pairs.append(step)
    return lax.ppermute(even, axis, pairs[0]), lax.ppermute(odd, axis, pairs[1])


def per_device(solution_old, right_side, acoef, bcoef, corners):
    fields = (solution_old, right_side, acoef, bcoef)
    plan, *pays = plan_and_pack(corners, fields)
    gots = [swap_round(plan[k], pays[k]) for k in range(ROUNDS)]
    home, even, odd = assemble(plan, fields, gots)
    x_even, x_odd = exchange("gx", N_GX, even, odd)
    face = jax.ShapeDtypeStruct((XE, 16, 128), F32)
    even, odd = on_vmem(pack_y_kernel, (face, face), [], "pack_y", home, x_even, x_odd)
    y_even, y_odd = exchange("gy", N_GY, even, odd)
    face = jax.ShapeDtypeStruct((XE, 8, 128), F32)
    ub, fa, even, odd = on_vmem(
        pack_z_kernel,
        (jax.ShapeDtypeStruct((2, XE, 64, 128), F32), jax.ShapeDtypeStruct((2, XE, 48, 128), F32), face, face),
        [],
        "pack_z",
        home,
        x_even,
        x_odd,
        y_even,
        y_odd,
    )
    z_even, z_odd = exchange("gz", N_GZ, even, odd)
    block = jax.ShapeDtypeStruct((BOX, BOX, 128), F32)
    return on_vmem(
        sweep_kernel,
        (block, block),
        [
            pltpu.VMEM((2, XE, 64, 128), F32),
            pltpu.VMEM((2, XE, 64, 128), F32),
            pltpu.VMEM((2, XE, 48, 128), F32),
            pltpu.VMEM((2, 7, XE - 2, 48, 128), F32),
            pltpu.VMEM((XE - 2, BOX, 128), F32),
        ],
        "sweeps",
        ub,
        fa,
        z_even,
        z_odd,
    )


def solution(mesh):
    boxes = P(("gx", "gy", "gz"), None, None)
    block = P("gx", "gy", "gz")
    return jax.shard_map(
        per_device,
        mesh=mesh,
        in_specs=(boxes, boxes, boxes, boxes, P()),
        out_specs=(block, block),
        check_vma=False,
    )
```

```python
import functools
import itertools

import jax
import jax.numpy as jnp
from jax import lax
from jax.experimental import pallas as pl
from jax.experimental.pallas import tpu as pltpu
from jax.sharding import PartitionSpec as P

BOX = 32
N_GX, N_GY, N_GZ = 4, 8, 8
PER_DEV = 4
ROUNDS = 3
HALF = BOX // 2
SIDE = 3
PAIRS = HALF + 2 * SIDE
SWEEPS = 2
F32 = jnp.float32
MIB = 1024 * 1024


def _colourings():
    table = {}
    for p1, p2 in itertools.combinations(range(1, 7), 2):
        spots = (0, p1, p2)
        for cyc in itertools.product(range(3), repeat=7):
            if any(cyc[p] == cyc[p - 1] for p in range(7)):
                continue
            star = [3 - cyc[p] - cyc[p - 1] for p in spots]
            if len(set(star)) == 3:
                code = sum(c << (2 * i) for i, c in enumerate(list(cyc) + star))
                table[p1 * 7 + p2] = code
                break
    return table


COLOURINGS = _colourings()


def _pick(flag, yes, no):
    return jnp.where(flag, jnp.int32(yes) if isinstance(yes, int) else yes, jnp.int32(no) if isinstance(no, int) else no)


def plan_kernel(corners, f0, f1, f2, f3, plan, pay0, pay1, pay2, own, succ, swap, spot, sems):
    gx, me, gz = lax.axis_index("gx"), lax.axis_index("gy"), lax.axis_index("gz")
    base = gx * (N_GY * N_GZ * PER_DEV) + gz * PER_DEV
    stride = N_GZ * PER_DEV

    def owner(g, s):
        return lax.shift_right_logical(corners[1, base + g * stride + s], 5)

    def inner(g, s):
        return lax.shift_right_logical(corners[2, base + g * stride + s], 5) & 3

    hot = jnp.int32(0)
    rows = []
    for g in range(N_GY):
        row = [owner(g, s) for s in range(PER_DEV)]
        rows.append(row)
        leaving = sum(_pick(o != g, 1, 0) for o in row)
        hot = hot + _pick(leaving == 3, g, 0)
        for s in range(PER_DEV):
            own[g * PER_DEV + s] = row[s]
    first = jnp.int32(0)
    for g in reversed(range(N_GY)):
        to_hot = jnp.int32(0)
        nxt = jnp.int32(0)
        for o in rows[g]:
            to_hot = to_hot + _pick(o == hot, 1, 0)
            nxt = nxt + _pick((o != g) & (o != hot), o, 0)
        is_swap = _pick(hot == g, 0, to_hot)
        succ[g] = nxt
        swap[g] = is_swap
        first = _pick(is_swap == 1, g, first)
    v = first
    p1 = jnp.int32(0)
    p2 = jnp.int32(0)
    mine = jnp.int32(-1)
    pred = jnp.int32(0)
    for p in range(7):
        spot[p] = v
        if p:
            sw = swap[v] == 1
            p2 = _pick(sw & (p1 != 0), p, p2)
            p1 = _pick(sw & (p1 == 0), p, p1)
        mine = _pick(v == me, p, mine)
        pred = _pick(succ[v] == me, v, pred)
        v = succ[v]
    key = p1 * 7 + p2
    code = jnp.int32(0)
    for k, c in COLOURINGS.items():
        code = _pick(key == k, c, code)

    def cycle_colour(p):
        return lax.shift_right_logical(code, 2 * p) & 3

    star = [lax.shift_right_logical(code, 14 + 2 * i) & 3 for i in range(3)]
    spots = [spot[0], spot[p1], spot[p2]]
    is_hot = me == hot
    at = jnp.maximum(mine, 0)
    out_colour = cycle_colour(at)
    in_colour = cycle_colour(_pick(at == 0, 6, at - 1))
    my_succ = succ[me]
    swaps_here = jnp.logical_not(is_hot) & (swap[me] == 1)
    swap_colour = _pick(swaps_here, _pick(at == 0, star[0], _pick(at == p1, star[1], star[2])), -1)
    partners, slots, places, arrives = [], [], [], []
    for k in range(ROUNDS):
        hot_partner = sum(_pick(star[i] == k, spots[i], 0) for i in range(3))
        kind = _pick(swap_colour == k, 3, _pick(out_colour == k, 1, _pick(in_colour == k, 2, 0)))
        partner = _pick(swap_colour == k, hot, _pick(out_colour == k, my_succ, pred))
        kind = _pick(is_hot, 3, kind)
        partner = _pick(is_hot, hot_partner, partner)
        way = me ^ partner
        up = ((kind == 1) & (me < partner)) | ((kind == 2) & (partner < me))
        branch = _pick(kind == 0, 0, _pick(kind == 3, way, _pick(up, 7 + way, 14 + way)))
        plan[k] = branch
        slot = jnp.int32(0)
        place = jnp.int32(0)
        for s in range(PER_DEV):
            slot = slot + _pick(own[me * PER_DEV + s] == partner, s, 0)
            place = place + _pick(own[partner * PER_DEV + s] == me, inner(partner, s), 0)
        slot = jnp.minimum(slot, PER_DEV - 1)
        slots.append(slot)
        places.append(place)
        arrives.append((kind == 2) | (kind == 3))
    fields = (f0, f1, f2, f3)
    pays = (pay0, pay1, pay2)
    copies = [
        pltpu.make_async_copy(fields[f].at[slots[k]], pays[k].at[f], sems.at[k, f])
        for k in range(ROUNDS)
        for f in range(4)
    ]
    for copy in copies:
        copy.start()
    for q in range(PER_DEV):
        source = jnp.int32(0)
        for s in range(PER_DEV):
            source = source + _pick((own[me * PER_DEV + s] == me) & (inner(me, s) == q), s, 0)
        for k in range(ROUNDS):
            source = source + _pick(arrives[k] & (places[k] == q), 4 + k, 0)
        plan[4 + q] = source
    plan[3] = jnp.int32(0)
    for copy in copies:
        copy.wait()


def plan_and_pack(corners, fields):
    any_spec = pl.BlockSpec(memory_space=pl.ANY)
    smem = pl.BlockSpec(memory_space=pltpu.SMEM)
    pay = jax.ShapeDtypeStruct((4,) + fields[0].shape[1:], F32)
    return pl.pallas_call(
        plan_kernel,
        out_shape=(jax.ShapeDtypeStruct((8,), jnp.int32), pay, pay, pay),
        in_specs=[smem] + [any_spec] * 4,
        out_specs=(smem, any_spec, any_spec, any_spec),
        scratch_shapes=[
            pltpu.SMEM((32,), jnp.int32),
            pltpu.SMEM((8,), jnp.int32),
            pltpu.SMEM((8,), jnp.int32),
            pltpu.SMEM((8,), jnp.int32),
            pltpu.SemaphoreType.DMA((ROUNDS, 4)),
        ],
        name="plan",
    )(corners, *fields)


def swap_round(branch, pay):
    def stay(x):
        return x

    def move(pairs, x):
        return lax.ppermute(x, "gy", pairs)

    branches = [stay]
    for r in range(1, 8):
        branches.append(functools.partial(move, [(i, i ^ r) for i in range(8)]))
    for r in range(1, 8):
        branches.append(functools.partial(move, [(i, i ^ r) for i in range(8) if i < i ^ r]))
    for r in range(1, 8):
        branches.append(functools.partial(move, [(i, i ^ r) for i in range(8) if i > i ^ r]))
    return lax.switch(branch, branches, pay)


def iota(dim):
    return lax.broadcasted_iota(jnp.int32, (8, 128), dim)


def lroll(v, shift):
    shift %= 128
    return pltpu.roll(v, shift, 1) if shift else v


def sroll(v, shift):
    shift %= 8
    return pltpu.roll(v, shift, 0) if shift else v


U1, B1, B0, F0, A0, F1, A1 = range(7)
WIDTH = (5, 5, 4, 4, 4, 3, 3)
LAYERS = [(n, i) for n in range(7) for i in range(3 if n < 2 else 2)]


def odd_cell():
    return ((iota(0) + iota(1)) & 1) == 1


def assemble_kernel(plan, f0, f1, f2, f3, r0, r1, r2, home, even, odd, raw, tmp, sems):
    fields = (f0, f1, f2, f3)
    gots = (r0, r1, r2)
    for q in range(PER_DEV):
        source = plan[4 + q]

        @pl.when(source < 4)
        def _():
            for f in range(4):
                pltpu.make_async_copy(fields[f].at[jnp.minimum(source, 3)], raw.at[f, q], sems.at[f, q]).start()

        for k in range(ROUNDS):

            @pl.when(source == 4 + k)
            def _():
                for f in range(4):
                    pltpu.make_async_copy(gots[k].at[f], raw.at[f, q], sems.at[f, q]).start()

    lane = iota(1)
    m64 = (lane & 64) != 0
    m32 = (lane & 32) != 0
    is_odd = odd_cell()

    for f in range(4):
        for q in range(PER_DEV):
            pltpu.make_async_copy(f0.at[0], raw.at[f, q], sems.at[f, q]).wait()

        def step(i, carry):
            xt = pl.multiple_of(i * 8, 8)
            for t in range(4):
                for jj in range(2):
                    j = 2 * t + jj
                    a = [raw[f, k, pl.ds(xt, 8), j * 128 : (j + 1) * 128] for k in range(4)]
                    n0 = jnp.where(m64, lroll(a[2], 64), a[0])
                    n2 = jnp.where(m64, a[2], lroll(a[0], 64))
                    n1 = jnp.where(m64, lroll(a[3], 64), a[1])
                    n3 = jnp.where(m64, a[3], lroll(a[1], 64))
                    b = [
                        jnp.where(m32, lroll(n1, 32), n0),
                        jnp.where(m32, n1, lroll(n0, 96)),
                        jnp.where(m32, lroll(n3, 32), n2),
                        jnp.where(m32, n3, lroll(n2, 96)),
                    ]
                    for q in range(4):
                        y = jj * 4 + q
                        tmp[t, y * 8 : y * 8 + 8, :] = b[q]
            for t in range(4):
                ys = slice(t * 8, t * 8 + 8)
                for x in range(0, 8, 2):
                    lower = tmp[t, pl.ds(x, 8, stride=8), :]
                    upper = tmp[t, pl.ds(x + 1, 8, stride=8), :]
                    j = i * 4 + x // 2
                    home[(U1, F1, A1, B1)[f], j, ys, :] = jnp.where(is_odd, lower, upper)
                    if f:
                        home[(None, F0, A0, B0)[f], j, ys, :] = jnp.where(is_odd, upper, lower)
            return carry

        lax.fori_loop(0, 4, step, 0)

    low = (lax.axis_index("gx") & 1) == 1
    for k, (n, i) in enumerate(LAYERS):
        last = HALF - (3 if n < 2 else 2) + i
        even[k] = home[n, jnp.where(low, i, last)]
        odd[k] = home[n, jnp.where(low, last, i)]


def assemble(plan, fields, gots):
    any_spec = pl.BlockSpec(memory_space=pl.ANY)
    vmem = pl.BlockSpec(memory_space=pltpu.VMEM)
    face = jax.ShapeDtypeStruct((16, BOX, 128), F32)
    return pl.pallas_call(
        assemble_kernel,
        out_shape=(jax.ShapeDtypeStruct((7, HALF, BOX, 128), F32), face, face),
        in_specs=[pl.BlockSpec(memory_space=pltpu.SMEM)] + [any_spec] * 7,
        out_specs=(vmem, vmem, vmem),
        scratch_shapes=[
            pltpu.VMEM((4, PER_DEV, BOX, BOX * BOX), F32),
            pltpu.VMEM((4, 64, 128), F32),
            pltpu.SemaphoreType.DMA((4, PER_DEV)),
        ],
        compiler_params=pltpu.CompilerParams(vmem_limit_bytes=12 * MIB),
        name="assemble",
    )(plan, *fields, *gots)


def halo_of(axis, count, even, odd):
    i = lax.axis_index(axis)
    low_first = (i & 1) == 1
    low = jnp.where(i > 0, jnp.where(low_first, even, odd), 0.0)
    high = jnp.where(i < count - 1, jnp.where(low_first, odd, even), 0.0)
    return low, high


def x_halo_tiles(even, odd, t):
    ys = slice(t * 8, t * 8 + 8)
    pairs = {}
    for k, (n, i) in enumerate(LAYERS):
        low, high = halo_of("gx", N_GX, even[k, ys, :], odd[k, ys, :])
        pairs.setdefault(SIDE - (3 if n < 2 else 2) + i, {})[n] = low
        pairs.setdefault(SIDE + HALF + i, {})[n] = high
    return pairs


def pack_y_kernel(home, x_even, x_odd, even, odd):
    low = (lax.axis_index("gy") & 1) == 1
    sub = iota(0)

    def put(at, lo, hi):
        even[at] = jnp.where(low, lo, hi)
        odd[at] = jnp.where(low, hi, lo)

    def put_pairs(k, first, second):
        for i, (near, far) in enumerate((first, second)):
            put(3 * (k + i), jnp.where(sub < 5, near[U1], sroll(near[F1], 5)), jnp.where(sub < 5, sroll(far[U1], -3), far[F1]))
            put(3 * (k + i) + 1, jnp.where(sub < 5, near[B1], sroll(near[A1], 5)), jnp.where(sub < 5, sroll(far[B1], -3), far[A1]))
            put(3 * (k + i) + 2, jnp.where(sub < 4, near[B0], sroll(near[F0], 4)), jnp.where(sub < 4, sroll(far[B0], 4), far[F0]))
        (n0, f0), (n1, f1) = first, second
        lo = jnp.where(sub < 4, n0[A0], sroll(n1[A0], 4))
        hi = jnp.where(sub < 4, sroll(f0[A0], 4), f1[A0])
        put(3 * PAIRS + (k // 2), lo, hi)

    halo = (x_halo_tiles(x_even, x_odd, 0), x_halo_tiles(x_even, x_odd, 3))
    zero = jnp.zeros((8, 128), F32)

    def tiles(k):
        inside = SIDE <= k < SIDE + HALF
        out = []
        for near_far in range(2):
            ys = slice(24 * near_far, 24 * near_far + 8)
            if inside:
                out.append([home[n, k - SIDE, ys, :] for n in range(7)])
            else:
                out.append([halo[near_far][k].get(n, zero) for n in range(7)])
        return out

    for k in range(0, PAIRS, 2):
        put_pairs(k, tiles(k), tiles(k + 1))


PAD = (8, 8, 8, 0, 0, 0, 0)


def pack_z_kernel(home, x_even, x_odd, y_even, y_odd, u1, b1, b0, f0, a0, f1, a1, face):
    outs = (u1, b1, b0, f0, a0, f1, a1)

    def copy(j, carry):
        for n in range(7):
            outs[n][j + SIDE, PAD[n] + 8 : PAD[n] + 40, :] = home[n, j]
        return carry

    lax.fori_loop(0, HALF, copy, 0, unroll=2)
    for t in range(4):
        for k, tiles in x_halo_tiles(x_even, x_odd, t).items():
            for n, tile in tiles.items():
                outs[n][k, PAD[n] + 8 + t * 8 : PAD[n] + 16 + t * 8, :] = tile

    def halo(m, carry):
        l3, h3 = halo_of("gy", N_GY, y_even[3 * PAIRS + m], y_odd[3 * PAIRS + m])
        for i in range(2):
            k = 2 * m + i
            (l0, h0), (l1, h1), (l2, h2) = [
                halo_of("gy", N_GY, y_even[3 * k + w], y_odd[3 * k + w]) for w in range(3)
            ]
            lows = (sroll(l0, 3), sroll(l1, 3), sroll(l2, 4), l2, sroll(l3, 4) if i == 0 else l3, l0, l1)
            highs = (h0, h1, h2, sroll(h2, 4), h3 if i == 0 else sroll(h3, 4), sroll(h0, 3), sroll(h1, 3))
            for n in range(7):
                outs[n][k, PAD[n] : PAD[n] + 8, :] = lows[n]
                outs[n][k, PAD[n] + 40 : PAD[n] + 48, :] = highs[n]
        return carry

    lax.fori_loop(0, PAIRS // 2, halo, 0)
    lane = iota(1)
    place = lane & 63

    def pack(k, carry):
        for v in range(3):
            both = []
            for w in range(2):
                t = 2 * v + w
                at = 64 * w
                group = None
                ends = []
                for n in range(7):
                    tile = outs[n][k, PAD[n] + t * 8 : PAD[n] + t * 8 + 8, :]
                    ends.append((lroll(tile, at + WIDTH[n]), at + 2 * WIDTH[n]))
                    at += 2 * WIDTH[n]
                group = ends[-1][0]
                for tile, end in reversed(ends[:-1]):
                    group = jnp.where(place < end - 64 * w, tile, group)
                both.append(group)
            face[k, v] = jnp.where(lane < 64, both[0], both[1])
        return carry

    lax.fori_loop(0, PAIRS, pack, 0, unroll=2)


def sweep_kernel(u1, b1, b0, f0, a0, f1, a1, z_even, z_odd, sol, res, um0, um1, ua0, ua1, ba0, ba1, fax, co, dg):
    lane = iota(1)
    first, last = lane == 0, lane == 127
    place = lane & 63
    is_odd = odd_cell()
    u = ((um0, ua0), (um1, ua1))
    b = ((b0, ba0), (b1, ba1))
    fa = (((f0, a0), (fax.at[0], fax.at[1])), ((f1, a1), (fax.at[2], fax.at[3])))
    starts = [2 * sum(WIDTH[:n]) for n in range(7)]
    high_part = functools.reduce(
        jnp.logical_or, [(place >= starts[n]) & (place < starts[n] + WIDTH[n]) for n in range(7)]
    )
    aux = (ua1, ba1, ba0, fax.at[0], fax.at[1], fax.at[2], fax.at[3])

    def unpack(k, carry):
        um1[k] = u1[k]
        for v in range(3):
            low, high = halo_of("gz", N_GZ, z_even[k, v], z_odd[k, v])
            both = jnp.where(high_part, low, high)
            for w in range(2):
                t = 2 * v + w
                for n in range(7):
                    aux[n][k, PAD[n] + t * 8 : PAD[n] + t * 8 + 8, :] = lroll(both, -(64 * w + starts[n] + WIDTH[n]))
        return carry

    lax.fori_loop(0, PAIRS, unpack, 0, unroll=2)

    def around(c, field, k, t, spans):
        r = 8 + t * 8
        main, side = field[1 - c]
        m, a = main[k, r : r + 8, :], side[k, r : r + 8, :]
        m1, a1 = lroll(m, 1), lroll(a, 1)
        m2, a2 = lroll(m, 127), lroll(a, 127)
        below = (jnp.where(first, a1, m1), jnp.where(first, m1, a1))
        above = (jnp.where(last, a2, m2), jnp.where(last, m2, a2))
        out = []
        for s in spans:
            ref = (main, side)[s]
            back, ahead = ref[k - 1, r : r + 8, :], ref[k + 1, r : r + 8, :]
            beside = jnp.where(is_odd, back, ahead) if c else jnp.where(is_odd, ahead, back)
            out.append(((m, a)[s], beside, ref[k, r - 1 : r + 7, :], ref[k, r + 1 : r + 9, :], below[s], above[s]))
        return out

    def coefs(k, carry):
        for c in range(2):
            for t in range(6):
                rows = slice(t * 8, 8 + t * 8)
                near = around(c, b, k, t, (0, 1))
                for s in range(2):
                    mid = b[c][s][k, 8 + t * 8 : 16 + t * 8, :]
                    f, a = [ref[k, rows, :] for ref in fa[c][s]]
                    faces = [0.5 * (mid + v) for v in near[s]]
                    diag = a + (faces[0] + faces[1]) + (faces[2] + faces[3]) + (faces[4] + faces[5])
                    inverse = jnp.where(mid > 0, 1.0 / diag, 0.0)
                    for n in range(6):
                        co[c, s, n, k - 1, rows, :] = faces[n] * inverse
                    co[c, s, 6, k - 1, rows, :] = f * inverse
                    if s == 0:
                        dg[c, k - 1, rows, :] = diag
        return carry

    lax.fori_loop(1, PAIRS - 1, coefs, 0)

    def update(c, k, t, spans):
        rows = slice(t * 8, 8 + t * 8)
        new = []
        for s, v in zip(spans, around(c, u, k, t, spans)):
            w = [co[c, s, n, k - 1, rows, :] for n in range(7)]
            x = w[0] * v[0] + w[1] * v[1]
            y = w[2] * v[2] + w[3] * v[3]
            z = w[4] * v[4] + w[5] * v[5]
            new.append(w[6] + ((x + y) + z))
        return new

    for half in range(2 * SWEEPS):
        c = half % 2

        def sweep(k, carry):
            for t in range(6):
                for s, new in enumerate(update(c, k, t, (0, 1))):
                    u[c][s][k, 8 + t * 8 : 16 + t * 8, :] = new
            return carry

        out = half // 2
        lax.fori_loop(1 + out, PAIRS - 1 - out, sweep, 0, unroll=2)

    def finish(j, carry):
        k = j + SIDE
        for t in range(1, 5):
            ys = slice(t * 8 - 8, t * 8)
            rows = slice(t * 8, t * 8 + 8)
            now = [u[c][0][k, 8 + t * 8 : 16 + t * 8, :] for c in range(2)]
            rest = [dg[c, k - 1, rows, :] * (update(c, k, t, (0,))[0] - now[c]) for c in range(2)]
            for ref, (v0, v1) in ((sol, now), (res, rest)):
                ref[2 * j, ys, :] = jnp.where(is_odd, v1, v0)
                ref[2 * j + 1, ys, :] = jnp.where(is_odd, v0, v1)
        return carry

    lax.fori_loop(0, HALF, finish, 0, unroll=2)


def on_vmem(kernel, out_shape, scratch, name, limit, *args):
    vmem = pl.BlockSpec(memory_space=pltpu.VMEM)
    return pl.pallas_call(
        kernel,
        out_shape=out_shape,
        in_specs=[vmem] * len(args),
        out_specs=tuple([vmem] * len(out_shape)),
        scratch_shapes=scratch,
        compiler_params=pltpu.CompilerParams(vmem_limit_bytes=limit * MIB),
        name=name,
    )(*args)


def pack_y(home, x_even, x_odd):
    face = jax.ShapeDtypeStruct((3 * PAIRS + PAIRS // 2, 8, 128), F32)
    return on_vmem(pack_y_kernel, (face, face), [], "pack_y", 10, home, x_even, x_odd)


def pack_z(home, x_even, x_odd, y_even, y_odd):
    grown = [jax.ShapeDtypeStruct((PAIRS, 48 + 2 * PAD[n], 128), F32) for n in range(7)]
    face = jax.ShapeDtypeStruct((PAIRS, 3, 8, 128), F32)
    return on_vmem(pack_z_kernel, (*grown, face), [], "pack_z", 16, home, x_even, x_odd, y_even, y_odd)


def sweeps(grown, z_even, z_odd):
    block = jax.ShapeDtypeStruct((BOX, BOX, 128), F32)
    padded = pltpu.VMEM((PAIRS, 64, 128), F32)
    scratch = [padded] * 6 + [
        pltpu.VMEM((4, PAIRS, 48, 128), F32),
        pltpu.VMEM((2, 2, 7, PAIRS - 2, 48, 128), F32),
        pltpu.VMEM((2, PAIRS - 2, 48, 128), F32),
    ]
    return on_vmem(sweep_kernel, (block, block), scratch, "sweeps", 40, *grown, z_even, z_odd)


def exchange(axis, count, even, odd):
    pairs = []
    for start in (0, 1):
        step = []
        for i in range(start, count, 2):
            j = (i + 1) % count
            step += [(i, j), (j, i)]
        pairs.append(step)
    return lax.ppermute(even, axis, pairs[0]), lax.ppermute(odd, axis, pairs[1])


def per_device(solution_old, right_side, acoef, bcoef, corners):
    fields = (solution_old, right_side, acoef, bcoef)
    plan, *pays = plan_and_pack(corners, fields)
    gots = [swap_round(plan[k], pays[k]) for k in range(ROUNDS)]
    home, even, odd = assemble(plan, fields, gots)
    x_even, x_odd = exchange("gx", N_GX, even, odd)
    y_even, y_odd = exchange("gy", N_GY, *pack_y(home, x_even, x_odd))
    *grown, face = pack_z(home, x_even, x_odd, y_even, y_odd)
    z_even, z_odd = exchange("gz", N_GZ, face, face)
    return sweeps(grown, z_even, z_odd)


def solution(mesh):
    boxes = P(("gx", "gy", "gz"), None, None)
    block = P("gx", "gy", "gz")
    return jax.shard_map(
        per_device,
        mesh=mesh,
        in_specs=(boxes, boxes, boxes, boxes, P()),
        out_specs=(block, block),
        check_vma=False,
    )
```

```python
import functools
import itertools

import jax
import jax.numpy as jnp
from jax import lax
from jax.experimental import pallas as pl
from jax.experimental.pallas import tpu as pltpu
from jax.sharding import PartitionSpec as P

BOX = 32
N_GX, N_GY, N_GZ = 4, 8, 8
PER_DEV = 4
ROUNDS = 3
HALF = BOX // 2
SIDE = 3
PAIRS = HALF + 2 * SIDE
SENT = PAIRS - 2
SWEEPS = 2
F32 = jnp.float32
MIB = 1024 * 1024


def _colourings():
    table = {}
    for p1, p2 in itertools.combinations(range(1, 7), 2):
        codes = set()
        for cyc in itertools.product(range(3), repeat=7):
            if any(cyc[p] == cyc[p - 1] for p in range(7)):
                continue
            if [3 - cyc[p] - cyc[p - 1] for p in (0, p1, p2)] == [0, 1, 2]:
                codes.add(sum(c << (2 * i) for i, c in enumerate(list(cyc) + [0, 1, 2])))
        codes = sorted(codes)
        table[p1 * 7 + p2] = [codes[i % len(codes)] for i in range(CHOICES)]
    return table


CHOICES = 4
COLOURINGS = _colourings()
ORDERS = [sum(c << (2 * i) for i, c in enumerate(o)) for o in itertools.permutations(range(3))]


def _pick(flag, yes, no):
    return jnp.where(flag, jnp.int32(yes) if isinstance(yes, int) else yes, jnp.int32(no) if isinstance(no, int) else no)


def _chain(index, values):
    out = values[-1]
    for i in reversed(range(len(values) - 1)):
        out = jnp.where(index == i, values[i], out)
    return out


def _colour(code, edge):
    return lax.shift_right_logical(code, 2 * edge) & 3


def plan_kernel(
    table, f0, f1, f2, f3, plan, pay0, pay1, pay2, corners, own, succ, swap, spot, ubox, rows8, sems, sem
):
    whole = pltpu.make_async_copy(table, corners, sem)
    whole.start()
    whole.wait()
    gx, me, gz = lax.axis_index("gx"), lax.axis_index("gy"), lax.axis_index("gz")
    stride = N_GZ * PER_DEV
    bases = [gx * (N_GY * stride) + ((gz & 6) + c) * PER_DEV for c in range(2)]

    groups = []
    for c, base in enumerate(bases):
        hot = jnp.int32(0)
        rows = []
        for g in range(N_GY):
            row = [lax.shift_right_logical(corners[1, base + g * stride + s], 5) for s in range(PER_DEV)]
            rows.append(row)
            leaving = sum(_pick(o != g, 1, 0) for o in row)
            hot = hot + _pick(leaving == 3, g, 0)
            for s in range(PER_DEV):
                own[c * 32 + g * PER_DEV + s] = row[s]
        first = jnp.int32(0)
        for g in reversed(range(N_GY)):
            to_hot = jnp.int32(0)
            nxt = jnp.int32(0)
            for o in rows[g]:
                to_hot = to_hot + _pick(o == hot, 1, 0)
                nxt = nxt + _pick((o != g) & (o != hot), o, 0)
            is_swap = _pick(hot == g, 0, to_hot)
            succ[c * 8 + g] = nxt
            swap[c * 8 + g] = is_swap
            first = _pick(is_swap == 1, g, first)
        v = first
        p1 = jnp.int32(0)
        p2 = jnp.int32(0)
        mine = jnp.int32(-1)
        pred = jnp.int32(0)
        cycle = []
        for p in range(7):
            spot[c * 8 + p] = v
            cycle.append(v)
            if p:
                sw = swap[c * 8 + v] == 1
                p2 = _pick(sw & (p1 != 0), p, p2)
                p1 = _pick(sw & (p1 == 0), p, p1)
            mine = _pick(v == me, p, mine)
            nxt = succ[c * 8 + v]
            pred = _pick(nxt == me, v, pred)
            v = nxt
        key = p1 * 7 + p2
        codes = [jnp.int32(0)] * CHOICES
        for k, options in COLOURINGS.items():
            codes = [_pick(key == k, o, code) for o, code in zip(options, codes)]
        swaps = [cycle[0], spot[c * 8 + p1], spot[c * 8 + p2]]
        groups.append((hot, cycle, swaps, codes, mine, pred, p1))

    link, lane = iota(0), iota(1)
    order = _chain(lane & 7, ORDERS + ORDERS[:2])
    load = [jnp.zeros((8, 128), jnp.int32) for _ in range(2)]
    for c in range(2):
        hot, cycle, swaps, codes = groups[c][:4]
        code = _chain(lax.shift_right_logical(lane, 5 - 2 * c) & 3, codes)
        for e in range(10):
            colour = _colour(code, e)
            if c:
                colour = lax.shift_right_logical(order, 2 * colour) & 3
            unit = lax.shift_left(jnp.ones((8, 128), jnp.int32), 8 * colour)
            flows = [(cycle[e], cycle[(e + 1) % 7])] if e < 7 else [(hot, swaps[e - 7]), (swaps[e - 7], hot)]
            for i, j in flows:
                d = (j - i) & 7
                ahead = _pick(d <= 4, d, 0)
                back = _pick(d <= 4, 0, 8 - d)
                load[0] = load[0] + jnp.where(((link - i) & 7) < ahead, unit, 0)
                load[1] = load[1] + jnp.where(((i - link) & 7) < back, unit, 0)
    cost = jnp.zeros((8, 128), F32)
    for r in range(ROUNDS):
        busiest = jnp.maximum(*[(lax.shift_right_logical(v, 8 * r) & 255).astype(F32) for v in load])
        for shift in (4, 2, 1):
            busiest = jnp.maximum(busiest, sroll(busiest, shift))
        cost = cost + busiest
    best = jnp.min(cost * 128.0 + lane.astype(F32)).astype(jnp.int32) & 127

    mine_second = (gz & 1) == 1

    def of_mine(values):
        return jnp.where(mine_second, values[1], values[0])

    code_a = _chain(lax.shift_right_logical(best, 5) & 3, groups[0][3])
    code_b = _chain(lax.shift_right_logical(best, 3) & 3, groups[1][3])
    order = jnp.where(mine_second, _chain(best & 7, [jnp.int32(o) for o in ORDERS + ORDERS[:2]]), ORDERS[0])
    code = of_mine((code_a, code_b))

    def round_of(edge):
        return lax.shift_right_logical(order, 2 * _colour(code, edge)) & 3

    hot = of_mine([g[0] for g in groups])
    spots = [of_mine([g[2][i] for g in groups]) for i in range(3)]
    mine, pred, p1 = [of_mine([g[i] for g in groups]) for i in (4, 5, 6)]
    c8, c32 = (gz & 1) * 8, (gz & 1) * 32
    base = of_mine(bases)

    def inner(g, s):
        return lax.shift_right_logical(corners[2, base + g * stride + s], 5) & 3

    star = [round_of(7 + i) for i in range(3)]
    is_hot = me == hot
    at = jnp.maximum(mine, 0)
    out_round = round_of(at)
    in_round = round_of(_pick(at == 0, 6, at - 1))
    my_succ = succ[c8 + me]
    swaps_here = jnp.logical_not(is_hot) & (swap[c8 + me] == 1)
    swap_at = _pick(swaps_here, _pick(at == 0, star[0], _pick(at == p1, star[1], star[2])), -1)
    places, arrives, slots = [], [], []
    for k in range(ROUNDS):
        hot_partner = sum(_pick(star[i] == k, spots[i], 0) for i in range(3))
        kind = _pick(swap_at == k, 3, _pick(out_round == k, 1, _pick(in_round == k, 2, 0)))
        partner = _pick(swap_at == k, hot, _pick(out_round == k, my_succ, pred))
        kind = _pick(is_hot, 3, kind)
        partner = _pick(is_hot, hot_partner, partner)
        way = me ^ partner
        up = ((kind == 1) & (me < partner)) | ((kind == 2) & (partner < me))
        plan[k] = _pick(kind == 0, 0, _pick(kind == 3, way, _pick(up, 7 + way, 14 + way)))
        slot = jnp.int32(0)
        place = jnp.int32(0)
        for s in range(PER_DEV):
            slot = slot + _pick(own[c32 + me * PER_DEV + s] == partner, s, 0)
            place = place + _pick(own[c32 + partner * PER_DEV + s] == me, inner(partner, s), 0)
        slots.append(jnp.minimum(slot, PER_DEV - 1))
        places.append(place)
        arrives.append((kind == 2) | (kind == 3))
    pays = (pay0, pay1, pay2)
    u_copies = [pltpu.make_async_copy(f0.at[slots[k]], ubox.at[k], sems.at[k, 3]) for k in range(ROUNDS)]
    copies = [
        pltpu.make_async_copy(field.at[slots[k]], pays[k].at[pl.ds(f * BOX, BOX)], sems.at[k, f])
        for k in range(ROUNDS)
        for f, field in enumerate((f1, f2, f3))
    ]
    for copy in u_copies + copies:
        copy.start()
    for q in range(PER_DEV):
        source = jnp.int32(0)
        for s in range(PER_DEV):
            source = source + _pick((own[c32 + me * PER_DEV + s] == me) & (inner(me, s) == q), s, 0)
        for k in range(ROUNDS):
            source = source + _pick(arrives[k] & (places[k] == q), 4 + k, 0)
        plan[4 + q] = source
    plan[3] = jnp.int32(0)
    for k in range(ROUNDS):
        u_copies[k].wait()
        halve(ubox.at[k], rows8.at[k], pays[k].at[pl.ds(3 * BOX, HALF)])
    for copy in copies:
        copy.wait()


def halve(box, tmp, out):
    lane = iota(1)
    is_odd = ((lax.shift_right_logical(lane, 5) + lane) & 1) == 1
    for j in range(8):
        tmp[j] = box[:, j * 128 : j * 128 + 128]
    for h in range(2):
        for j in range(8):
            lower = tmp[j, pl.ds(16 * h, 8, stride=2), :]
            upper = tmp[j, pl.ds(16 * h + 1, 8, stride=2), :]
            out[8 * h : 8 * h + 8, j * 128 : j * 128 + 128] = jnp.where(is_odd, lower, upper)


def plan_and_pack(corners, fields):
    hbm = pl.BlockSpec(memory_space=pltpu.HBM)
    smem = pl.BlockSpec(memory_space=pltpu.SMEM)
    vmem = pl.BlockSpec(memory_space=pltpu.VMEM)
    pay = jax.ShapeDtypeStruct((3 * BOX + HALF, BOX * BOX), F32)
    return pl.pallas_call(
        plan_kernel,
        out_shape=(jax.ShapeDtypeStruct((8,), jnp.int32), pay, pay, pay),
        in_specs=[hbm] * 5,
        out_specs=(smem, vmem, vmem, vmem),
        scratch_shapes=[
            pltpu.SMEM(corners.shape, jnp.int32),
            pltpu.SMEM((64,), jnp.int32),
            pltpu.SMEM((16,), jnp.int32),
            pltpu.SMEM((16,), jnp.int32),
            pltpu.SMEM((16,), jnp.int32),
            pltpu.VMEM((ROUNDS, BOX, BOX * BOX), F32),
            pltpu.VMEM((ROUNDS, 8, BOX, 128), F32),
            pltpu.SemaphoreType.DMA((ROUNDS, 4)),
            pltpu.SemaphoreType.DMA,
        ],
        compiler_params=pltpu.CompilerParams(vmem_limit_bytes=60 * MIB),
        name="plan",
    )(corners, *fields)


def swap_round(branch, pay):
    def stay(x):
        return x

    def move(pairs, x):
        return lax.ppermute(x, "gy", pairs)

    branches = [stay]
    for r in range(1, 8):
        branches.append(functools.partial(move, [(i, i ^ r) for i in range(8)]))
    for r in range(1, 8):
        branches.append(functools.partial(move, [(i, i ^ r) for i in range(8) if i < i ^ r]))
    for r in range(1, 8):
        branches.append(functools.partial(move, [(i, i ^ r) for i in range(8) if i > i ^ r]))
    return lax.switch(branch, branches, pay)


def iota(dim):
    return lax.broadcasted_iota(jnp.int32, (8, 128), dim)


def lroll(v, shift):
    shift %= 128
    return pltpu.roll(v, shift, 1) if shift else v


def sroll(v, shift):
    shift %= 8
    return pltpu.roll(v, shift, 0) if shift else v


U1, B1, B0, F0, A0, F1, A1 = range(7)
WIDTH = (5, 5, 4, 4, 4, 3, 3)
LAYERS = [(n, i) for n in range(7) for i in range(3 if n < 2 else 2)]


def odd_cell():
    return ((iota(0) + iota(1)) & 1) == 1


def assemble_kernel(plan, f0, f1, f2, f3, r0, r1, r2, home, even, odd, ubox, uhalf, rows8, raw, tmp, sems):
    fields = (f1, f2, f3)
    gots = (r0, r1, r2)
    rows = pl.ds(3 * BOX, HALF)
    for q in range(PER_DEV):
        source = plan[4 + q]

        @pl.when(source < 4)
        def _():
            box = jnp.minimum(source, 3)
            pltpu.make_async_copy(f0.at[box], ubox.at[q], sems.at[3, q]).start()
            for f in range(3):
                pltpu.make_async_copy(fields[f].at[box], raw.at[f, q], sems.at[f, q]).start()

        for k in range(ROUNDS):

            @pl.when(source == 4 + k)
            def _():
                pltpu.make_async_copy(gots[k].at[rows], uhalf.at[q], sems.at[3, q]).start()
                for f in range(3):
                    pltpu.make_async_copy(gots[k].at[pl.ds(f * BOX, BOX)], raw.at[f, q], sems.at[f, q]).start()

    lane = iota(1)
    m64 = (lane & 64) != 0
    m32 = (lane & 32) != 0
    is_odd = odd_cell()

    def relayout(load):
        for t in range(4):
            for jj in range(2):
                j = 2 * t + jj
                a = [load(k, slice(j * 128, (j + 1) * 128)) for k in range(4)]
                n0 = jnp.where(m64, lroll(a[2], 64), a[0])
                n2 = jnp.where(m64, a[2], lroll(a[0], 64))
                n1 = jnp.where(m64, lroll(a[3], 64), a[1])
                n3 = jnp.where(m64, a[3], lroll(a[1], 64))
                b = [
                    jnp.where(m32, lroll(n1, 32), n0),
                    jnp.where(m32, n1, lroll(n0, 96)),
                    jnp.where(m32, lroll(n3, 32), n2),
                    jnp.where(m32, n3, lroll(n2, 96)),
                ]
                for q in range(4):
                    y = jj * 4 + q
                    tmp[t, y * 8 : y * 8 + 8, :] = b[q]

    for f in range(3):
        for q in range(PER_DEV):
            pltpu.make_async_copy(f0.at[0], raw.at[f, q], sems.at[f, q]).wait()

        def step(i, carry):
            xt = pl.multiple_of(i * 8, 8)
            relayout(lambda k, lanes: raw[f, k, pl.ds(xt, 8), lanes])
            for t in range(4):
                ys = slice(t * 8, t * 8 + 8)
                for x in range(0, 8, 2):
                    lower = tmp[t, pl.ds(x, 8, stride=8), :]
                    upper = tmp[t, pl.ds(x + 1, 8, stride=8), :]
                    j = i * 4 + x // 2
                    home[(F1, A1, B1)[f], j, ys, :] = jnp.where(is_odd, lower, upper)
                    home[(F0, A0, B0)[f], j, ys, :] = jnp.where(is_odd, upper, lower)
            return carry

        lax.fori_loop(0, 4, step, 0, unroll=2)

    for q in range(PER_DEV):
        mine = plan[4 + q] < 4

        @pl.when(mine)
        def _():
            pltpu.make_async_copy(f0.at[0], ubox.at[q], sems.at[3, q]).wait()
            halve(ubox.at[q], rows8.at[q], uhalf.at[q])

        @pl.when(jnp.logical_not(mine))
        def _():
            pltpu.make_async_copy(r0.at[rows], uhalf.at[q], sems.at[3, q]).wait()

    for i in range(2):
        relayout(lambda k, lanes: uhalf[k, 8 * i : 8 * i + 8, lanes])
        for t in range(4):
            for x in range(8):
                home[U1, i * 8 + x, t * 8 : t * 8 + 8, :] = tmp[t, pl.ds(x, 8, stride=8), :]

    low = (lax.axis_index("gx") & 1) == 1
    for k, (n, i) in enumerate(LAYERS):
        last = HALF - (3 if n < 2 else 2) + i
        even[k] = home[n, jnp.where(low, i, last)]
        odd[k] = home[n, jnp.where(low, last, i)]


def assemble(plan, fields, gots):
    any_spec = pl.BlockSpec(memory_space=pl.ANY)
    hbm = pl.BlockSpec(memory_space=pltpu.HBM)
    vmem = pl.BlockSpec(memory_space=pltpu.VMEM)
    face = jax.ShapeDtypeStruct((16, BOX, 128), F32)
    return pl.pallas_call(
        assemble_kernel,
        out_shape=(jax.ShapeDtypeStruct((7, HALF, BOX, 128), F32), face, face),
        in_specs=[pl.BlockSpec(memory_space=pltpu.SMEM)] + [hbm] * 4 + [any_spec] * 3,
        out_specs=(vmem, vmem, vmem),
        scratch_shapes=[
            pltpu.VMEM((PER_DEV, BOX, BOX * BOX), F32),
            pltpu.VMEM((PER_DEV, HALF, BOX * BOX), F32),
            pltpu.VMEM((PER_DEV, 8, BOX, 128), F32),
            pltpu.VMEM((3, PER_DEV, BOX, BOX * BOX), F32),
            pltpu.VMEM((4, 64, 128), F32),
            pltpu.SemaphoreType.DMA((4, PER_DEV)),
        ],
        compiler_params=pltpu.CompilerParams(vmem_limit_bytes=12 * MIB),
        name="assemble",
    )(plan, *fields, *gots)


def halo_of(axis, count, even, odd):
    i = lax.axis_index(axis)
    low_first = (i & 1) == 1
    low = jnp.where(i > 0, jnp.where(low_first, even, odd), 0.0)
    high = jnp.where(i < count - 1, jnp.where(low_first, odd, even), 0.0)
    return low, high


def x_halo_tiles(even, odd, t):
    ys = slice(t * 8, t * 8 + 8)
    pairs = {}
    for k, (n, i) in enumerate(LAYERS):
        low, high = halo_of("gx", N_GX, even[k, ys, :], odd[k, ys, :])
        pairs.setdefault(SIDE - (3 if n < 2 else 2) + i, {})[n] = low
        pairs.setdefault(SIDE + HALF + i, {})[n] = high
    return pairs


def pack_y_kernel(home, x_even, x_odd, even, odd):
    low = (lax.axis_index("gy") & 1) == 1
    sub = iota(0)

    def put(at, lo, hi):
        even[at] = jnp.where(low, lo, hi)
        odd[at] = jnp.where(low, hi, lo)

    def put_pairs(k, first, second):
        for i, (near, far) in enumerate((first, second)):
            at = 3 * (k - 1 + i)
            put(at, jnp.where(sub < 5, near[U1], sroll(near[F1], 5)), jnp.where(sub < 5, sroll(far[U1], -3), far[F1]))
            put(at + 1, jnp.where(sub < 5, near[B1], sroll(near[A1], 5)), jnp.where(sub < 5, sroll(far[B1], -3), far[A1]))
            put(at + 2, jnp.where(sub < 4, near[B0], sroll(near[F0], 4)), jnp.where(sub < 4, sroll(far[B0], 4), far[F0]))
        (n0, f0), (n1, f1) = first, second
        lo = jnp.where(sub < 4, n0[A0], sroll(n1[A0], 4))
        hi = jnp.where(sub < 4, sroll(f0[A0], 4), f1[A0])
        put(3 * SENT + k // 2, lo, hi)

    halo = (x_halo_tiles(x_even, x_odd, 0), x_halo_tiles(x_even, x_odd, 3))
    zero = jnp.zeros((8, 128), F32)

    def tiles(k):
        inside = SIDE <= k < SIDE + HALF
        out = []
        for near_far in range(2):
            ys = slice(24 * near_far, 24 * near_far + 8)
            if inside:
                out.append([home[n, k - SIDE, ys, :] for n in range(7)])
            else:
                out.append([halo[near_far][k].get(n, zero) for n in range(7)])
        return out

    for k in range(1, PAIRS - 1, 2):
        put_pairs(k, tiles(k), tiles(k + 1))


PAD = (8, 8, 8, 0, 0, 0, 0)


def pack_z_kernel(home, x_even, x_odd, y_even, y_odd, u1, b1, b0, f0, a0, f1, a1, face):
    outs = (u1, b1, b0, f0, a0, f1, a1)

    def copy(j, carry):
        for n in range(7):
            outs[n][j + SIDE, PAD[n] + 8 : PAD[n] + 40, :] = home[n, j]
        return carry

    lax.fori_loop(0, HALF, copy, 0, unroll=2)
    for t in range(4):
        for k, tiles in x_halo_tiles(x_even, x_odd, t).items():
            for n, tile in tiles.items():
                outs[n][k, PAD[n] + 8 + t * 8 : PAD[n] + 16 + t * 8, :] = tile

    def halo(m, carry):
        l3, h3 = halo_of("gy", N_GY, y_even[3 * SENT + m], y_odd[3 * SENT + m])
        for i in range(2):
            k = 2 * m + 1 + i
            (l0, h0), (l1, h1), (l2, h2) = [
                halo_of("gy", N_GY, y_even[3 * k - 3 + w], y_odd[3 * k - 3 + w]) for w in range(3)
            ]
            lows = (sroll(l0, 3), sroll(l1, 3), sroll(l2, 4), l2, sroll(l3, 4) if i == 0 else l3, l0, l1)
            highs = (h0, h1, h2, sroll(h2, 4), h3 if i == 0 else sroll(h3, 4), sroll(h0, 3), sroll(h1, 3))
            for n in range(7):
                outs[n][k, PAD[n] : PAD[n] + 8, :] = lows[n]
                outs[n][k, PAD[n] + 40 : PAD[n] + 48, :] = highs[n]
        return carry

    lax.fori_loop(0, SENT // 2, halo, 0)
    lane = iota(1)
    place = lane & 63

    def pack(k, carry):
        for v in range(3):
            both = []
            for w in range(2):
                t = 2 * v + w
                at = 64 * w
                group = None
                ends = []
                for n in range(7):
                    tile = outs[n][k, PAD[n] + t * 8 : PAD[n] + t * 8 + 8, :]
                    ends.append((lroll(tile, at + WIDTH[n]), at + 2 * WIDTH[n]))
                    at += 2 * WIDTH[n]
                group = ends[-1][0]
                for tile, end in reversed(ends[:-1]):
                    group = jnp.where(place < end - 64 * w, tile, group)
                both.append(group)
            face[k - 1, v] = jnp.where(lane < 64, both[0], both[1])
        return carry

    lax.fori_loop(1, PAIRS - 1, pack, 0, unroll=2)


def sweep_kernel(u1, b1, b0, f0, a0, f1, a1, z_even, z_odd, sol, res, um0, um1, ua0, ua1, ba0, ba1, fax, co, dg):
    lane = iota(1)
    first, last = lane == 0, lane == 127
    place = lane & 63
    is_odd = odd_cell()
    u = ((um0, ua0), (um1, ua1))
    b = ((b0, ba0), (b1, ba1))
    fa = (((f0, a0), (fax.at[0], fax.at[1])), ((f1, a1), (fax.at[2], fax.at[3])))
    starts = [2 * sum(WIDTH[:n]) for n in range(7)]
    high_part = functools.reduce(
        jnp.logical_or, [(place >= starts[n]) & (place < starts[n] + WIDTH[n]) for n in range(7)]
    )
    aux = (ua1, ba1, ba0, fax.at[0], fax.at[1], fax.at[2], fax.at[3])

    def unpack(k, carry):
        for v in range(3):
            low, high = halo_of("gz", N_GZ, z_even[k - 1, v], z_odd[k - 1, v])
            both = jnp.where(high_part, low, high)
            for w in range(2):
                t = 2 * v + w
                for n in range(7):
                    aux[n][k, PAD[n] + t * 8 : PAD[n] + t * 8 + 8, :] = lroll(both, -(64 * w + starts[n] + WIDTH[n]))
        return carry

    um1[...] = u1[...]
    lax.fori_loop(1, PAIRS - 1, unpack, 0, unroll=2)

    def around(c, field, k, t, spans):
        r = 8 + t * 8
        main, side = field[1 - c]
        m, a = main[k, r : r + 8, :], side[k, r : r + 8, :]
        m1, a1 = lroll(m, 1), lroll(a, 1)
        m2, a2 = lroll(m, 127), lroll(a, 127)
        below = (jnp.where(first, a1, m1), jnp.where(first, m1, a1))
        above = (jnp.where(last, a2, m2), jnp.where(last, m2, a2))
        out = []
        for s in spans:
            ref = (main, side)[s]
            back, ahead = ref[k - 1, r : r + 8, :], ref[k + 1, r : r + 8, :]
            beside = jnp.where(is_odd, back, ahead) if c else jnp.where(is_odd, ahead, back)
            out.append(((m, a)[s], beside, ref[k, r - 1 : r + 7, :], ref[k, r + 1 : r + 9, :], below[s], above[s]))
        return out

    def coefs(k, carry):
        for c in range(2):
            for t in range(6):
                rows = slice(t * 8, 8 + t * 8)
                near = around(c, b, k, t, (0, 1))
                for s in range(2):
                    mid = b[c][s][k, 8 + t * 8 : 16 + t * 8, :]
                    f, a = [ref[k, rows, :] for ref in fa[c][s]]
                    faces = [0.5 * (mid + v) for v in near[s]]
                    diag = a + (faces[0] + faces[1]) + (faces[2] + faces[3]) + (faces[4] + faces[5])
                    inverse = jnp.where(mid > 0, 1.0 / diag, 0.0)
                    for n in range(6):
                        co[c, s, n, k - 1, rows, :] = faces[n] * inverse
                    co[c, s, 6, k - 1, rows, :] = f * inverse
                    if s == 0:
                        dg[c, k - 1, rows, :] = diag
        return carry

    lax.fori_loop(1, PAIRS - 1, coefs, 0)

    def update(c, k, t, spans):
        rows = slice(t * 8, 8 + t * 8)
        new = []
        for s, v in zip(spans, around(c, u, k, t, spans)):
            w = [co[c, s, n, k - 1, rows, :] for n in range(7)]
            x = w[0] * v[0] + w[1] * v[1]
            y = w[2] * v[2] + w[3] * v[3]
            z = w[4] * v[4] + w[5] * v[5]
            new.append(w[6] + ((x + y) + z))
        return new

    for half in range(2 * SWEEPS):
        c = half % 2

        def sweep(k, carry):
            for t in range(6):
                for s, new in enumerate(update(c, k, t, (0, 1))):
                    u[c][s][k, 8 + t * 8 : 16 + t * 8, :] = new
            return carry

        out = half // 2
        lax.fori_loop(1 + out, PAIRS - 1 - out, sweep, 0, unroll=2)

    def finish(j, carry):
        k = j + SIDE
        for t in range(1, 5):
            ys = slice(t * 8 - 8, t * 8)
            rows = slice(t * 8, t * 8 + 8)
            now = [u[c][0][k, 8 + t * 8 : 16 + t * 8, :] for c in range(2)]
            rest = [dg[c, k - 1, rows, :] * (update(c, k, t, (0,))[0] - now[c]) for c in range(2)]
            for ref, (v0, v1) in ((sol, now), (res, rest)):
                ref[2 * j, ys, :] = jnp.where(is_odd, v1, v0)
                ref[2 * j + 1, ys, :] = jnp.where(is_odd, v0, v1)
        return carry

    lax.fori_loop(0, HALF, finish, 0, unroll=2)


def on_vmem(kernel, out_shape, scratch, name, limit, *args):
    vmem = pl.BlockSpec(memory_space=pltpu.VMEM)
    return pl.pallas_call(
        kernel,
        out_shape=out_shape,
        in_specs=[vmem] * len(args),
        out_specs=tuple([vmem] * len(out_shape)),
        scratch_shapes=scratch,
        compiler_params=pltpu.CompilerParams(vmem_limit_bytes=limit * MIB),
        name=name,
    )(*args)


def pack_y(home, x_even, x_odd):
    face = jax.ShapeDtypeStruct((3 * SENT + SENT // 2, 8, 128), F32)
    return on_vmem(pack_y_kernel, (face, face), [], "pack_y", 10, home, x_even, x_odd)


def pack_z(home, x_even, x_odd, y_even, y_odd):
    grown = [jax.ShapeDtypeStruct((PAIRS, 48 + 2 * PAD[n], 128), F32) for n in range(7)]
    face = jax.ShapeDtypeStruct((SENT, 3, 8, 128), F32)
    return on_vmem(pack_z_kernel, (*grown, face), [], "pack_z", 16, home, x_even, x_odd, y_even, y_odd)


def sweeps(grown, z_even, z_odd):
    block = jax.ShapeDtypeStruct((BOX, BOX, 128), F32)
    padded = pltpu.VMEM((PAIRS, 64, 128), F32)
    scratch = [padded] * 6 + [
        pltpu.VMEM((4, PAIRS, 48, 128), F32),
        pltpu.VMEM((2, 2, 7, PAIRS - 2, 48, 128), F32),
        pltpu.VMEM((2, PAIRS - 2, 48, 128), F32),
    ]
    return on_vmem(sweep_kernel, (block, block), scratch, "sweeps", 40, *grown, z_even, z_odd)


def exchange(axis, count, even, odd):
    pairs = []
    for start in (0, 1):
        step = []
        for i in range(start, count, 2):
            j = (i + 1) % count
            step += [(i, j), (j, i)]
        pairs.append(step)
    return lax.ppermute(even, axis, pairs[0]), lax.ppermute(odd, axis, pairs[1])


def per_device(solution_old, right_side, acoef, bcoef, corners):
    fields = (solution_old, right_side, acoef, bcoef)
    plan, *pays = plan_and_pack(corners, fields)
    gots = [swap_round(plan[k], pays[k]) for k in range(ROUNDS)]
    home, even, odd = assemble(plan, fields, gots)
    x_even, x_odd = exchange("gx", N_GX, even, odd)
    y_even, y_odd = exchange("gy", N_GY, *pack_y(home, x_even, x_odd))
    *grown, face = pack_z(home, x_even, x_odd, y_even, y_odd)
    z_even, z_odd = exchange("gz", N_GZ, face, face)
    return sweeps(grown, z_even, z_odd)


def solution(mesh):
    boxes = P(("gx", "gy", "gz"), None, None)
    block = P("gx", "gy", "gz")
    return jax.shard_map(
        per_device,
        mesh=mesh,
        in_specs=(boxes, boxes, boxes, boxes, P()),
        out_specs=(block, block),
        check_vma=False,
    )
```

```python
import functools
import itertools

import jax
import jax.numpy as jnp
from jax import lax
from jax.experimental import pallas as pl
from jax.experimental.pallas import tpu as pltpu
from jax.sharding import PartitionSpec as P

BOX = 32
N_GX, N_GY, N_GZ = 4, 8, 8
PER_DEV = 4
ROUNDS = 3
HALF = BOX // 2
SIDE = 3
PAIRS = HALF + 2 * SIDE
SWEEPS = 2
F32 = jnp.float32
MIB = 1024 * 1024


def _colourings():
    table = {}
    for p1, p2 in itertools.combinations(range(1, 7), 2):
        codes = set()
        for cyc in itertools.product(range(3), repeat=7):
            if any(cyc[p] == cyc[p - 1] for p in range(7)):
                continue
            if [3 - cyc[p] - cyc[p - 1] for p in (0, p1, p2)] == [0, 1, 2]:
                codes.add(sum(c << (2 * i) for i, c in enumerate(list(cyc) + [0, 1, 2])))
        codes = sorted(codes)
        table[p1 * 7 + p2] = [codes[i % len(codes)] for i in range(CHOICES)]
    return table


CHOICES = 4
COLOURINGS = _colourings()
ORDERS = [sum(c << (2 * i) for i, c in enumerate(o)) for o in itertools.permutations(range(3))]


def _pick(flag, yes, no):
    return jnp.where(flag, jnp.int32(yes) if isinstance(yes, int) else yes, jnp.int32(no) if isinstance(no, int) else no)


def _chain(index, values):
    out = values[-1]
    for i in reversed(range(len(values) - 1)):
        out = jnp.where(index == i, values[i], out)
    return out


def _colour(code, edge):
    return lax.shift_right_logical(code, 2 * edge) & 3


def plan_kernel(
    table, f0, f1, f2, f3, plan, pay0, pay1, pay2, corners, own, succ, swap, spot, ubox, rows8, sems, sem
):
    whole = pltpu.make_async_copy(table, corners, sem)
    whole.start()
    whole.wait()
    gx, me, gz = lax.axis_index("gx"), lax.axis_index("gy"), lax.axis_index("gz")
    stride = N_GZ * PER_DEV
    bases = [gx * (N_GY * stride) + ((gz & 6) + c) * PER_DEV for c in range(2)]

    groups = []
    for c, base in enumerate(bases):
        hot = jnp.int32(0)
        rows = []
        for g in range(N_GY):
            row = [lax.shift_right_logical(corners[1, base + g * stride + s], 5) for s in range(PER_DEV)]
            rows.append(row)
            leaving = sum(_pick(o != g, 1, 0) for o in row)
            hot = hot + _pick(leaving == 3, g, 0)
            for s in range(PER_DEV):
                own[c * 32 + g * PER_DEV + s] = row[s]
        first = jnp.int32(0)
        for g in reversed(range(N_GY)):
            to_hot = jnp.int32(0)
            nxt = jnp.int32(0)
            for o in rows[g]:
                to_hot = to_hot + _pick(o == hot, 1, 0)
                nxt = nxt + _pick((o != g) & (o != hot), o, 0)
            is_swap = _pick(hot == g, 0, to_hot)
            succ[c * 8 + g] = nxt
            swap[c * 8 + g] = is_swap
            first = _pick(is_swap == 1, g, first)
        v = first
        p1 = jnp.int32(0)
        p2 = jnp.int32(0)
        mine = jnp.int32(-1)
        pred = jnp.int32(0)
        cycle = []
        for p in range(7):
            spot[c * 8 + p] = v
            cycle.append(v)
            if p:
                sw = swap[c * 8 + v] == 1
                p2 = _pick(sw & (p1 != 0), p, p2)
                p1 = _pick(sw & (p1 == 0), p, p1)
            mine = _pick(v == me, p, mine)
            nxt = succ[c * 8 + v]
            pred = _pick(nxt == me, v, pred)
            v = nxt
        key = p1 * 7 + p2
        codes = [jnp.int32(0)] * CHOICES
        for k, options in COLOURINGS.items():
            codes = [_pick(key == k, o, code) for o, code in zip(options, codes)]
        swaps = [cycle[0], spot[c * 8 + p1], spot[c * 8 + p2]]
        groups.append((hot, cycle, swaps, codes, mine, pred, p1))

    link, lane = iota(0), iota(1)
    order = _chain(lane & 7, ORDERS + ORDERS[:2])
    load = [jnp.zeros((8, 128), jnp.int32) for _ in range(2)]
    for c in range(2):
        hot, cycle, swaps, codes = groups[c][:4]
        code = _chain(lax.shift_right_logical(lane, 5 - 2 * c) & 3, codes)
        for e in range(10):
            colour = _colour(code, e)
            if c:
                colour = lax.shift_right_logical(order, 2 * colour) & 3
            unit = lax.shift_left(jnp.ones((8, 128), jnp.int32), 8 * colour)
            flows = [(cycle[e], cycle[(e + 1) % 7])] if e < 7 else [(hot, swaps[e - 7]), (swaps[e - 7], hot)]
            for i, j in flows:
                d = (j - i) & 7
                ahead = _pick(d <= 4, d, 0)
                back = _pick(d <= 4, 0, 8 - d)
                load[0] = load[0] + jnp.where(((link - i) & 7) < ahead, unit, 0)
                load[1] = load[1] + jnp.where(((i - link) & 7) < back, unit, 0)
    cost = jnp.zeros((8, 128), F32)
    for r in range(ROUNDS):
        busiest = jnp.maximum(*[(lax.shift_right_logical(v, 8 * r) & 255).astype(F32) for v in load])
        for shift in (4, 2, 1):
            busiest = jnp.maximum(busiest, sroll(busiest, shift))
        cost = cost + busiest
    best = jnp.min(cost * 128.0 + lane.astype(F32)).astype(jnp.int32) & 127

    mine_second = (gz & 1) == 1

    def of_mine(values):
        return jnp.where(mine_second, values[1], values[0])

    code_a = _chain(lax.shift_right_logical(best, 5) & 3, groups[0][3])
    code_b = _chain(lax.shift_right_logical(best, 3) & 3, groups[1][3])
    order = jnp.where(mine_second, _chain(best & 7, [jnp.int32(o) for o in ORDERS + ORDERS[:2]]), ORDERS[0])
    code = of_mine((code_a, code_b))

    def round_of(edge):
        return lax.shift_right_logical(order, 2 * _colour(code, edge)) & 3

    hot = of_mine([g[0] for g in groups])
    spots = [of_mine([g[2][i] for g in groups]) for i in range(3)]
    mine, pred, p1 = [of_mine([g[i] for g in groups]) for i in (4, 5, 6)]
    c8, c32 = (gz & 1) * 8, (gz & 1) * 32
    base = of_mine(bases)

    def inner(g, s):
        return lax.shift_right_logical(corners[2, base + g * stride + s], 5) & 3

    star = [round_of(7 + i) for i in range(3)]
    is_hot = me == hot
    at = jnp.maximum(mine, 0)
    out_round = round_of(at)
    in_round = round_of(_pick(at == 0, 6, at - 1))
    my_succ = succ[c8 + me]
    swaps_here = jnp.logical_not(is_hot) & (swap[c8 + me] == 1)
    swap_at = _pick(swaps_here, _pick(at == 0, star[0], _pick(at == p1, star[1], star[2])), -1)
    places, arrives, slots = [], [], []
    for k in range(ROUNDS):
        hot_partner = sum(_pick(star[i] == k, spots[i], 0) for i in range(3))
        kind = _pick(swap_at == k, 3, _pick(out_round == k, 1, _pick(in_round == k, 2, 0)))
        partner = _pick(swap_at == k, hot, _pick(out_round == k, my_succ, pred))
        kind = _pick(is_hot, 3, kind)
        partner = _pick(is_hot, hot_partner, partner)
        way = me ^ partner
        up = ((kind == 1) & (me < partner)) | ((kind == 2) & (partner < me))
        plan[k] = _pick(kind == 0, 0, _pick(kind == 3, way, _pick(up, 7 + way, 14 + way)))
        slot = jnp.int32(0)
        place = jnp.int32(0)
        for s in range(PER_DEV):
            slot = slot + _pick(own[c32 + me * PER_DEV + s] == partner, s, 0)
            place = place + _pick(own[c32 + partner * PER_DEV + s] == me, inner(partner, s), 0)
        slots.append(jnp.minimum(slot, PER_DEV - 1))
        places.append(place)
        arrives.append((kind == 2) | (kind == 3))
    pays = (pay0, pay1, pay2)
    u_copies = [pltpu.make_async_copy(f0.at[slots[k]], ubox.at[k], sems.at[k, 3]) for k in range(ROUNDS)]
    copies = [
        pltpu.make_async_copy(field.at[slots[k]], pays[k].at[pl.ds(f * BOX, BOX)], sems.at[k, f])
        for k in range(ROUNDS)
        for f, field in enumerate((f1, f2, f3))
    ]
    for copy in u_copies + copies:
        copy.start()
    for q in range(PER_DEV):
        source = jnp.int32(0)
        for s in range(PER_DEV):
            source = source + _pick((own[c32 + me * PER_DEV + s] == me) & (inner(me, s) == q), s, 0)
        for k in range(ROUNDS):
            source = source + _pick(arrives[k] & (places[k] == q), 4 + k, 0)
        plan[4 + q] = source
    plan[3] = jnp.int32(0)
    for k in range(ROUNDS):
        u_copies[k].wait()
        halve(ubox.at[k], rows8.at[k], pays[k].at[pl.ds(3 * BOX, HALF)])
    for copy in copies:
        copy.wait()


def halve(box, tmp, out):
    lane = iota(1)
    is_odd = ((lax.shift_right_logical(lane, 5) + lane) & 1) == 1
    for j in range(8):
        tmp[j] = box[:, j * 128 : j * 128 + 128]
    for h in range(2):
        for j in range(8):
            lower = tmp[j, pl.ds(16 * h, 8, stride=2), :]
            upper = tmp[j, pl.ds(16 * h + 1, 8, stride=2), :]
            out[8 * h : 8 * h + 8, j * 128 : j * 128 + 128] = jnp.where(is_odd, lower, upper)


def plan_and_pack(corners, fields):
    hbm = pl.BlockSpec(memory_space=pltpu.HBM)
    smem = pl.BlockSpec(memory_space=pltpu.SMEM)
    vmem = pl.BlockSpec(memory_space=pltpu.VMEM)
    pay = jax.ShapeDtypeStruct((3 * BOX + HALF, BOX * BOX), F32)
    return pl.pallas_call(
        plan_kernel,
        out_shape=(jax.ShapeDtypeStruct((8,), jnp.int32), pay, pay, pay),
        in_specs=[hbm] * 5,
        out_specs=(smem, vmem, vmem, vmem),
        scratch_shapes=[
            pltpu.SMEM(corners.shape, jnp.int32),
            pltpu.SMEM((64,), jnp.int32),
            pltpu.SMEM((16,), jnp.int32),
            pltpu.SMEM((16,), jnp.int32),
            pltpu.SMEM((16,), jnp.int32),
            pltpu.VMEM((ROUNDS, BOX, BOX * BOX), F32),
            pltpu.VMEM((ROUNDS, 8, BOX, 128), F32),
            pltpu.SemaphoreType.DMA((ROUNDS, 4)),
            pltpu.SemaphoreType.DMA,
        ],
        compiler_params=pltpu.CompilerParams(vmem_limit_bytes=60 * MIB),
        name="plan",
    )(corners, *fields)


def swap_round(branch, pay):
    def stay(x):
        return x

    def move(pairs, x):
        return lax.ppermute(x, "gy", pairs)

    branches = [stay]
    for r in range(1, 8):
        branches.append(functools.partial(move, [(i, i ^ r) for i in range(8)]))
    for r in range(1, 8):
        branches.append(functools.partial(move, [(i, i ^ r) for i in range(8) if i < i ^ r]))
    for r in range(1, 8):
        branches.append(functools.partial(move, [(i, i ^ r) for i in range(8) if i > i ^ r]))
    return lax.switch(branch, branches, pay)


def iota(dim):
    return lax.broadcasted_iota(jnp.int32, (8, 128), dim)


def lroll(v, shift):
    shift %= 128
    return pltpu.roll(v, shift, 1) if shift else v


def sroll(v, shift):
    shift %= 8
    return pltpu.roll(v, shift, 0) if shift else v


U1, B1, B0, F0, A0, F1, A1 = range(7)
WIDTH = (5, 5, 4, 4, 4, 3, 3)
LAYERS = [(n, i) for n in range(7) for i in range(3 if n < 2 else 2)]


def odd_cell():
    return ((iota(0) + iota(1)) & 1) == 1


def face_rows(first, second):
    sub = iota(0)
    out = []
    for near, far in (first, second):
        out.append((jnp.where(sub < 5, near[U1], sroll(near[F1], 5)), jnp.where(sub < 5, sroll(far[U1], -3), far[F1])))
        out.append((jnp.where(sub < 5, near[B1], sroll(near[A1], 5)), jnp.where(sub < 5, sroll(far[B1], -3), far[A1])))
        out.append((jnp.where(sub < 4, near[B0], sroll(near[F0], 4)), jnp.where(sub < 4, sroll(far[B0], 4), far[F0])))
    (n0, f0), (n1, f1) = first, second
    lo = jnp.where(sub < 4, n0[A0], sroll(n1[A0], 4))
    hi = jnp.where(sub < 4, sroll(f0[A0], 4), f1[A0])
    return out + [(lo, hi)]


def face_lanes(first, second):
    lane = iota(1)
    place = lane & 63
    both = []
    for w, tiles in enumerate((first, second)):
        at = 0
        ends = []
        for n in range(7):
            ends.append((lroll(tiles[n], 64 * w + at + WIDTH[n]), at + 2 * WIDTH[n]))
            at += 2 * WIDTH[n]
        group = ends[-1][0]
        for tile, end in reversed(ends[:-1]):
            group = jnp.where(place < end, tile, group)
        both.append(group)
    return jnp.where(lane < 64, both[0], both[1])


def assemble_kernel(
    plan, f0, f1, f2, f3, r0, r1, r2, home, even, odd, y_even, y_odd, z_face, ubox, uhalf, rows8, raw, tmp, sems
):
    fields = (f1, f2, f3)
    gots = (r0, r1, r2)
    rows = pl.ds(3 * BOX, HALF)
    for q in range(PER_DEV):
        source = plan[4 + q]

        @pl.when(source < 4)
        def _():
            box = jnp.minimum(source, 3)
            pltpu.make_async_copy(f0.at[box], ubox.at[q], sems.at[3, q]).start()
            for f in range(3):
                pltpu.make_async_copy(fields[f].at[box], raw.at[f, q], sems.at[f, q]).start()

        for k in range(ROUNDS):

            @pl.when(source == 4 + k)
            def _():
                pltpu.make_async_copy(gots[k].at[rows], uhalf.at[q], sems.at[3, q]).start()
                for f in range(3):
                    pltpu.make_async_copy(gots[k].at[pl.ds(f * BOX, BOX)], raw.at[f, q], sems.at[f, q]).start()

    lane = iota(1)
    m64 = (lane & 64) != 0
    m32 = (lane & 32) != 0
    is_odd = odd_cell()

    def relayout(load):
        for t in range(4):
            for jj in range(2):
                j = 2 * t + jj
                a = [load(k, slice(j * 128, (j + 1) * 128)) for k in range(4)]
                n0 = jnp.where(m64, lroll(a[2], 64), a[0])
                n2 = jnp.where(m64, a[2], lroll(a[0], 64))
                n1 = jnp.where(m64, lroll(a[3], 64), a[1])
                n3 = jnp.where(m64, a[3], lroll(a[1], 64))
                b = [
                    jnp.where(m32, lroll(n1, 32), n0),
                    jnp.where(m32, n1, lroll(n0, 96)),
                    jnp.where(m32, lroll(n3, 32), n2),
                    jnp.where(m32, n3, lroll(n2, 96)),
                ]
                for q in range(4):
                    y = jj * 4 + q
                    tmp[t, y * 8 : y * 8 + 8, :] = b[q]

    for f in range(3):
        for q in range(PER_DEV):
            pltpu.make_async_copy(f0.at[0], raw.at[f, q], sems.at[f, q]).wait()

        def step(i, carry):
            xt = pl.multiple_of(i * 8, 8)
            relayout(lambda k, lanes: raw[f, k, pl.ds(xt, 8), lanes])
            for t in range(4):
                ys = slice(t * 8, t * 8 + 8)
                for x in range(0, 8, 2):
                    lower = tmp[t, pl.ds(x, 8, stride=8), :]
                    upper = tmp[t, pl.ds(x + 1, 8, stride=8), :]
                    j = i * 4 + x // 2
                    home[(F1, A1, B1)[f], j, ys, :] = jnp.where(is_odd, lower, upper)
                    home[(F0, A0, B0)[f], j, ys, :] = jnp.where(is_odd, upper, lower)
            return carry

        lax.fori_loop(0, 4, step, 0, unroll=2)

    for q in range(PER_DEV):
        mine = plan[4 + q] < 4

        @pl.when(mine)
        def _():
            pltpu.make_async_copy(f0.at[0], ubox.at[q], sems.at[3, q]).wait()
            halve(ubox.at[q], rows8.at[q], uhalf.at[q])

        @pl.when(jnp.logical_not(mine))
        def _():
            pltpu.make_async_copy(r0.at[rows], uhalf.at[q], sems.at[3, q]).wait()

    for i in range(2):
        relayout(lambda k, lanes: uhalf[k, 8 * i : 8 * i + 8, lanes])
        for t in range(4):
            for x in range(8):
                home[U1, i * 8 + x, t * 8 : t * 8 + 8, :] = tmp[t, pl.ds(x, 8, stride=8), :]

    low = (lax.axis_index("gx") & 1) == 1
    for k, (n, i) in enumerate(LAYERS):
        last = HALF - (3 if n < 2 else 2) + i
        even[k] = home[n, jnp.where(low, i, last)]
        odd[k] = home[n, jnp.where(low, last, i)]

    low_y = (lax.axis_index("gy") & 1) == 1

    def faces(m, carry):
        tiles = [[[home[n, 2 * m + i, 8 * t : 8 * t + 8, :] for n in range(7)] for t in range(4)] for i in range(2)]
        for w, (lo, hi) in enumerate(face_rows(*[(tiles[i][0], tiles[i][3]) for i in range(2)])):
            y_even[7 * m + w] = jnp.where(low_y, lo, hi)
            y_odd[7 * m + w] = jnp.where(low_y, hi, lo)
        for i in range(2):
            for v in range(2):
                z_face[2 * m + i, v] = face_lanes(tiles[i][2 * v], tiles[i][2 * v + 1])
        return carry

    lax.fori_loop(0, HALF // 2, faces, 0)


def assemble(plan, fields, gots):
    any_spec = pl.BlockSpec(memory_space=pl.ANY)
    hbm = pl.BlockSpec(memory_space=pltpu.HBM)
    vmem = pl.BlockSpec(memory_space=pltpu.VMEM)
    face = jax.ShapeDtypeStruct((16, BOX, 128), F32)
    rows = jax.ShapeDtypeStruct((7 * HALF // 2, 8, 128), F32)
    return pl.pallas_call(
        assemble_kernel,
        out_shape=(
            jax.ShapeDtypeStruct((7, HALF, BOX, 128), F32),
            face,
            face,
            rows,
            rows,
            jax.ShapeDtypeStruct((HALF, 2, 8, 128), F32),
        ),
        in_specs=[pl.BlockSpec(memory_space=pltpu.SMEM)] + [hbm] * 4 + [any_spec] * 3,
        out_specs=(vmem,) * 6,
        scratch_shapes=[
            pltpu.VMEM((PER_DEV, BOX, BOX * BOX), F32),
            pltpu.VMEM((PER_DEV, HALF, BOX * BOX), F32),
            pltpu.VMEM((PER_DEV, 8, BOX, 128), F32),
            pltpu.VMEM((3, PER_DEV, BOX, BOX * BOX), F32),
            pltpu.VMEM((4, 64, 128), F32),
            pltpu.SemaphoreType.DMA((4, PER_DEV)),
        ],
        compiler_params=pltpu.CompilerParams(vmem_limit_bytes=12 * MIB),
        name="assemble",
    )(plan, *fields, *gots)


def halo_of(axis, count, even, odd):
    i = lax.axis_index(axis)
    low_first = (i & 1) == 1
    low = jnp.where(i > 0, jnp.where(low_first, even, odd), 0.0)
    high = jnp.where(i < count - 1, jnp.where(low_first, odd, even), 0.0)
    return low, high


def x_halo_tiles(even, odd, t):
    ys = slice(t * 8, t * 8 + 8)
    pairs = {}
    for k, (n, i) in enumerate(LAYERS):
        low, high = halo_of("gx", N_GX, even[k, ys, :], odd[k, ys, :])
        pairs.setdefault(SIDE - (3 if n < 2 else 2) + i, {})[n] = low
        pairs.setdefault(SIDE + HALF + i, {})[n] = high
    return pairs


EDGES = (1, 2, SIDE + HALF, SIDE + HALF + 1)


def edge_y_kernel(x_even, x_odd, even, odd):
    low = (lax.axis_index("gy") & 1) == 1
    near, far = x_halo_tiles(x_even, x_odd, 0), x_halo_tiles(x_even, x_odd, 3)
    for m in range(2):
        for w, (lo, hi) in enumerate(face_rows(*[(near[k], far[k]) for k in EDGES[2 * m : 2 * m + 2]])):
            even[7 * m + w] = jnp.where(low, lo, hi)
            odd[7 * m + w] = jnp.where(low, hi, lo)


PAD = (8, 8, 8, 0, 0, 0, 0)


def edge_z_kernel(home, x_even, x_odd, y_even, y_odd, e_even, e_odd, u1, b1, b0, f0, a0, f1, a1, edge):
    outs = (u1, b1, b0, f0, a0, f1, a1)

    def halo(even, odd, m, pairs):
        low_high = [halo_of("gy", N_GY, even[7 * m + w], odd[7 * m + w]) for w in range(7)]
        l3, h3 = low_high[6]
        for i, k in enumerate(pairs):
            (l0, h0), (l1, h1), (l2, h2) = low_high[3 * i : 3 * i + 3]
            lows = (sroll(l0, 3), sroll(l1, 3), sroll(l2, 4), l2, sroll(l3, 4) if i == 0 else l3, l0, l1)
            highs = (h0, h1, h2, sroll(h2, 4), h3 if i == 0 else sroll(h3, 4), sroll(h0, 3), sroll(h1, 3))
            for n in range(7):
                outs[n][k, PAD[n] : PAD[n] + 8, :] = lows[n]
                outs[n][k, PAD[n] + 40 : PAD[n] + 48, :] = highs[n]

    def tiles(k, t):
        return [outs[n][k, PAD[n] + t * 8 : PAD[n] + t * 8 + 8, :] for n in range(7)]

    def copy(m, carry):
        for i in range(2):
            for n in range(7):
                outs[n][2 * m + i + SIDE, PAD[n] + 8 : PAD[n] + 40, :] = home[n, 2 * m + i]
        halo(y_even, y_odd, m, (2 * m + SIDE, 2 * m + SIDE + 1))
        for i in range(2):
            k = 2 * m + i + SIDE
            edge[12 + 2 * m + i] = face_lanes(tiles(k, 0), tiles(k, 5))
        return carry

    lax.fori_loop(0, HALF // 2, copy, 0)
    for t in range(4):
        for k, fields in x_halo_tiles(x_even, x_odd, t).items():
            for n, tile in fields.items():
                outs[n][k, PAD[n] + 8 + t * 8 : PAD[n] + 16 + t * 8, :] = tile
    for m in range(2):
        halo(e_even, e_odd, m, EDGES[2 * m : 2 * m + 2])
    for i, k in enumerate(EDGES):
        for v in range(3):
            edge[3 * i + v] = face_lanes(tiles(k, 2 * v), tiles(k, 2 * v + 1))


def sweep_kernel(
    u1, b1, b0, f0, a0, f1, a1, z_even, z_odd, e_even, e_odd, sol, res, um0, um1, ua0, ua1, ba0, ba1, fax, co, dg
):
    lane = iota(1)
    first, last = lane == 0, lane == 127
    place = lane & 63
    is_odd = odd_cell()
    u = ((um0, ua0), (um1, ua1))
    b = ((b0, ba0), (b1, ba1))
    fa = (((f0, a0), (fax.at[0], fax.at[1])), ((f1, a1), (fax.at[2], fax.at[3])))
    starts = [2 * sum(WIDTH[:n]) for n in range(7)]
    high_part = functools.reduce(
        jnp.logical_or, [(place >= starts[n]) & (place < starts[n] + WIDTH[n]) for n in range(7)]
    )
    aux = (ua1, ba1, ba0, fax.at[0], fax.at[1], fax.at[2], fax.at[3])

    def unpack(k, even, odd, spots):
        low, high = halo_of("gz", N_GZ, even, odd)
        both = jnp.where(high_part, low, high)
        for w, t in enumerate(spots):
            for n in range(7):
                aux[n][k, PAD[n] + t * 8 : PAD[n] + t * 8 + 8, :] = lroll(both, -(64 * w + starts[n] + WIDTH[n]))

    def unpack_pair(j, carry):
        for v in range(2):
            unpack(j + SIDE, z_even[j, v], z_odd[j, v], (1 + 2 * v, 2 + 2 * v))
        unpack(j + SIDE, e_even[12 + j], e_odd[12 + j], (0, 5))
        return carry

    um1[...] = u1[...]
    lax.fori_loop(0, HALF, unpack_pair, 0, unroll=2)
    for i, k in enumerate(EDGES):
        for v in range(3):
            unpack(k, e_even[3 * i + v], e_odd[3 * i + v], (2 * v, 2 * v + 1))

    def around(c, field, k, t, spans):
        r = 8 + t * 8
        main, side = field[1 - c]
        m, a = main[k, r : r + 8, :], side[k, r : r + 8, :]
        m1, a1 = lroll(m, 1), lroll(a, 1)
        m2, a2 = lroll(m, 127), lroll(a, 127)
        below = (jnp.where(first, a1, m1), jnp.where(first, m1, a1))
        above = (jnp.where(last, a2, m2), jnp.where(last, m2, a2))
        out = []
        for s in spans:
            ref = (main, side)[s]
            back, ahead = ref[k - 1, r : r + 8, :], ref[k + 1, r : r + 8, :]
            beside = jnp.where(is_odd, back, ahead) if c else jnp.where(is_odd, ahead, back)
            out.append(((m, a)[s], beside, ref[k, r - 1 : r + 7, :], ref[k, r + 1 : r + 9, :], below[s], above[s]))
        return out

    def coefs(k, carry):
        for c in range(2):
            for t in range(6):
                rows = slice(t * 8, 8 + t * 8)
                near = around(c, b, k, t, (0, 1))
                for s in range(2):
                    mid = b[c][s][k, 8 + t * 8 : 16 + t * 8, :]
                    f, a = [ref[k, rows, :] for ref in fa[c][s]]
                    faces = [0.5 * (mid + v) for v in near[s]]
                    diag = a + (faces[0] + faces[1]) + (faces[2] + faces[3]) + (faces[4] + faces[5])
                    inverse = jnp.where(mid > 0, 1.0 / diag, 0.0)
                    for n in range(6):
                        co[c, s, n, k - 1, rows, :] = faces[n] * inverse
                    co[c, s, 6, k - 1, rows, :] = f * inverse
                    if s == 0:
                        dg[c, k - 1, rows, :] = diag
        return carry

    lax.fori_loop(1, PAIRS - 1, coefs, 0)

    def update(c, k, t, spans):
        rows = slice(t * 8, 8 + t * 8)
        new = []
        for s, v in zip(spans, around(c, u, k, t, spans)):
            w = [co[c, s, n, k - 1, rows, :] for n in range(7)]
            x = w[0] * v[0] + w[1] * v[1]
            y = w[2] * v[2] + w[3] * v[3]
            z = w[4] * v[4] + w[5] * v[5]
            new.append(w[6] + ((x + y) + z))
        return new

    for half in range(2 * SWEEPS):
        c = half % 2

        def sweep(k, carry):
            for t in range(6):
                for s, new in enumerate(update(c, k, t, (0, 1))):
                    u[c][s][k, 8 + t * 8 : 16 + t * 8, :] = new
            return carry

        out = half // 2
        lax.fori_loop(1 + out, PAIRS - 1 - out, sweep, 0, unroll=2)

    def finish(j, carry):
        k = j + SIDE
        for t in range(1, 5):
            ys = slice(t * 8 - 8, t * 8)
            rows = slice(t * 8, t * 8 + 8)
            now = [u[c][0][k, 8 + t * 8 : 16 + t * 8, :] for c in range(2)]
            rest = [dg[c, k - 1, rows, :] * (update(c, k, t, (0,))[0] - now[c]) for c in range(2)]
            for ref, (v0, v1) in ((sol, now), (res, rest)):
                ref[2 * j, ys, :] = jnp.where(is_odd, v1, v0)
                ref[2 * j + 1, ys, :] = jnp.where(is_odd, v0, v1)
        return carry

    lax.fori_loop(0, HALF, finish, 0, unroll=2)


def on_vmem(kernel, out_shape, scratch, name, limit, *args):
    vmem = pl.BlockSpec(memory_space=pltpu.VMEM)
    return pl.pallas_call(
        kernel,
        out_shape=out_shape,
        in_specs=[vmem] * len(args),
        out_specs=tuple([vmem] * len(out_shape)),
        scratch_shapes=scratch,
        compiler_params=pltpu.CompilerParams(vmem_limit_bytes=limit * MIB),
        name=name,
    )(*args)


def edge_y(x_even, x_odd):
    face = jax.ShapeDtypeStruct((14, 8, 128), F32)
    return on_vmem(edge_y_kernel, (face, face), [], "edge_y", 10, x_even, x_odd)


def edge_z(*args):
    grown = [jax.ShapeDtypeStruct((PAIRS, 48 + 2 * PAD[n], 128), F32) for n in range(7)]
    face = jax.ShapeDtypeStruct((12 + HALF, 8, 128), F32)
    return on_vmem(edge_z_kernel, (*grown, face), [], "edge_z", 16, *args)


def sweeps(grown, *faces):
    block = jax.ShapeDtypeStruct((BOX, BOX, 128), F32)
    padded = pltpu.VMEM((PAIRS, 64, 128), F32)
    scratch = [padded] * 6 + [
        pltpu.VMEM((4, PAIRS, 48, 128), F32),
        pltpu.VMEM((2, 2, 7, PAIRS - 2, 48, 128), F32),
        pltpu.VMEM((2, PAIRS - 2, 48, 128), F32),
    ]
    return on_vmem(sweep_kernel, (block, block), scratch, "sweeps", 40, *grown, *faces)


def exchange(axis, count, even, odd):
    pairs = []
    for start in (0, 1):
        step = []
        for i in range(start, count, 2):
            j = (i + 1) % count
            step += [(i, j), (j, i)]
        pairs.append(step)
    return lax.ppermute(even, axis, pairs[0]), lax.ppermute(odd, axis, pairs[1])


def per_device(solution_old, right_side, acoef, bcoef, corners):
    fields = (solution_old, right_side, acoef, bcoef)
    plan, *pays = plan_and_pack(corners, fields)
    gots = [swap_round(plan[k], pays[k]) for k in range(ROUNDS)]
    home, even, odd, near_even, near_odd, face = assemble(plan, fields, gots)
    x = exchange("gx", N_GX, even, odd)
    y = exchange("gy", N_GY, near_even, near_odd)
    z = exchange("gz", N_GZ, face, face)
    y_edges = exchange("gy", N_GY, *edge_y(*x))
    *grown, edge = edge_z(home, *x, *y, *y_edges)
    return sweeps(grown, *z, *exchange("gz", N_GZ, edge, edge))


def solution(mesh):
    boxes = P(("gx", "gy", "gz"), None, None)
    block = P("gx", "gy", "gz")
    return jax.shard_map(
        per_device,
        mesh=mesh,
        in_specs=(boxes, boxes, boxes, boxes, P()),
        out_specs=(block, block),
        check_vma=False,
    )
```

```python
import functools
import itertools

import jax
import jax.numpy as jnp
from jax import lax
from jax.experimental import pallas as pl
from jax.experimental.pallas import tpu as pltpu
from jax.sharding import PartitionSpec as P

BOX = 32
N_GX, N_GY, N_GZ = 4, 8, 8
PER_DEV = 4
ROUNDS = 3
HALF = BOX // 2
SIDE = 3
PAIRS = HALF + 2 * SIDE
SWEEPS = 2
F32 = jnp.float32
MIB = 1024 * 1024


def _colourings():
    table = {}
    for p1, p2 in itertools.combinations(range(1, 7), 2):
        codes = set()
        for cyc in itertools.product(range(3), repeat=7):
            if any(cyc[p] == cyc[p - 1] for p in range(7)):
                continue
            if [3 - cyc[p] - cyc[p - 1] for p in (0, p1, p2)] == [0, 1, 2]:
                codes.add(sum(c << (2 * i) for i, c in enumerate(list(cyc) + [0, 1, 2])))
        codes = sorted(codes)
        table[p1 * 7 + p2] = [codes[i % len(codes)] for i in range(CHOICES)]
    return table


CHOICES = 4
COLOURINGS = _colourings()
ORDERS = [sum(c << (2 * i) for i, c in enumerate(o)) for o in itertools.permutations(range(3))]


def _pick(flag, yes, no):
    return jnp.where(flag, jnp.int32(yes) if isinstance(yes, int) else yes, jnp.int32(no) if isinstance(no, int) else no)


def _chain(index, values):
    out = values[-1]
    for i in reversed(range(len(values) - 1)):
        out = jnp.where(index == i, values[i], out)
    return out


def _colour(code, edge):
    return lax.shift_right_logical(code, 2 * edge) & 3


def plan_kernel(
    table, f0, f1, f2, f3, go0, go1, go2, plan, pay0, pay1, pay2, corners, own, succ, swap, spot, ubox, rows8, sems, sem
):
    whole = pltpu.make_async_copy(table, corners, sem)
    whole.start()
    whole.wait()
    gx, me, gz = lax.axis_index("gx"), lax.axis_index("gy"), lax.axis_index("gz")
    stride = N_GZ * PER_DEV
    bases = [gx * (N_GY * stride) + ((gz & 6) + c) * PER_DEV for c in range(2)]

    groups = []
    for c, base in enumerate(bases):
        hot = jnp.int32(0)
        rows = []
        for g in range(N_GY):
            row = [lax.shift_right_logical(corners[1, base + g * stride + s], 5) for s in range(PER_DEV)]
            rows.append(row)
            leaving = sum(_pick(o != g, 1, 0) for o in row)
            hot = hot + _pick(leaving == 3, g, 0)
            for s in range(PER_DEV):
                own[c * 32 + g * PER_DEV + s] = row[s]
        first = jnp.int32(0)
        for g in reversed(range(N_GY)):
            to_hot = jnp.int32(0)
            nxt = jnp.int32(0)
            for o in rows[g]:
                to_hot = to_hot + _pick(o == hot, 1, 0)
                nxt = nxt + _pick((o != g) & (o != hot), o, 0)
            is_swap = _pick(hot == g, 0, to_hot)
            succ[c * 8 + g] = nxt
            swap[c * 8 + g] = is_swap
            first = _pick(is_swap == 1, g, first)
        v = first
        p1 = jnp.int32(0)
        p2 = jnp.int32(0)
        mine = jnp.int32(-1)
        pred = jnp.int32(0)
        cycle = []
        for p in range(7):
            spot[c * 8 + p] = v
            cycle.append(v)
            if p:
                sw = swap[c * 8 + v] == 1
                p2 = _pick(sw & (p1 != 0), p, p2)
                p1 = _pick(sw & (p1 == 0), p, p1)
            mine = _pick(v == me, p, mine)
            nxt = succ[c * 8 + v]
            pred = _pick(nxt == me, v, pred)
            v = nxt
        key = p1 * 7 + p2
        codes = [jnp.int32(0)] * CHOICES
        for k, options in COLOURINGS.items():
            codes = [_pick(key == k, o, code) for o, code in zip(options, codes)]
        swaps = [cycle[0], spot[c * 8 + p1], spot[c * 8 + p2]]
        groups.append((hot, cycle, swaps, codes, mine, pred, p1))

    link, lane = iota(0), iota(1)
    order = _chain(lane & 7, ORDERS + ORDERS[:2])
    load = [jnp.zeros((8, 128), jnp.int32) for _ in range(2)]
    for c in range(2):
        hot, cycle, swaps, codes = groups[c][:4]
        code = _chain(lax.shift_right_logical(lane, 5 - 2 * c) & 3, codes)
        for e in range(10):
            colour = _colour(code, e)
            if c:
                colour = lax.shift_right_logical(order, 2 * colour) & 3
            unit = lax.shift_left(jnp.ones((8, 128), jnp.int32), 8 * colour)
            flows = [(cycle[e], cycle[(e + 1) % 7])] if e < 7 else [(hot, swaps[e - 7]), (swaps[e - 7], hot)]
            for i, j in flows:
                d = (j - i) & 7
                ahead = _pick(d <= 4, d, 0)
                back = _pick(d <= 4, 0, 8 - d)
                load[0] = load[0] + jnp.where(((link - i) & 7) < ahead, unit, 0)
                load[1] = load[1] + jnp.where(((i - link) & 7) < back, unit, 0)
    cost = jnp.zeros((8, 128), F32)
    for r in range(ROUNDS):
        busiest = jnp.maximum(*[(lax.shift_right_logical(v, 8 * r) & 255).astype(F32) for v in load])
        for shift in (4, 2, 1):
            busiest = jnp.maximum(busiest, sroll(busiest, shift))
        cost = cost + busiest
    best = jnp.min(cost * 128.0 + lane.astype(F32)).astype(jnp.int32) & 127

    mine_second = (gz & 1) == 1

    def of_mine(values):
        return jnp.where(mine_second, values[1], values[0])

    code_a = _chain(lax.shift_right_logical(best, 5) & 3, groups[0][3])
    code_b = _chain(lax.shift_right_logical(best, 3) & 3, groups[1][3])
    order = jnp.where(mine_second, _chain(best & 7, [jnp.int32(o) for o in ORDERS + ORDERS[:2]]), ORDERS[0])
    code = of_mine((code_a, code_b))

    def round_of(edge):
        return lax.shift_right_logical(order, 2 * _colour(code, edge)) & 3

    hot = of_mine([g[0] for g in groups])
    spots = [of_mine([g[2][i] for g in groups]) for i in range(3)]
    mine, pred, p1 = [of_mine([g[i] for g in groups]) for i in (4, 5, 6)]
    c8, c32 = (gz & 1) * 8, (gz & 1) * 32
    base = of_mine(bases)

    def inner(g, s):
        return lax.shift_right_logical(corners[2, base + g * stride + s], 5) & 3

    star = [round_of(7 + i) for i in range(3)]
    is_hot = me == hot
    at = jnp.maximum(mine, 0)
    out_round = round_of(at)
    in_round = round_of(_pick(at == 0, 6, at - 1))
    my_succ = succ[c8 + me]
    swaps_here = jnp.logical_not(is_hot) & (swap[c8 + me] == 1)
    swap_at = _pick(swaps_here, _pick(at == 0, star[0], _pick(at == p1, star[1], star[2])), -1)
    places, arrives, slots = [], [], []
    for k in range(ROUNDS):
        hot_partner = sum(_pick(star[i] == k, spots[i], 0) for i in range(3))
        kind = _pick(swap_at == k, 3, _pick(out_round == k, 1, _pick(in_round == k, 2, 0)))
        partner = _pick(swap_at == k, hot, _pick(out_round == k, my_succ, pred))
        kind = _pick(is_hot, 3, kind)
        partner = _pick(is_hot, hot_partner, partner)
        way = me ^ partner
        up = ((kind == 1) & (me < partner)) | ((kind == 2) & (partner < me))
        (go0, go1, go2)[k][0] = _pick(kind == 0, 0, _pick(kind == 3, way, _pick(up, 7 + way, 14 + way)))
        slot = jnp.int32(0)
        place = jnp.int32(0)
        for s in range(PER_DEV):
            slot = slot + _pick(own[c32 + me * PER_DEV + s] == partner, s, 0)
            place = place + _pick(own[c32 + partner * PER_DEV + s] == me, inner(partner, s), 0)
        slots.append(jnp.minimum(slot, PER_DEV - 1))
        places.append(place)
        arrives.append((kind == 2) | (kind == 3))
    pays = (pay0, pay1, pay2)
    u_copies = [pltpu.make_async_copy(f0.at[slots[k]], ubox.at[k], sems.at[k, 3]) for k in range(ROUNDS)]
    copies = [
        pltpu.make_async_copy(field.at[slots[k]], pays[k].at[pl.ds(f * BOX, BOX)], sems.at[k, f])
        for k in range(ROUNDS)
        for f, field in enumerate((f1, f2, f3))
    ]
    for copy in u_copies + copies:
        copy.start()
    for q in range(PER_DEV):
        source = jnp.int32(0)
        for s in range(PER_DEV):
            source = source + _pick((own[c32 + me * PER_DEV + s] == me) & (inner(me, s) == q), s, 0)
        for k in range(ROUNDS):
            source = source + _pick(arrives[k] & (places[k] == q), 4 + k, 0)
        plan[q] = source
    for k in range(ROUNDS):
        u_copies[k].wait()
        halve(ubox.at[k], rows8.at[k], pays[k].at[pl.ds(3 * BOX, HALF)])
    for copy in copies:
        copy.wait()


def halve(box, tmp, out):
    lane = iota(1)
    is_odd = ((lax.shift_right_logical(lane, 5) + lane) & 1) == 1
    for j in range(8):
        tmp[j] = box[:, j * 128 : j * 128 + 128]
    for h in range(2):
        for j in range(8):
            lower = tmp[j, pl.ds(16 * h, 8, stride=2), :]
            upper = tmp[j, pl.ds(16 * h + 1, 8, stride=2), :]
            out[8 * h : 8 * h + 8, j * 128 : j * 128 + 128] = jnp.where(is_odd, lower, upper)


def plan_and_pack(corners, fields):
    hbm = pl.BlockSpec(memory_space=pltpu.HBM)
    smem = pl.BlockSpec(memory_space=pltpu.SMEM)
    vmem = pl.BlockSpec(memory_space=pltpu.VMEM)
    pay = jax.ShapeDtypeStruct((3 * BOX + HALF, BOX * BOX), F32)
    return pl.pallas_call(
        plan_kernel,
        out_shape=(*[jax.ShapeDtypeStruct((1,), jnp.int32)] * 3, jax.ShapeDtypeStruct((PER_DEV,), jnp.int32), pay, pay, pay),
        in_specs=[hbm] * 5,
        out_specs=(smem, smem, smem, smem, vmem, vmem, vmem),
        scratch_shapes=[
            pltpu.SMEM(corners.shape, jnp.int32),
            pltpu.SMEM((64,), jnp.int32),
            pltpu.SMEM((16,), jnp.int32),
            pltpu.SMEM((16,), jnp.int32),
            pltpu.SMEM((16,), jnp.int32),
            pltpu.VMEM((ROUNDS, BOX, BOX * BOX), F32),
            pltpu.VMEM((ROUNDS, 8, BOX, 128), F32),
            pltpu.SemaphoreType.DMA((ROUNDS, 4)),
            pltpu.SemaphoreType.DMA,
        ],
        compiler_params=pltpu.CompilerParams(vmem_limit_bytes=60 * MIB),
        name="plan",
    )(corners, *fields)


def swap_round(branch, pay):
    def stay(x):
        return x

    def move(pairs, x):
        return lax.ppermute(x, "gy", pairs)

    branches = [stay]
    for r in range(1, 8):
        branches.append(functools.partial(move, [(i, i ^ r) for i in range(8)]))
    for r in range(1, 8):
        branches.append(functools.partial(move, [(i, i ^ r) for i in range(8) if i < i ^ r]))
    for r in range(1, 8):
        branches.append(functools.partial(move, [(i, i ^ r) for i in range(8) if i > i ^ r]))
    return lax.switch(branch, branches, pay)


def iota(dim):
    return lax.broadcasted_iota(jnp.int32, (8, 128), dim)


def lroll(v, shift):
    shift %= 128
    return pltpu.roll(v, shift, 1) if shift else v


def sroll(v, shift):
    shift %= 8
    return pltpu.roll(v, shift, 0) if shift else v


U1, B1, B0, F0, A0, F1, A1 = range(7)
WIDTH = (5, 5, 4, 4, 4, 3, 3)
LAYERS = [(U1, 0), (U1, 1), (U1, 2), (B1, 1), (B1, 2)]
LAYERS += [(n, i) for n in (B0, F0, A0) for i in range(2)] + [(F1, 0), (F1, 1), (A1, 1)]
SHARED = {U1: B1, F1: A1}


def odd_cell():
    return ((iota(0) + iota(1)) & 1) == 1


def face_rows(first, second):
    sub = iota(0)
    out = []
    for near, far in (first, second):
        out.append((jnp.where(sub < 5, near[U1], sroll(near[F1], 5)), jnp.where(sub < 5, sroll(far[U1], -3), far[F1])))
        out.append((jnp.where(sub < 5, near[B1], sroll(near[A1], 5)), jnp.where(sub < 5, sroll(far[B1], -3), far[A1])))
        out.append((jnp.where(sub < 4, near[B0], sroll(near[F0], 4)), jnp.where(sub < 4, sroll(far[B0], 4), far[F0])))
    (n0, f0), (n1, f1) = first, second
    lo = jnp.where(sub < 4, n0[A0], sroll(n1[A0], 4))
    hi = jnp.where(sub < 4, sroll(f0[A0], 4), f1[A0])
    return out + [(lo, hi)]


def face_lanes(first, second):
    lane = iota(1)
    place = lane & 63
    both = []
    for w, tiles in enumerate((first, second)):
        at = 0
        ends = []
        for n in range(7):
            ends.append((lroll(tiles[n], 64 * w + at + WIDTH[n]), at + 2 * WIDTH[n]))
            at += 2 * WIDTH[n]
        group = ends[-1][0]
        for tile, end in reversed(ends[:-1]):
            group = jnp.where(place < end, tile, group)
        both.append(group)
    return jnp.where(lane < 64, both[0], both[1])


def assemble_kernel(
    plan, f0, f1, f2, f3, r0, r1, r2, home, even, odd, y_even, y_odd, z_face, ubox, uhalf, rows8, raw, tmp, sems
):
    fields = (f1, f2, f3)
    gots = (r0, r1, r2)
    rows = pl.ds(3 * BOX, HALF)
    for q in range(PER_DEV):
        source = plan[q]

        @pl.when(source < 4)
        def _():
            box = jnp.minimum(source, 3)
            pltpu.make_async_copy(f0.at[box], ubox.at[q], sems.at[3, q]).start()
            for f in range(3):
                pltpu.make_async_copy(fields[f].at[box], raw.at[f, q], sems.at[f, q]).start()

        for k in range(ROUNDS):

            @pl.when(source == 4 + k)
            def _():
                pltpu.make_async_copy(gots[k].at[rows], uhalf.at[q], sems.at[3, q]).start()
                for f in range(3):
                    pltpu.make_async_copy(gots[k].at[pl.ds(f * BOX, BOX)], raw.at[f, q], sems.at[f, q]).start()

    lane = iota(1)
    m64 = (lane & 64) != 0
    m32 = (lane & 32) != 0
    is_odd = odd_cell()

    def relayout(load):
        for t in range(4):
            for jj in range(2):
                j = 2 * t + jj
                a = [load(k, slice(j * 128, (j + 1) * 128)) for k in range(4)]
                n02 = lroll(jnp.where(m64, a[0], a[2]), 64)
                n13 = lroll(jnp.where(m64, a[1], a[3]), 64)
                n0, n2 = jnp.where(m64, n02, a[0]), jnp.where(m64, a[2], n02)
                n1, n3 = jnp.where(m64, n13, a[1]), jnp.where(m64, a[3], n13)
                b = [
                    jnp.where(m32, lroll(n1, 32), n0),
                    jnp.where(m32, n1, lroll(n0, 96)),
                    jnp.where(m32, lroll(n3, 32), n2),
                    jnp.where(m32, n3, lroll(n2, 96)),
                ]
                for q in range(4):
                    y = jj * 4 + q
                    tmp[t, y * 8 : y * 8 + 8, :] = b[q]

    for f in range(3):
        for q in range(PER_DEV):
            pltpu.make_async_copy(f0.at[0], raw.at[f, q], sems.at[f, q]).wait()

        def step(i, carry):
            xt = pl.multiple_of(i * 8, 8)
            relayout(lambda k, lanes: raw[f, k, pl.ds(xt, 8), lanes])
            for t in range(4):
                ys = slice(t * 8, t * 8 + 8)
                for x in range(0, 8, 2):
                    lower = tmp[t, pl.ds(x, 8, stride=8), :]
                    upper = tmp[t, pl.ds(x + 1, 8, stride=8), :]
                    j = i * 4 + x // 2
                    home[(F1, A1, B1)[f], j, ys, :] = jnp.where(is_odd, lower, upper)
                    home[(F0, A0, B0)[f], j, ys, :] = jnp.where(is_odd, upper, lower)
            return carry

        lax.fori_loop(0, 4, step, 0, unroll=2)

    for q in range(PER_DEV):
        mine = plan[q] < 4

        @pl.when(mine)
        def _():
            pltpu.make_async_copy(f0.at[0], ubox.at[q], sems.at[3, q]).wait()
            halve(ubox.at[q], rows8.at[q], uhalf.at[q])

        @pl.when(jnp.logical_not(mine))
        def _():
            pltpu.make_async_copy(r0.at[rows], uhalf.at[q], sems.at[3, q]).wait()

    for i in range(2):
        relayout(lambda k, lanes: uhalf[k, 8 * i : 8 * i + 8, lanes])
        for t in range(4):
            for x in range(8):
                home[U1, i * 8 + x, t * 8 : t * 8 + 8, :] = tmp[t, pl.ds(x, 8, stride=8), :]

    low = (lax.axis_index("gx") & 1) == 1
    for k, (n, i) in enumerate(LAYERS):
        count = 3 if n < 2 else 2
        low_side, high_side = count - 1 - i, HALF - count + i
        for t in range(4):
            ys = slice(t * 8, t * 8 + 8)
            lo, hi = home[n, low_side, ys, :], home[n, high_side, ys, :]
            if i == 0 and n in SHARED:
                lo = jnp.where(is_odd, lo, lroll(home[SHARED[n], low_side, ys, :], 1))
                hi = jnp.where(is_odd, lroll(home[SHARED[n], high_side, ys, :], 1), hi)
            even[k, ys, :] = jnp.where(low, lo, hi)
            odd[k, ys, :] = jnp.where(low, hi, lo)

    low_y = (lax.axis_index("gy") & 1) == 1

    def faces(m, carry):
        tiles = [[[home[n, 2 * m + i, 8 * t : 8 * t + 8, :] for n in range(7)] for t in range(4)] for i in range(2)]
        for w, (lo, hi) in enumerate(face_rows(*[(tiles[i][0], tiles[i][3]) for i in range(2)])):
            y_even[7 * m + w] = jnp.where(low_y, lo, hi)
            y_odd[7 * m + w] = jnp.where(low_y, hi, lo)
        for i in range(2):
            for v in range(2):
                z_face[2 * m + i, v] = face_lanes(tiles[i][2 * v], tiles[i][2 * v + 1])
        return carry

    lax.fori_loop(0, HALF // 2, faces, 0)


def assemble(plan, fields, gots):
    any_spec = pl.BlockSpec(memory_space=pl.ANY)
    hbm = pl.BlockSpec(memory_space=pltpu.HBM)
    vmem = pl.BlockSpec(memory_space=pltpu.VMEM)
    face = jax.ShapeDtypeStruct((len(LAYERS), BOX, 128), F32)
    rows = jax.ShapeDtypeStruct((7 * HALF // 2, 8, 128), F32)
    return pl.pallas_call(
        assemble_kernel,
        out_shape=(
            jax.ShapeDtypeStruct((7, HALF, BOX, 128), F32),
            face,
            face,
            rows,
            rows,
            jax.ShapeDtypeStruct((HALF, 2, 8, 128), F32),
        ),
        in_specs=[pl.BlockSpec(memory_space=pltpu.SMEM)] + [hbm] * 4 + [any_spec] * 3,
        out_specs=(vmem,) * 6,
        scratch_shapes=[
            pltpu.VMEM((PER_DEV, BOX, BOX * BOX), F32),
            pltpu.VMEM((PER_DEV, HALF, BOX * BOX), F32),
            pltpu.VMEM((PER_DEV, 8, BOX, 128), F32),
            pltpu.VMEM((3, PER_DEV, BOX, BOX * BOX), F32),
            pltpu.VMEM((4, 64, 128), F32),
            pltpu.SemaphoreType.DMA((4, PER_DEV)),
        ],
        compiler_params=pltpu.CompilerParams(vmem_limit_bytes=12 * MIB),
        name="assemble",
    )(plan, *fields, *gots)


def halo_of(axis, count, even, odd):
    i = lax.axis_index(axis)
    low_first = (i & 1) == 1
    low = jnp.where(i > 0, jnp.where(low_first, even, odd), 0.0)
    high = jnp.where(i < count - 1, jnp.where(low_first, odd, even), 0.0)
    return low, high


def x_halo_tiles(even, odd, t):
    ys = slice(t * 8, t * 8 + 8)
    pairs = {}
    for k, (n, i) in enumerate(LAYERS):
        low, high = halo_of("gx", N_GX, even[k, ys, :], odd[k, ys, :])
        count = 3 if n < 2 else 2
        spots = (SIDE - count + i, SIDE + HALF + count - 1 - i)
        for spot, tile in zip(spots, (low, high)):
            pairs.setdefault(spot, {})[n] = tile
            if i == 0 and n in SHARED:
                pairs[spot][SHARED[n]] = lroll(tile, -1)
    return pairs


EDGES = (1, 2, SIDE + HALF, SIDE + HALF + 1)


def edge_y_kernel(x_even, x_odd, even, odd):
    low = (lax.axis_index("gy") & 1) == 1
    near, far = x_halo_tiles(x_even, x_odd, 0), x_halo_tiles(x_even, x_odd, 3)
    for m in range(2):
        for w, (lo, hi) in enumerate(face_rows(*[(near[k], far[k]) for k in EDGES[2 * m : 2 * m + 2]])):
            even[7 * m + w] = jnp.where(low, lo, hi)
            odd[7 * m + w] = jnp.where(low, hi, lo)


PAD = (8, 8, 8, 0, 0, 0, 0)


def edge_z_kernel(home, x_even, x_odd, y_even, y_odd, e_even, e_odd, u1, b1, b0, f0, a0, f1, a1, edge):
    outs = (u1, b1, b0, f0, a0, f1, a1)

    def halo(even, odd, m, pairs):
        low_high = [halo_of("gy", N_GY, even[7 * m + w], odd[7 * m + w]) for w in range(7)]
        l3, h3 = low_high[6]
        for i, k in enumerate(pairs):
            (l0, h0), (l1, h1), (l2, h2) = low_high[3 * i : 3 * i + 3]
            lows = (sroll(l0, 3), sroll(l1, 3), sroll(l2, 4), l2, sroll(l3, 4) if i == 0 else l3, l0, l1)
            highs = (h0, h1, h2, sroll(h2, 4), h3 if i == 0 else sroll(h3, 4), sroll(h0, 3), sroll(h1, 3))
            for n in range(7):
                outs[n][k, PAD[n] : PAD[n] + 8, :] = lows[n]
                outs[n][k, PAD[n] + 40 : PAD[n] + 48, :] = highs[n]

    def tiles(k, t):
        return [outs[n][k, PAD[n] + t * 8 : PAD[n] + t * 8 + 8, :] for n in range(7)]

    def copy(m, carry):
        for i in range(2):
            for n in range(7):
                outs[n][2 * m + i + SIDE, PAD[n] + 8 : PAD[n] + 40, :] = home[n, 2 * m + i]
        halo(y_even, y_odd, m, (2 * m + SIDE, 2 * m + SIDE + 1))
        for i in range(2):
            k = 2 * m + i + SIDE
            edge[12 + 2 * m + i] = face_lanes(tiles(k, 0), tiles(k, 5))
        return carry

    lax.fori_loop(0, HALF // 2, copy, 0)
    for t in range(4):
        for k, fields in x_halo_tiles(x_even, x_odd, t).items():
            for n, tile in fields.items():
                outs[n][k, PAD[n] + 8 + t * 8 : PAD[n] + 16 + t * 8, :] = tile
    for m in range(2):
        halo(e_even, e_odd, m, EDGES[2 * m : 2 * m + 2])
    for i, k in enumerate(EDGES):
        for v in range(3):
            edge[3 * i + v] = face_lanes(tiles(k, 2 * v), tiles(k, 2 * v + 1))


def sweep_kernel(
    u1, b1, b0, f0, a0, f1, a1, z_even, z_odd, e_even, e_odd, sol, res, um0, um1, ua0, ua1, ba0, ba1, fax, co, dg
):
    lane = iota(1)
    first, last = lane == 0, lane == 127
    place = lane & 63
    is_odd = odd_cell()
    u = ((um0, ua0), (um1, ua1))
    b = ((b0, ba0), (b1, ba1))
    fa = (((f0, a0), (fax.at[0], fax.at[1])), ((f1, a1), (fax.at[2], fax.at[3])))
    starts = [2 * sum(WIDTH[:n]) for n in range(7)]
    high_part = functools.reduce(
        jnp.logical_or, [(place >= starts[n]) & (place < starts[n] + WIDTH[n]) for n in range(7)]
    )
    aux = (ua1, ba1, ba0, fax.at[0], fax.at[1], fax.at[2], fax.at[3])

    def unpack(k, even, odd, spots):
        low, high = halo_of("gz", N_GZ, even, odd)
        both = jnp.where(high_part, low, high)
        for w, t in enumerate(spots):
            for n in range(7):
                aux[n][k, PAD[n] + t * 8 : PAD[n] + t * 8 + 8, :] = lroll(both, -(64 * w + starts[n] + WIDTH[n]))

    def unpack_pair(j, carry):
        for v in range(2):
            unpack(j + SIDE, z_even[j, v], z_odd[j, v], (1 + 2 * v, 2 + 2 * v))
        unpack(j + SIDE, e_even[12 + j], e_odd[12 + j], (0, 5))
        return carry

    um1[...] = u1[...]
    lax.fori_loop(0, HALF, unpack_pair, 0, unroll=2)
    for i, k in enumerate(EDGES):
        for v in range(3):
            unpack(k, e_even[3 * i + v], e_odd[3 * i + v], (2 * v, 2 * v + 1))

    def around(c, field, k, t, spans):
        r = 8 + t * 8
        main, side = field[1 - c]
        m, a = main[k, r : r + 8, :], side[k, r : r + 8, :]
        m1, a1 = lroll(m, 1), lroll(a, 1)
        m2, a2 = lroll(m, 127), lroll(a, 127)
        below = (jnp.where(first, a1, m1), jnp.where(first, m1, a1))
        above = (jnp.where(last, a2, m2), jnp.where(last, m2, a2))
        out = []
        for s in spans:
            ref = (main, side)[s]
            back, ahead = ref[k - 1, r : r + 8, :], ref[k + 1, r : r + 8, :]
            beside = jnp.where(is_odd, back, ahead) if c else jnp.where(is_odd, ahead, back)
            out.append(((m, a)[s], beside, ref[k, r - 1 : r + 7, :], ref[k, r + 1 : r + 9, :], below[s], above[s]))
        return out

    def coefs(k, carry):
        for c in range(2):
            for t in range(6):
                rows = slice(t * 8, 8 + t * 8)
                near = around(c, b, k, t, (0, 1))
                for s in range(2):
                    mid = b[c][s][k, 8 + t * 8 : 16 + t * 8, :]
                    f, a = [ref[k, rows, :] for ref in fa[c][s]]
                    faces = [0.5 * (mid + v) for v in near[s]]
                    diag = a + (faces[0] + faces[1]) + (faces[2] + faces[3]) + (faces[4] + faces[5])
                    inverse = jnp.where(mid > 0, 1.0 / diag, 0.0)
                    for n in range(6):
                        co[c, s, n, k - 1, rows, :] = faces[n] * inverse
                    co[c, s, 6, k - 1, rows, :] = f * inverse
                    if s == 0:
                        dg[c, k - 1, rows, :] = diag
        return carry

    lax.fori_loop(1, PAIRS - 1, coefs, 0, unroll=2)

    def update(c, k, t, spans):
        rows = slice(t * 8, 8 + t * 8)
        new = []
        for s, v in zip(spans, around(c, u, k, t, spans)):
            w = [co[c, s, n, k - 1, rows, :] for n in range(7)]
            x = w[0] * v[0] + w[1] * v[1]
            y = w[2] * v[2] + w[3] * v[3]
            z = w[4] * v[4] + w[5] * v[5]
            new.append(w[6] + ((x + y) + z))
        return new

    for half in range(2 * SWEEPS):
        c = half % 2

        def sweep(k, carry):
            for t in range(6):
                for s, new in enumerate(update(c, k, t, (0, 1))):
                    u[c][s][k, 8 + t * 8 : 16 + t * 8, :] = new
            return carry

        out = half // 2
        lax.fori_loop(1 + out, PAIRS - 1 - out, sweep, 0, unroll=2)

    def finish(j, carry):
        k = j + SIDE
        for t in range(1, 5):
            ys = slice(t * 8 - 8, t * 8)
            rows = slice(t * 8, t * 8 + 8)
            now = [u[c][0][k, 8 + t * 8 : 16 + t * 8, :] for c in range(2)]
            rest = [dg[c, k - 1, rows, :] * (update(c, k, t, (0,))[0] - now[c]) for c in range(2)]
            for ref, (v0, v1) in ((sol, now), (res, rest)):
                ref[2 * j, ys, :] = jnp.where(is_odd, v1, v0)
                ref[2 * j + 1, ys, :] = jnp.where(is_odd, v0, v1)
        return carry

    lax.fori_loop(0, HALF, finish, 0, unroll=2)


def on_vmem(kernel, out_shape, scratch, name, limit, *args):
    vmem = pl.BlockSpec(memory_space=pltpu.VMEM)
    return pl.pallas_call(
        kernel,
        out_shape=out_shape,
        in_specs=[vmem] * len(args),
        out_specs=tuple([vmem] * len(out_shape)),
        scratch_shapes=scratch,
        compiler_params=pltpu.CompilerParams(vmem_limit_bytes=limit * MIB),
        name=name,
    )(*args)


def edge_y(x_even, x_odd):
    face = jax.ShapeDtypeStruct((14, 8, 128), F32)
    return on_vmem(edge_y_kernel, (face, face), [], "edge_y", 10, x_even, x_odd)


def edge_z(*args):
    grown = [jax.ShapeDtypeStruct((PAIRS, 48 + 2 * PAD[n], 128), F32) for n in range(7)]
    face = jax.ShapeDtypeStruct((12 + HALF, 8, 128), F32)
    return on_vmem(edge_z_kernel, (*grown, face), [], "edge_z", 16, *args)


def sweeps(grown, *faces):
    block = jax.ShapeDtypeStruct((BOX, BOX, 128), F32)
    padded = pltpu.VMEM((PAIRS, 64, 128), F32)
    scratch = [padded] * 6 + [
        pltpu.VMEM((4, PAIRS, 48, 128), F32),
        pltpu.VMEM((2, 2, 7, PAIRS - 2, 48, 128), F32),
        pltpu.VMEM((2, PAIRS - 2, 48, 128), F32),
    ]
    return on_vmem(sweep_kernel, (block, block), scratch, "sweeps", 40, *grown, *faces)


def exchange(axis, count, even, odd):
    pairs = []
    for start in (0, 1):
        step = []
        for i in range(start, count, 2):
            j = (i + 1) % count
            step += [(i, j), (j, i)]
        pairs.append(step)
    return lax.ppermute(even, axis, pairs[0]), lax.ppermute(odd, axis, pairs[1])


def per_device(solution_old, right_side, acoef, bcoef, corners):
    fields = (solution_old, right_side, acoef, bcoef)
    go0, go1, go2, plan, *pays = plan_and_pack(corners, fields)
    gots = [swap_round(go.reshape(()), pay) for go, pay in zip((go0, go1, go2), pays)]
    home, even, odd, near_even, near_odd, face = assemble(plan, fields, gots)
    x = exchange("gx", N_GX, even, odd)
    y = exchange("gy", N_GY, near_even, near_odd)
    z = exchange("gz", N_GZ, face, face)
    y_edges = exchange("gy", N_GY, *edge_y(*x))
    *grown, edge = edge_z(home, *x, *y, *y_edges)
    return sweeps(grown, *z, *exchange("gz", N_GZ, edge, edge))


def solution(mesh):
    boxes = P(("gx", "gy", "gz"), None, None)
    block = P("gx", "gy", "gz")
    return jax.shard_map(
        per_device,
        mesh=mesh,
        in_specs=(boxes, boxes, boxes, boxes, P()),
        out_specs=(block, block),
        check_vma=False,
    )
```

```python
import functools
import itertools

import jax
import jax.numpy as jnp
from jax import lax
from jax.experimental import pallas as pl
from jax.experimental.pallas import tpu as pltpu
from jax.sharding import PartitionSpec as P

BOX = 32
N_GX, N_GY, N_GZ = 4, 8, 8
PER_DEV = 4
ROUNDS = 3
HALF = BOX // 2
SIDE = 3
PAIRS = HALF + 2 * SIDE
SWEEPS = 2
F32 = jnp.float32
MIB = 1024 * 1024


def _colourings():
    table = {}
    for p1, p2 in itertools.combinations(range(1, 7), 2):
        codes = set()
        for cyc in itertools.product(range(3), repeat=7):
            if any(cyc[p] == cyc[p - 1] for p in range(7)):
                continue
            if [3 - cyc[p] - cyc[p - 1] for p in (0, p1, p2)] == [0, 1, 2]:
                codes.add(sum(c << (2 * i) for i, c in enumerate(list(cyc) + [0, 1, 2])))
        codes = sorted(codes)
        table[p1 * 7 + p2] = [codes[i % len(codes)] for i in range(CHOICES)]
    return table


CHOICES = 4
COLOURINGS = _colourings()
ORDERS = [sum(c << (2 * i) for i, c in enumerate(o)) for o in itertools.permutations(range(3))]


def _pick(flag, yes, no):
    return jnp.where(flag, jnp.int32(yes) if isinstance(yes, int) else yes, jnp.int32(no) if isinstance(no, int) else no)


def _chain(index, values):
    out = values[-1]
    for i in reversed(range(len(values) - 1)):
        out = jnp.where(index == i, values[i], out)
    return out


def _colour(code, edge):
    return lax.shift_right_logical(code, 2 * edge) & 3


def plan_kernel(
    table, f0, f1, f2, f3, go0, go1, go2, plan, pay0, pay1, pay2, corners, own, succ, swap, spot, boxes, rows8, sems, sem
):
    whole = pltpu.make_async_copy(table, corners, sem)
    whole.start()
    copies = [pltpu.make_async_copy(field, boxes.at[f], sems.at[f]) for f, field in enumerate((f1, f2, f3, f0))]
    for copy in copies:
        copy.start()
    whole.wait()
    gx, me, gz = lax.axis_index("gx"), lax.axis_index("gy"), lax.axis_index("gz")
    stride = N_GZ * PER_DEV
    bases = [gx * (N_GY * stride) + ((gz & 6) + c) * PER_DEV for c in range(2)]

    groups = []
    for c, base in enumerate(bases):
        hot = jnp.int32(0)
        rows = []
        for g in range(N_GY):
            row = [lax.shift_right_logical(corners[1, base + g * stride + s], 5) for s in range(PER_DEV)]
            rows.append(row)
            leaving = sum(_pick(o != g, 1, 0) for o in row)
            hot = hot + _pick(leaving == 3, g, 0)
            for s in range(PER_DEV):
                own[c * 32 + g * PER_DEV + s] = row[s]
        first = jnp.int32(0)
        for g in reversed(range(N_GY)):
            to_hot = jnp.int32(0)
            nxt = jnp.int32(0)
            for o in rows[g]:
                to_hot = to_hot + _pick(o == hot, 1, 0)
                nxt = nxt + _pick((o != g) & (o != hot), o, 0)
            is_swap = _pick(hot == g, 0, to_hot)
            succ[c * 8 + g] = nxt
            swap[c * 8 + g] = is_swap
            first = _pick(is_swap == 1, g, first)
        v = first
        p1 = jnp.int32(0)
        p2 = jnp.int32(0)
        mine = jnp.int32(-1)
        pred = jnp.int32(0)
        cycle = []
        for p in range(7):
            spot[c * 8 + p] = v
            cycle.append(v)
            if p:
                sw = swap[c * 8 + v] == 1
                p2 = _pick(sw & (p1 != 0), p, p2)
                p1 = _pick(sw & (p1 == 0), p, p1)
            mine = _pick(v == me, p, mine)
            nxt = succ[c * 8 + v]
            pred = _pick(nxt == me, v, pred)
            v = nxt
        key = p1 * 7 + p2
        codes = [jnp.int32(0)] * CHOICES
        for k, options in COLOURINGS.items():
            codes = [_pick(key == k, o, code) for o, code in zip(options, codes)]
        swaps = [cycle[0], spot[c * 8 + p1], spot[c * 8 + p2]]
        groups.append((hot, cycle, swaps, codes, mine, pred, p1))

    link, lane = iota(0), iota(1)
    order = _chain(lane & 7, ORDERS + ORDERS[:2])
    load = [jnp.zeros((8, 128), jnp.int32) for _ in range(2)]
    for c in range(2):
        hot, cycle, swaps, codes = groups[c][:4]
        code = _chain(lax.shift_right_logical(lane, 5 - 2 * c) & 3, codes)
        for e in range(10):
            colour = _colour(code, e)
            if c:
                colour = lax.shift_right_logical(order, 2 * colour) & 3
            unit = lax.shift_left(jnp.ones((8, 128), jnp.int32), 8 * colour)
            flows = [(cycle[e], cycle[(e + 1) % 7])] if e < 7 else [(hot, swaps[e - 7]), (swaps[e - 7], hot)]
            for i, j in flows:
                d = (j - i) & 7
                ahead = _pick(d <= 4, d, 0)
                back = _pick(d <= 4, 0, 8 - d)
                load[0] = load[0] + jnp.where(((link - i) & 7) < ahead, unit, 0)
                load[1] = load[1] + jnp.where(((i - link) & 7) < back, unit, 0)
    cost = jnp.zeros((8, 128), F32)
    for r in range(ROUNDS):
        busiest = jnp.maximum(*[(lax.shift_right_logical(v, 8 * r) & 255).astype(F32) for v in load])
        for shift in (4, 2, 1):
            busiest = jnp.maximum(busiest, sroll(busiest, shift))
        cost = cost + busiest
    best = jnp.min(cost * 128.0 + lane.astype(F32)).astype(jnp.int32) & 127

    mine_second = (gz & 1) == 1

    def of_mine(values):
        return jnp.where(mine_second, values[1], values[0])

    code_a = _chain(lax.shift_right_logical(best, 5) & 3, groups[0][3])
    code_b = _chain(lax.shift_right_logical(best, 3) & 3, groups[1][3])
    order = jnp.where(mine_second, _chain(best & 7, [jnp.int32(o) for o in ORDERS + ORDERS[:2]]), ORDERS[0])
    code = of_mine((code_a, code_b))

    def round_of(edge):
        return lax.shift_right_logical(order, 2 * _colour(code, edge)) & 3

    hot = of_mine([g[0] for g in groups])
    spots = [of_mine([g[2][i] for g in groups]) for i in range(3)]
    mine, pred, p1 = [of_mine([g[i] for g in groups]) for i in (4, 5, 6)]
    c8, c32 = (gz & 1) * 8, (gz & 1) * 32
    base = of_mine(bases)

    def inner(g, s):
        return lax.shift_right_logical(corners[2, base + g * stride + s], 5) & 3

    star = [round_of(7 + i) for i in range(3)]
    is_hot = me == hot
    at = jnp.maximum(mine, 0)
    out_round = round_of(at)
    in_round = round_of(_pick(at == 0, 6, at - 1))
    my_succ = succ[c8 + me]
    swaps_here = jnp.logical_not(is_hot) & (swap[c8 + me] == 1)
    swap_at = _pick(swaps_here, _pick(at == 0, star[0], _pick(at == p1, star[1], star[2])), -1)
    places, arrives, slots = [], [], []
    for k in range(ROUNDS):
        hot_partner = sum(_pick(star[i] == k, spots[i], 0) for i in range(3))
        kind = _pick(swap_at == k, 3, _pick(out_round == k, 1, _pick(in_round == k, 2, 0)))
        partner = _pick(swap_at == k, hot, _pick(out_round == k, my_succ, pred))
        kind = _pick(is_hot, 3, kind)
        partner = _pick(is_hot, hot_partner, partner)
        way = me ^ partner
        up = ((kind == 1) & (me < partner)) | ((kind == 2) & (partner < me))
        (go0, go1, go2)[k][0] = _pick(kind == 0, 0, _pick(kind == 3, way, _pick(up, 7 + way, 14 + way)))
        slot = jnp.int32(0)
        place = jnp.int32(0)
        for s in range(PER_DEV):
            slot = slot + _pick(own[c32 + me * PER_DEV + s] == partner, s, 0)
            place = place + _pick(own[c32 + partner * PER_DEV + s] == me, inner(partner, s), 0)
        slots.append(jnp.minimum(slot, PER_DEV - 1))
        places.append(place)
        arrives.append((kind == 2) | (kind == 3))
    pays = (pay0, pay1, pay2)
    for q in range(PER_DEV):
        source = jnp.int32(0)
        for s in range(PER_DEV):
            source = source + _pick((own[c32 + me * PER_DEV + s] == me) & (inner(me, s) == q), s, 0)
        for k in range(ROUNDS):
            source = source + _pick(arrives[k] & (places[k] == q), 4 + k, 0)
        plan[q] = source
    for copy in copies:
        copy.wait()
    for k in range(ROUNDS):
        for f in range(3):
            pays[k][f * BOX : (f + 1) * BOX, :] = boxes[f, slots[k]]
        halve(boxes.at[3, slots[k]], rows8.at[k], pays[k].at[pl.ds(3 * BOX, HALF)])


def halve(box, tmp, out):
    lane = iota(1)
    is_odd = ((lax.shift_right_logical(lane, 5) + lane) & 1) == 1
    for j in range(8):
        tmp[j] = box[:, j * 128 : j * 128 + 128]
    for h in range(2):
        for j in range(8):
            lower = tmp[j, pl.ds(16 * h, 8, stride=2), :]
            upper = tmp[j, pl.ds(16 * h + 1, 8, stride=2), :]
            out[8 * h : 8 * h + 8, j * 128 : j * 128 + 128] = jnp.where(is_odd, lower, upper)


def plan_and_pack(corners, fields):
    hbm = pl.BlockSpec(memory_space=pltpu.HBM)
    smem = pl.BlockSpec(memory_space=pltpu.SMEM)
    vmem = pl.BlockSpec(memory_space=pltpu.VMEM)
    pay = jax.ShapeDtypeStruct((3 * BOX + HALF, BOX * BOX), F32)
    return pl.pallas_call(
        plan_kernel,
        out_shape=(*[jax.ShapeDtypeStruct((1,), jnp.int32)] * 3, jax.ShapeDtypeStruct((PER_DEV,), jnp.int32), pay, pay, pay),
        in_specs=[hbm] * 5,
        out_specs=(smem, smem, smem, smem, vmem, vmem, vmem),
        scratch_shapes=[
            pltpu.SMEM(corners.shape, jnp.int32),
            pltpu.SMEM((64,), jnp.int32),
            pltpu.SMEM((16,), jnp.int32),
            pltpu.SMEM((16,), jnp.int32),
            pltpu.SMEM((16,), jnp.int32),
            pltpu.VMEM((4, PER_DEV, BOX, BOX * BOX), F32),
            pltpu.VMEM((ROUNDS, 8, BOX, 128), F32),
            pltpu.SemaphoreType.DMA((4,)),
            pltpu.SemaphoreType.DMA,
        ],
        compiler_params=pltpu.CompilerParams(vmem_limit_bytes=60 * MIB),
        name="plan",
    )(corners, *fields)


def swap_round(branch, pay):
    def stay(x):
        return x

    def move(pairs, x):
        return lax.ppermute(x, "gy", pairs)

    branches = [stay]
    for r in range(1, 8):
        branches.append(functools.partial(move, [(i, i ^ r) for i in range(8)]))
    for r in range(1, 8):
        branches.append(functools.partial(move, [(i, i ^ r) for i in range(8) if i < i ^ r]))
    for r in range(1, 8):
        branches.append(functools.partial(move, [(i, i ^ r) for i in range(8) if i > i ^ r]))
    return lax.switch(branch, branches, pay)


def iota(dim):
    return lax.broadcasted_iota(jnp.int32, (8, 128), dim)


def lroll(v, shift):
    shift %= 128
    return pltpu.roll(v, shift, 1) if shift else v


def sroll(v, shift):
    shift %= 8
    return pltpu.roll(v, shift, 0) if shift else v


U1, B1, B0, F0, A0, F1, A1 = range(7)
WIDTH = (5, 5, 4, 4, 4, 3, 3)
LAYERS = [(U1, 0), (U1, 1), (U1, 2), (B1, 1), (B1, 2)]
LAYERS += [(n, i) for n in (B0, F0, A0) for i in range(2)] + [(F1, 0), (F1, 1), (A1, 1)]
SHARED = {U1: B1, F1: A1}


def odd_cell():
    return ((iota(0) + iota(1)) & 1) == 1


def face_rows(first, second):
    sub = iota(0)
    out = []
    for near, far in (first, second):
        out.append((jnp.where(sub < 5, near[U1], sroll(near[F1], 5)), jnp.where(sub < 5, sroll(far[U1], -3), far[F1])))
        out.append((jnp.where(sub < 5, near[B1], sroll(near[A1], 5)), jnp.where(sub < 5, sroll(far[B1], -3), far[A1])))
        out.append((jnp.where(sub < 4, near[B0], sroll(near[F0], 4)), jnp.where(sub < 4, sroll(far[B0], 4), far[F0])))
    (n0, f0), (n1, f1) = first, second
    lo = jnp.where(sub < 4, n0[A0], sroll(n1[A0], 4))
    hi = jnp.where(sub < 4, sroll(f0[A0], 4), f1[A0])
    return out + [(lo, hi)]


def face_lanes(first, second):
    lane = iota(1)
    place = lane & 63
    both = []
    for w, tiles in enumerate((first, second)):
        at = 0
        ends = []
        for n in range(7):
            ends.append((lroll(tiles[n], 64 * w + at + WIDTH[n]), at + 2 * WIDTH[n]))
            at += 2 * WIDTH[n]
        group = ends[-1][0]
        for tile, end in reversed(ends[:-1]):
            group = jnp.where(place < end, tile, group)
        both.append(group)
    return jnp.where(lane < 64, both[0], both[1])


def assemble_kernel(
    plan, f0, f1, f2, f3, r0, r1, r2, home, even, odd, y_even, y_odd, z_face, ubox, uhalf, rows8, raw, tmp, sems
):
    fields = (f1, f2, f3)
    gots = (r0, r1, r2)
    rows = pl.ds(3 * BOX, HALF)
    for q in range(PER_DEV):
        source = plan[q]

        @pl.when(source < 4)
        def _():
            box = jnp.minimum(source, 3)
            pltpu.make_async_copy(f0.at[box], ubox.at[q], sems.at[3, q]).start()
            for f in range(3):
                pltpu.make_async_copy(fields[f].at[box], raw.at[f, q], sems.at[f, q]).start()

        for k in range(ROUNDS):

            @pl.when(source == 4 + k)
            def _():
                pltpu.make_async_copy(gots[k].at[rows], uhalf.at[q], sems.at[3, q]).start()
                for f in range(3):
                    pltpu.make_async_copy(gots[k].at[pl.ds(f * BOX, BOX)], raw.at[f, q], sems.at[f, q]).start()

    lane = iota(1)
    m64 = (lane & 64) != 0
    m32 = (lane & 32) != 0
    is_odd = odd_cell()

    def relayout(load):
        for t in range(4):
            for jj in range(2):
                j = 2 * t + jj
                a = [load(k, slice(j * 128, (j + 1) * 128)) for k in range(4)]
                n02 = lroll(jnp.where(m64, a[0], a[2]), 64)
                n13 = lroll(jnp.where(m64, a[1], a[3]), 64)
                n0, n2 = jnp.where(m64, n02, a[0]), jnp.where(m64, a[2], n02)
                n1, n3 = jnp.where(m64, n13, a[1]), jnp.where(m64, a[3], n13)
                b = [
                    jnp.where(m32, lroll(n1, 32), n0),
                    jnp.where(m32, n1, lroll(n0, 96)),
                    jnp.where(m32, lroll(n3, 32), n2),
                    jnp.where(m32, n3, lroll(n2, 96)),
                ]
                for q in range(4):
                    y = jj * 4 + q
                    tmp[t, y * 8 : y * 8 + 8, :] = b[q]

    for f in range(3):
        for q in range(PER_DEV):
            pltpu.make_async_copy(f0.at[0], raw.at[f, q], sems.at[f, q]).wait()

        def step(i, carry):
            xt = pl.multiple_of(i * 8, 8)
            relayout(lambda k, lanes: raw[f, k, pl.ds(xt, 8), lanes])
            for t in range(4):
                ys = slice(t * 8, t * 8 + 8)
                for x in range(0, 8, 2):
                    lower = tmp[t, pl.ds(x, 8, stride=8), :]
                    upper = tmp[t, pl.ds(x + 1, 8, stride=8), :]
                    j = i * 4 + x // 2
                    home[(F1, A1, B1)[f], j, ys, :] = jnp.where(is_odd, lower, upper)
                    home[(F0, A0, B0)[f], j, ys, :] = jnp.where(is_odd, upper, lower)
            return carry

        lax.fori_loop(0, 4, step, 0, unroll=2)

    for q in range(PER_DEV):
        mine = plan[q] < 4

        @pl.when(mine)
        def _():
            pltpu.make_async_copy(f0.at[0], ubox.at[q], sems.at[3, q]).wait()
            halve(ubox.at[q], rows8.at[q], uhalf.at[q])

        @pl.when(jnp.logical_not(mine))
        def _():
            pltpu.make_async_copy(r0.at[rows], uhalf.at[q], sems.at[3, q]).wait()

    for i in range(2):
        relayout(lambda k, lanes: uhalf[k, 8 * i : 8 * i + 8, lanes])
        for t in range(4):
            for x in range(8):
                home[U1, i * 8 + x, t * 8 : t * 8 + 8, :] = tmp[t, pl.ds(x, 8, stride=8), :]

    low = (lax.axis_index("gx") & 1) == 1
    for k, (n, i) in enumerate(LAYERS):
        count = 3 if n < 2 else 2
        low_side, high_side = count - 1 - i, HALF - count + i
        for t in range(4):
            ys = slice(t * 8, t * 8 + 8)
            lo, hi = home[n, low_side, ys, :], home[n, high_side, ys, :]
            if i == 0 and n in SHARED:
                lo = jnp.where(is_odd, lo, lroll(home[SHARED[n], low_side, ys, :], 1))
                hi = jnp.where(is_odd, lroll(home[SHARED[n], high_side, ys, :], 1), hi)
            even[k, ys, :] = jnp.where(low, lo, hi)
            odd[k, ys, :] = jnp.where(low, hi, lo)

    low_y = (lax.axis_index("gy") & 1) == 1

    def faces(m, carry):
        tiles = [[[home[n, 2 * m + i, 8 * t : 8 * t + 8, :] for n in range(7)] for t in range(4)] for i in range(2)]
        for w, (lo, hi) in enumerate(face_rows(*[(tiles[i][0], tiles[i][3]) for i in range(2)])):
            y_even[7 * m + w] = jnp.where(low_y, lo, hi)
            y_odd[7 * m + w] = jnp.where(low_y, hi, lo)
        for i in range(2):
            for v in range(2):
                z_face[2 * m + i, v] = face_lanes(tiles[i][2 * v], tiles[i][2 * v + 1])
        return carry

    lax.fori_loop(0, HALF // 2, faces, 0)


def assemble(plan, fields, gots):
    any_spec = pl.BlockSpec(memory_space=pl.ANY)
    hbm = pl.BlockSpec(memory_space=pltpu.HBM)
    vmem = pl.BlockSpec(memory_space=pltpu.VMEM)
    face = jax.ShapeDtypeStruct((len(LAYERS), BOX, 128), F32)
    rows = jax.ShapeDtypeStruct((7 * HALF // 2, 8, 128), F32)
    return pl.pallas_call(
        assemble_kernel,
        out_shape=(
            jax.ShapeDtypeStruct((7, HALF, BOX, 128), F32),
            face,
            face,
            rows,
            rows,
            jax.ShapeDtypeStruct((HALF, 2, 8, 128), F32),
        ),
        in_specs=[pl.BlockSpec(memory_space=pltpu.SMEM)] + [hbm] * 4 + [any_spec] * 3,
        out_specs=(vmem,) * 6,
        scratch_shapes=[
            pltpu.VMEM((PER_DEV, BOX, BOX * BOX), F32),
            pltpu.VMEM((PER_DEV, HALF, BOX * BOX), F32),
            pltpu.VMEM((PER_DEV, 8, BOX, 128), F32),
            pltpu.VMEM((3, PER_DEV, BOX, BOX * BOX), F32),
            pltpu.VMEM((4, 64, 128), F32),
            pltpu.SemaphoreType.DMA((4, PER_DEV)),
        ],
        compiler_params=pltpu.CompilerParams(vmem_limit_bytes=12 * MIB),
        name="assemble",
    )(plan, *fields, *gots)


def halo_of(axis, count, even, odd):
    i = lax.axis_index(axis)
    low_first = (i & 1) == 1
    low = jnp.where(i > 0, jnp.where(low_first, even, odd), 0.0)
    high = jnp.where(i < count - 1, jnp.where(low_first, odd, even), 0.0)
    return low, high


def x_halo_tiles(even, odd, t):
    ys = slice(t * 8, t * 8 + 8)
    pairs = {}
    for k, (n, i) in enumerate(LAYERS):
        low, high = halo_of("gx", N_GX, even[k, ys, :], odd[k, ys, :])
        count = 3 if n < 2 else 2
        spots = (SIDE - count + i, SIDE + HALF + count - 1 - i)
        for spot, tile in zip(spots, (low, high)):
            pairs.setdefault(spot, {})[n] = tile
            if i == 0 and n in SHARED:
                pairs[spot][SHARED[n]] = lroll(tile, -1)
    return pairs


EDGES = (1, 2, SIDE + HALF, SIDE + HALF + 1)


def edge_y_kernel(x_even, x_odd, even, odd):
    low = (lax.axis_index("gy") & 1) == 1
    near, far = x_halo_tiles(x_even, x_odd, 0), x_halo_tiles(x_even, x_odd, 3)
    for m in range(2):
        for w, (lo, hi) in enumerate(face_rows(*[(near[k], far[k]) for k in EDGES[2 * m : 2 * m + 2]])):
            even[7 * m + w] = jnp.where(low, lo, hi)
            odd[7 * m + w] = jnp.where(low, hi, lo)


PAD = (8, 8, 8, 0, 0, 0, 0)


def edge_z_kernel(home, x_even, x_odd, y_even, y_odd, e_even, e_odd, u1, b1, b0, f0, a0, f1, a1, edge):
    outs = (u1, b1, b0, f0, a0, f1, a1)

    def halo(even, odd, m, pairs):
        low_high = [halo_of("gy", N_GY, even[7 * m + w], odd[7 * m + w]) for w in range(7)]
        l3, h3 = low_high[6]
        for i, k in enumerate(pairs):
            (l0, h0), (l1, h1), (l2, h2) = low_high[3 * i : 3 * i + 3]
            lows = (sroll(l0, 3), sroll(l1, 3), sroll(l2, 4), l2, sroll(l3, 4) if i == 0 else l3, l0, l1)
            highs = (h0, h1, h2, sroll(h2, 4), h3 if i == 0 else sroll(h3, 4), sroll(h0, 3), sroll(h1, 3))
            for n in range(7):
                outs[n][k, PAD[n] : PAD[n] + 8, :] = lows[n]
                outs[n][k, PAD[n] + 40 : PAD[n] + 48, :] = highs[n]

    def tiles(k, t):
        return [outs[n][k, PAD[n] + t * 8 : PAD[n] + t * 8 + 8, :] for n in range(7)]

    def copy(m, carry):
        for i in range(2):
            for n in range(7):
                outs[n][2 * m + i + SIDE, PAD[n] + 8 : PAD[n] + 40, :] = home[n, 2 * m + i]
        halo(y_even, y_odd, m, (2 * m + SIDE, 2 * m + SIDE + 1))
        for i in range(2):
            k = 2 * m + i + SIDE
            edge[12 + 2 * m + i] = face_lanes(tiles(k, 0), tiles(k, 5))
        return carry

    lax.fori_loop(0, HALF // 2, copy, 0)
    for t in range(4):
        for k, fields in x_halo_tiles(x_even, x_odd, t).items():
            for n, tile in fields.items():
                outs[n][k, PAD[n] + 8 + t * 8 : PAD[n] + 16 + t * 8, :] = tile
    for m in range(2):
        halo(e_even, e_odd, m, EDGES[2 * m : 2 * m + 2])
    for i, k in enumerate(EDGES):
        for v in range(3):
            edge[3 * i + v] = face_lanes(tiles(k, 2 * v), tiles(k, 2 * v + 1))


def sweep_kernel(
    u1, b1, b0, f0, a0, f1, a1, z_even, z_odd, e_even, e_odd, sol, res, um0, um1, ua0, ua1, ba0, ba1, fax, co, dg
):
    lane = iota(1)
    first, last = lane == 0, lane == 127
    place = lane & 63
    is_odd = odd_cell()
    u = ((um0, ua0), (um1, ua1))
    b = ((b0, ba0), (b1, ba1))
    fa = (((f0, a0), (fax.at[0], fax.at[1])), ((f1, a1), (fax.at[2], fax.at[3])))
    starts = [2 * sum(WIDTH[:n]) for n in range(7)]
    high_part = functools.reduce(
        jnp.logical_or, [(place >= starts[n]) & (place < starts[n] + WIDTH[n]) for n in range(7)]
    )
    aux = (ua1, ba1, ba0, fax.at[0], fax.at[1], fax.at[2], fax.at[3])

    def unpack(k, even, odd, spots):
        low, high = halo_of("gz", N_GZ, even, odd)
        both = jnp.where(high_part, low, high)
        for w, t in enumerate(spots):
            for n in range(7):
                aux[n][k, PAD[n] + t * 8 : PAD[n] + t * 8 + 8, :] = lroll(both, -(64 * w + starts[n] + WIDTH[n]))

    def unpack_pair(j, carry):
        for v in range(2):
            unpack(j + SIDE, z_even[j, v], z_odd[j, v], (1 + 2 * v, 2 + 2 * v))
        unpack(j + SIDE, e_even[12 + j], e_odd[12 + j], (0, 5))
        return carry

    um1[...] = u1[...]
    lax.fori_loop(0, HALF, unpack_pair, 0, unroll=2)
    for i, k in enumerate(EDGES):
        for v in range(3):
            unpack(k, e_even[3 * i + v], e_odd[3 * i + v], (2 * v, 2 * v + 1))

    def around(c, field, k, t, spans):
        r = 8 + t * 8
        main, side = field[1 - c]
        m, a = main[k, r : r + 8, :], side[k, r : r + 8, :]
        m1, a1 = lroll(m, 1), lroll(a, 1)
        m2, a2 = lroll(m, 127), lroll(a, 127)
        below = (jnp.where(first, a1, m1), jnp.where(first, m1, a1))
        above = (jnp.where(last, a2, m2), jnp.where(last, m2, a2))
        out = []
        for s in spans:
            ref = (main, side)[s]
            back, ahead = ref[k - 1, r : r + 8, :], ref[k + 1, r : r + 8, :]
            beside = jnp.where(is_odd, back, ahead) if c else jnp.where(is_odd, ahead, back)
            out.append(((m, a)[s], beside, ref[k, r - 1 : r + 7, :], ref[k, r + 1 : r + 9, :], below[s], above[s]))
        return out

    def coefs(k, carry):
        for c in range(2):
            for t in range(6):
                rows = slice(t * 8, 8 + t * 8)
                near = around(c, b, k, t, (0, 1))
                for s in range(2):
                    mid = b[c][s][k, 8 + t * 8 : 16 + t * 8, :]
                    f, a = [ref[k, rows, :] for ref in fa[c][s]]
                    faces = [0.5 * (mid + v) for v in near[s]]
                    diag = a + (faces[0] + faces[1]) + (faces[2] + faces[3]) + (faces[4] + faces[5])
                    inverse = jnp.where(mid > 0, 1.0 / diag, 0.0)
                    for n in range(6):
                        co[c, s, n, k - 1, rows, :] = faces[n] * inverse
                    co[c, s, 6, k - 1, rows, :] = f * inverse
                    if s == 0:
                        dg[c, k - 1, rows, :] = diag
        return carry

    lax.fori_loop(1, PAIRS - 1, coefs, 0, unroll=2)

    def update(c, k, t, spans):
        rows = slice(t * 8, 8 + t * 8)
        new = []
        for s, v in zip(spans, around(c, u, k, t, spans)):
            w = [co[c, s, n, k - 1, rows, :] for n in range(7)]
            x = w[0] * v[0] + w[1] * v[1]
            y = w[2] * v[2] + w[3] * v[3]
            z = w[4] * v[4] + w[5] * v[5]
            new.append(w[6] + ((x + y) + z))
        return new

    for half in range(2 * SWEEPS):
        c = half % 2

        def sweep(k, carry):
            for t in range(6):
                for s, new in enumerate(update(c, k, t, (0, 1))):
                    u[c][s][k, 8 + t * 8 : 16 + t * 8, :] = new
            return carry

        out = half // 2
        lax.fori_loop(1 + out, PAIRS - 1 - out, sweep, 0, unroll=3 if out else 4)

    def finish(j, carry):
        k = j + SIDE
        for t in range(1, 5):
            ys = slice(t * 8 - 8, t * 8)
            rows = slice(t * 8, t * 8 + 8)
            now = [u[c][0][k, 8 + t * 8 : 16 + t * 8, :] for c in range(2)]
            rest = [dg[c, k - 1, rows, :] * (update(c, k, t, (0,))[0] - now[c]) for c in range(2)]
            for ref, (v0, v1) in ((sol, now), (res, rest)):
                ref[2 * j, ys, :] = jnp.where(is_odd, v1, v0)
                ref[2 * j + 1, ys, :] = jnp.where(is_odd, v0, v1)
        return carry

    lax.fori_loop(0, HALF, finish, 0, unroll=2)


def on_vmem(kernel, out_shape, scratch, name, limit, *args):
    vmem = pl.BlockSpec(memory_space=pltpu.VMEM)
    return pl.pallas_call(
        kernel,
        out_shape=out_shape,
        in_specs=[vmem] * len(args),
        out_specs=tuple([vmem] * len(out_shape)),
        scratch_shapes=scratch,
        compiler_params=pltpu.CompilerParams(vmem_limit_bytes=limit * MIB),
        name=name,
    )(*args)


def edge_y(x_even, x_odd):
    face = jax.ShapeDtypeStruct((14, 8, 128), F32)
    return on_vmem(edge_y_kernel, (face, face), [], "edge_y", 10, x_even, x_odd)


def edge_z(*args):
    grown = [jax.ShapeDtypeStruct((PAIRS, 48 + 2 * PAD[n], 128), F32) for n in range(7)]
    face = jax.ShapeDtypeStruct((12 + HALF, 8, 128), F32)
    return on_vmem(edge_z_kernel, (*grown, face), [], "edge_z", 16, *args)


def sweeps(grown, *faces):
    block = jax.ShapeDtypeStruct((BOX, BOX, 128), F32)
    padded = pltpu.VMEM((PAIRS, 64, 128), F32)
    scratch = [padded] * 6 + [
        pltpu.VMEM((4, PAIRS, 48, 128), F32),
        pltpu.VMEM((2, 2, 7, PAIRS - 2, 48, 128), F32),
        pltpu.VMEM((2, PAIRS - 2, 48, 128), F32),
    ]
    return on_vmem(sweep_kernel, (block, block), scratch, "sweeps", 40, *grown, *faces)


def exchange(axis, count, even, odd):
    pairs = []
    for start in (0, 1):
        step = []
        for i in range(start, count, 2):
            j = (i + 1) % count
            step += [(i, j), (j, i)]
        pairs.append(step)
    return lax.ppermute(even, axis, pairs[0]), lax.ppermute(odd, axis, pairs[1])


def per_device(solution_old, right_side, acoef, bcoef, corners):
    fields = (solution_old, right_side, acoef, bcoef)
    go0, go1, go2, plan, *pays = plan_and_pack(corners, fields)
    gots = [swap_round(go.reshape(()), pay) for go, pay in zip((go0, go1, go2), pays)]
    home, even, odd, near_even, near_odd, face = assemble(plan, fields, gots)
    x = exchange("gx", N_GX, even, odd)
    y = exchange("gy", N_GY, near_even, near_odd)
    z = exchange("gz", N_GZ, face, face)
    y_edges = exchange("gy", N_GY, *edge_y(*x))
    *grown, edge = edge_z(home, *x, *y, *y_edges)
    return sweeps(grown, *z, *exchange("gz", N_GZ, edge, edge))


def solution(mesh):
    boxes = P(("gx", "gy", "gz"), None, None)
    block = P("gx", "gy", "gz")
    return jax.shard_map(
        per_device,
        mesh=mesh,
        in_specs=(boxes, boxes, boxes, boxes, P()),
        out_specs=(block, block),
        check_vma=False,
    )
```

```python
import functools
import itertools

import jax
import jax.numpy as jnp
from jax import lax
from jax.experimental import pallas as pl
from jax.experimental.pallas import tpu as pltpu
from jax.sharding import PartitionSpec as P

BOX = 32
N_GX, N_GY, N_GZ = 4, 8, 8
PER_DEV = 4
ROUNDS = 3
HALF = BOX // 2
SIDE = 3
PAIRS = HALF + 2 * SIDE
SWEEPS = 2
F32 = jnp.float32
MIB = 1024 * 1024


def _colourings():
    table = {}
    for p1, p2 in itertools.combinations(range(1, 7), 2):
        codes = set()
        for cyc in itertools.product(range(3), repeat=7):
            if any(cyc[p] == cyc[p - 1] for p in range(7)):
                continue
            if [3 - cyc[p] - cyc[p - 1] for p in (0, p1, p2)] == [0, 1, 2]:
                codes.add(sum(c << (2 * i) for i, c in enumerate(list(cyc) + [0, 1, 2])))
        codes = sorted(codes)
        table[p1 * 7 + p2] = [codes[i % len(codes)] for i in range(CHOICES)]
    return table


CHOICES = 4
COLOURINGS = _colourings()
ORDERS = [sum(c << (2 * i) for i, c in enumerate(o)) for o in itertools.permutations(range(3))]


def _pick(flag, yes, no):
    return jnp.where(flag, jnp.int32(yes) if isinstance(yes, int) else yes, jnp.int32(no) if isinstance(no, int) else no)


def _chain(index, values):
    out = values[-1]
    for i in reversed(range(len(values) - 1)):
        out = jnp.where(index == i, values[i], out)
    return out


def _colour(code, edge):
    return lax.shift_right_logical(code, 2 * edge) & 3


def plan_kernel(
    table, f0, f1, f2, f3, go0, go1, go2, plan, pay0, pay1, pay2, corners, own, succ, swap, spot, boxes, rows8, sems, sem
):
    whole = pltpu.make_async_copy(table, corners, sem)
    whole.start()
    copies = [pltpu.make_async_copy(field, boxes.at[f], sems.at[f]) for f, field in enumerate((f1, f2, f3, f0))]
    for copy in copies:
        copy.start()
    whole.wait()
    gx, me, gz = lax.axis_index("gx"), lax.axis_index("gy"), lax.axis_index("gz")
    stride = N_GZ * PER_DEV
    bases = [gx * (N_GY * stride) + ((gz & 6) + c) * PER_DEV for c in range(2)]

    groups = []
    for c, base in enumerate(bases):
        hot = jnp.int32(0)
        rows = []
        for g in range(N_GY):
            row = [lax.shift_right_logical(corners[1, base + g * stride + s], 5) for s in range(PER_DEV)]
            rows.append(row)
            leaving = sum(_pick(o != g, 1, 0) for o in row)
            hot = hot + _pick(leaving == 3, g, 0)
            for s in range(PER_DEV):
                own[c * 32 + g * PER_DEV + s] = row[s]
        first = jnp.int32(0)
        for g in reversed(range(N_GY)):
            to_hot = jnp.int32(0)
            nxt = jnp.int32(0)
            for o in rows[g]:
                to_hot = to_hot + _pick(o == hot, 1, 0)
                nxt = nxt + _pick((o != g) & (o != hot), o, 0)
            is_swap = _pick(hot == g, 0, to_hot)
            succ[c * 8 + g] = nxt
            swap[c * 8 + g] = is_swap
            first = _pick(is_swap == 1, g, first)
        v = first
        p1 = jnp.int32(0)
        p2 = jnp.int32(0)
        mine = jnp.int32(-1)
        pred = jnp.int32(0)
        cycle = []
        for p in range(7):
            spot[c * 8 + p] = v
            cycle.append(v)
            if p:
                sw = swap[c * 8 + v] == 1
                p2 = _pick(sw & (p1 != 0), p, p2)
                p1 = _pick(sw & (p1 == 0), p, p1)
            mine = _pick(v == me, p, mine)
            nxt = succ[c * 8 + v]
            pred = _pick(nxt == me, v, pred)
            v = nxt
        key = p1 * 7 + p2
        codes = [jnp.int32(0)] * CHOICES
        for k, options in COLOURINGS.items():
            codes = [_pick(key == k, o, code) for o, code in zip(options, codes)]
        swaps = [cycle[0], spot[c * 8 + p1], spot[c * 8 + p2]]
        groups.append((hot, cycle, swaps, codes, mine, pred, p1))

    link, lane = iota(0), iota(1)
    order = _chain(lane & 7, ORDERS + ORDERS[:2])
    load = [jnp.zeros((8, 128), jnp.int32) for _ in range(2)]
    for c in range(2):
        hot, cycle, swaps, codes = groups[c][:4]
        code = _chain(lax.shift_right_logical(lane, 5 - 2 * c) & 3, codes)
        for e in range(10):
            colour = _colour(code, e)
            if c:
                colour = lax.shift_right_logical(order, 2 * colour) & 3
            unit = lax.shift_left(jnp.ones((8, 128), jnp.int32), 8 * colour)
            flows = [(cycle[e], cycle[(e + 1) % 7])] if e < 7 else [(hot, swaps[e - 7]), (swaps[e - 7], hot)]
            for i, j in flows:
                d = (j - i) & 7
                ahead = _pick(d <= 4, d, 0)
                back = _pick(d <= 4, 0, 8 - d)
                load[0] = load[0] + jnp.where(((link - i) & 7) < ahead, unit, 0)
                load[1] = load[1] + jnp.where(((i - link) & 7) < back, unit, 0)
    cost = jnp.zeros((8, 128), F32)
    for r in range(ROUNDS):
        busiest = jnp.maximum(*[(lax.shift_right_logical(v, 8 * r) & 255).astype(F32) for v in load])
        for shift in (4, 2, 1):
            busiest = jnp.maximum(busiest, sroll(busiest, shift))
        cost = cost + busiest
    best = jnp.min(cost * 128.0 + lane.astype(F32)).astype(jnp.int32) & 127

    mine_second = (gz & 1) == 1

    def of_mine(values):
        return jnp.where(mine_second, values[1], values[0])

    code_a = _chain(lax.shift_right_logical(best, 5) & 3, groups[0][3])
    code_b = _chain(lax.shift_right_logical(best, 3) & 3, groups[1][3])
    order = jnp.where(mine_second, _chain(best & 7, [jnp.int32(o) for o in ORDERS + ORDERS[:2]]), ORDERS[0])
    code = of_mine((code_a, code_b))

    def round_of(edge):
        return lax.shift_right_logical(order, 2 * _colour(code, edge)) & 3

    hot = of_mine([g[0] for g in groups])
    spots = [of_mine([g[2][i] for g in groups]) for i in range(3)]
    mine, pred, p1 = [of_mine([g[i] for g in groups]) for i in (4, 5, 6)]
    c8, c32 = (gz & 1) * 8, (gz & 1) * 32
    base = of_mine(bases)

    def inner(g, s):
        return lax.shift_right_logical(corners[2, base + g * stride + s], 5) & 3

    star = [round_of(7 + i) for i in range(3)]
    is_hot = me == hot
    at = jnp.maximum(mine, 0)
    out_round = round_of(at)
    in_round = round_of(_pick(at == 0, 6, at - 1))
    my_succ = succ[c8 + me]
    swaps_here = jnp.logical_not(is_hot) & (swap[c8 + me] == 1)
    swap_at = _pick(swaps_here, _pick(at == 0, star[0], _pick(at == p1, star[1], star[2])), -1)
    places, arrives, slots = [], [], []
    for k in range(ROUNDS):
        hot_partner = sum(_pick(star[i] == k, spots[i], 0) for i in range(3))
        kind = _pick(swap_at == k, 3, _pick(out_round == k, 1, _pick(in_round == k, 2, 0)))
        partner = _pick(swap_at == k, hot, _pick(out_round == k, my_succ, pred))
        kind = _pick(is_hot, 3, kind)
        partner = _pick(is_hot, hot_partner, partner)
        way = me ^ partner
        up = ((kind == 1) & (me < partner)) | ((kind == 2) & (partner < me))
        (go0, go1, go2)[k][0] = _pick(kind == 0, 0, _pick(kind == 3, way, _pick(up, 7 + way, 14 + way)))
        slot = jnp.int32(0)
        place = jnp.int32(0)
        for s in range(PER_DEV):
            slot = slot + _pick(own[c32 + me * PER_DEV + s] == partner, s, 0)
            place = place + _pick(own[c32 + partner * PER_DEV + s] == me, inner(partner, s), 0)
        slots.append(jnp.minimum(slot, PER_DEV - 1))
        places.append(place)
        arrives.append((kind == 2) | (kind == 3))
    pays = (pay0, pay1, pay2)
    for q in range(PER_DEV):
        source = jnp.int32(0)
        for s in range(PER_DEV):
            source = source + _pick((own[c32 + me * PER_DEV + s] == me) & (inner(me, s) == q), s, 0)
        for k in range(ROUNDS):
            source = source + _pick(arrives[k] & (places[k] == q), 4 + k, 0)
        plan[q] = source
    for copy in copies:
        copy.wait()
    for k in range(ROUNDS):
        for f in range(3):
            pays[k][f * BOX : (f + 1) * BOX, :] = boxes[f, slots[k]]
        halve(boxes.at[3, slots[k]], rows8.at[k], pays[k].at[pl.ds(3 * BOX, HALF)])


def halve(box, tmp, out):
    lane = iota(1)
    is_odd = ((lax.shift_right_logical(lane, 5) + lane) & 1) == 1
    for j in range(8):
        tmp[j] = box[:, j * 128 : j * 128 + 128]
    for h in range(2):
        for j in range(8):
            lower = tmp[j, pl.ds(16 * h, 8, stride=2), :]
            upper = tmp[j, pl.ds(16 * h + 1, 8, stride=2), :]
            out[8 * h : 8 * h + 8, j * 128 : j * 128 + 128] = jnp.where(is_odd, lower, upper)


def plan_and_pack(corners, fields):
    hbm = pl.BlockSpec(memory_space=pltpu.HBM)
    smem = pl.BlockSpec(memory_space=pltpu.SMEM)
    vmem = pl.BlockSpec(memory_space=pltpu.VMEM)
    pay = jax.ShapeDtypeStruct((3 * BOX + HALF, BOX * BOX), F32)
    return pl.pallas_call(
        plan_kernel,
        out_shape=(*[jax.ShapeDtypeStruct((1,), jnp.int32)] * 3, jax.ShapeDtypeStruct((PER_DEV,), jnp.int32), pay, pay, pay),
        in_specs=[hbm] * 5,
        out_specs=(smem, smem, smem, smem, vmem, vmem, vmem),
        scratch_shapes=[
            pltpu.SMEM(corners.shape, jnp.int32),
            pltpu.SMEM((64,), jnp.int32),
            pltpu.SMEM((16,), jnp.int32),
            pltpu.SMEM((16,), jnp.int32),
            pltpu.SMEM((16,), jnp.int32),
            pltpu.VMEM((4, PER_DEV, BOX, BOX * BOX), F32),
            pltpu.VMEM((ROUNDS, 8, BOX, 128), F32),
            pltpu.SemaphoreType.DMA((4,)),
            pltpu.SemaphoreType.DMA,
        ],
        compiler_params=pltpu.CompilerParams(vmem_limit_bytes=60 * MIB),
        name="plan",
    )(corners, *fields)


def swap_round(branch, pay):
    def stay(x):
        return x

    def move(pairs, x):
        return lax.ppermute(x, "gy", pairs)

    branches = [stay]
    for r in range(1, 8):
        branches.append(functools.partial(move, [(i, i ^ r) for i in range(8)]))
    for r in range(1, 8):
        branches.append(functools.partial(move, [(i, i ^ r) for i in range(8) if i < i ^ r]))
    for r in range(1, 8):
        branches.append(functools.partial(move, [(i, i ^ r) for i in range(8) if i > i ^ r]))
    return lax.switch(branch, branches, pay)


def iota(dim):
    return lax.broadcasted_iota(jnp.int32, (8, 128), dim)


def lroll(v, shift):
    shift %= 128
    return pltpu.roll(v, shift, 1) if shift else v


def sroll(v, shift):
    shift %= 8
    return pltpu.roll(v, shift, 0) if shift else v


U1, B1, B0, F0, A0, F1, A1 = range(7)
WIDTH = (5, 5, 4, 4, 4, 3, 3)
LAYERS = [(U1, 0), (U1, 1), (U1, 2), (B1, 1), (B1, 2)]
LAYERS += [(n, i) for n in (B0, F0, A0) for i in range(2)] + [(F1, 0), (F1, 1), (A1, 1)]
SHARED = {U1: B1, F1: A1}


def odd_cell():
    return ((iota(0) + iota(1)) & 1) == 1


def face_rows(first, second):
    sub = iota(0)
    out = []
    for near, far in (first, second):
        out.append((jnp.where(sub < 5, near[U1], sroll(near[F1], 5)), jnp.where(sub < 5, sroll(far[U1], -3), far[F1])))
        out.append((jnp.where(sub < 5, near[B1], sroll(near[A1], 5)), jnp.where(sub < 5, sroll(far[B1], -3), far[A1])))
        out.append((jnp.where(sub < 4, near[B0], sroll(near[F0], 4)), jnp.where(sub < 4, sroll(far[B0], 4), far[F0])))
    (n0, f0), (n1, f1) = first, second
    lo = jnp.where(sub < 4, n0[A0], sroll(n1[A0], 4))
    hi = jnp.where(sub < 4, sroll(f0[A0], 4), f1[A0])
    return out + [(lo, hi)]


def face_lanes(first, second):
    lane = iota(1)
    place = lane & 63
    both = []
    for w, tiles in enumerate((first, second)):
        at = 0
        ends = []
        for n in range(7):
            ends.append((lroll(tiles[n], 64 * w + at + WIDTH[n]), at + 2 * WIDTH[n]))
            at += 2 * WIDTH[n]
        group = ends[-1][0]
        for tile, end in reversed(ends[:-1]):
            group = jnp.where(place < end, tile, group)
        both.append(group)
    return jnp.where(lane < 64, both[0], both[1])


def assemble_kernel(
    plan, f0, f1, f2, f3, r0, r1, r2, home, even, odd, y_even, y_odd, z_face, ubox, uhalf, rows8, raw, tmp, sems
):
    fields = (f1, f2, f3)
    gots = (r0, r1, r2)
    rows = pl.ds(3 * BOX, HALF)
    for q in range(PER_DEV):
        source = plan[q]

        @pl.when(source < 4)
        def _():
            box = jnp.minimum(source, 3)
            pltpu.make_async_copy(f0.at[box], ubox.at[q], sems.at[3, q]).start()
            for f in range(3):
                pltpu.make_async_copy(fields[f].at[box], raw.at[f, q], sems.at[f, q]).start()

        for k in range(ROUNDS):

            @pl.when(source == 4 + k)
            def _():
                pltpu.make_async_copy(gots[k].at[rows], uhalf.at[q], sems.at[3, q]).start()
                for f in range(3):
                    pltpu.make_async_copy(gots[k].at[pl.ds(f * BOX, BOX)], raw.at[f, q], sems.at[f, q]).start()

    lane = iota(1)
    m64 = (lane & 64) != 0
    m32 = (lane & 32) != 0
    is_odd = odd_cell()

    def relayout(load):
        for t in range(4):
            for jj in range(2):
                j = 2 * t + jj
                a = [load(k, slice(j * 128, (j + 1) * 128)) for k in range(4)]
                n02 = lroll(jnp.where(m64, a[0], a[2]), 64)
                n13 = lroll(jnp.where(m64, a[1], a[3]), 64)
                n0, n2 = jnp.where(m64, n02, a[0]), jnp.where(m64, a[2], n02)
                n1, n3 = jnp.where(m64, n13, a[1]), jnp.where(m64, a[3], n13)
                b = [
                    jnp.where(m32, lroll(n1, 32), n0),
                    jnp.where(m32, n1, lroll(n0, 96)),
                    jnp.where(m32, lroll(n3, 32), n2),
                    jnp.where(m32, n3, lroll(n2, 96)),
                ]
                for q in range(4):
                    y = jj * 4 + q
                    tmp[t, y * 8 : y * 8 + 8, :] = b[q]

    for f in range(3):
        for q in range(PER_DEV):
            pltpu.make_async_copy(f0.at[0], raw.at[f, q], sems.at[f, q]).wait()

        def step(i, carry):
            xt = pl.multiple_of(i * 8, 8)
            relayout(lambda k, lanes: raw[f, k, pl.ds(xt, 8), lanes])
            for t in range(4):
                ys = slice(t * 8, t * 8 + 8)
                for x in range(0, 8, 2):
                    lower = tmp[t, pl.ds(x, 8, stride=8), :]
                    upper = tmp[t, pl.ds(x + 1, 8, stride=8), :]
                    j = i * 4 + x // 2
                    home[(F1, A1, B1)[f], j, ys, :] = jnp.where(is_odd, lower, upper)
                    home[(F0, A0, B0)[f], j, ys, :] = jnp.where(is_odd, upper, lower)
            return carry

        lax.fori_loop(0, 4, step, 0, unroll=2)

    for q in range(PER_DEV):
        mine = plan[q] < 4

        @pl.when(mine)
        def _():
            pltpu.make_async_copy(f0.at[0], ubox.at[q], sems.at[3, q]).wait()
            halve(ubox.at[q], rows8.at[q], uhalf.at[q])

        @pl.when(jnp.logical_not(mine))
        def _():
            pltpu.make_async_copy(r0.at[rows], uhalf.at[q], sems.at[3, q]).wait()

    for i in range(2):
        relayout(lambda k, lanes: uhalf[k, 8 * i : 8 * i + 8, lanes])
        for t in range(4):
            for x in range(8):
                home[U1, i * 8 + x, t * 8 : t * 8 + 8, :] = tmp[t, pl.ds(x, 8, stride=8), :]

    low = (lax.axis_index("gx") & 1) == 1
    for k, (n, i) in enumerate(LAYERS):
        count = 3 if n < 2 else 2
        low_side, high_side = count - 1 - i, HALF - count + i
        for t in range(4):
            ys = slice(t * 8, t * 8 + 8)
            lo, hi = home[n, low_side, ys, :], home[n, high_side, ys, :]
            if i == 0 and n in SHARED:
                lo = jnp.where(is_odd, lo, lroll(home[SHARED[n], low_side, ys, :], 1))
                hi = jnp.where(is_odd, lroll(home[SHARED[n], high_side, ys, :], 1), hi)
            even[k, ys, :] = jnp.where(low, lo, hi)
            odd[k, ys, :] = jnp.where(low, hi, lo)

    low_y = (lax.axis_index("gy") & 1) == 1

    def faces(m, carry):
        tiles = [[[home[n, 2 * m + i, 8 * t : 8 * t + 8, :] for n in range(7)] for t in range(4)] for i in range(2)]
        for w, (lo, hi) in enumerate(face_rows(*[(tiles[i][0], tiles[i][3]) for i in range(2)])):
            y_even[7 * m + w] = jnp.where(low_y, lo, hi)
            y_odd[7 * m + w] = jnp.where(low_y, hi, lo)
        for i in range(2):
            for v in range(2):
                z_face[2 * m + i, v] = face_lanes(tiles[i][2 * v], tiles[i][2 * v + 1])
        return carry

    lax.fori_loop(0, HALF // 2, faces, 0)


def assemble(plan, fields, gots):
    any_spec = pl.BlockSpec(memory_space=pl.ANY)
    hbm = pl.BlockSpec(memory_space=pltpu.HBM)
    vmem = pl.BlockSpec(memory_space=pltpu.VMEM)
    face = jax.ShapeDtypeStruct((len(LAYERS), BOX, 128), F32)
    rows = jax.ShapeDtypeStruct((7 * HALF // 2, 8, 128), F32)
    return pl.pallas_call(
        assemble_kernel,
        out_shape=(
            jax.ShapeDtypeStruct((7, HALF, BOX, 128), F32),
            face,
            face,
            rows,
            rows,
            jax.ShapeDtypeStruct((HALF, 2, 8, 128), F32),
        ),
        in_specs=[pl.BlockSpec(memory_space=pltpu.SMEM)] + [hbm] * 4 + [any_spec] * 3,
        out_specs=(vmem,) * 6,
        scratch_shapes=[
            pltpu.VMEM((PER_DEV, BOX, BOX * BOX), F32),
            pltpu.VMEM((PER_DEV, HALF, BOX * BOX), F32),
            pltpu.VMEM((PER_DEV, 8, BOX, 128), F32),
            pltpu.VMEM((3, PER_DEV, BOX, BOX * BOX), F32),
            pltpu.VMEM((4, 64, 128), F32),
            pltpu.SemaphoreType.DMA((4, PER_DEV)),
        ],
        compiler_params=pltpu.CompilerParams(vmem_limit_bytes=12 * MIB),
        name="assemble",
    )(plan, *fields, *gots)


def halo_of(axis, count, even, odd):
    i = lax.axis_index(axis)
    low_first = (i & 1) == 1
    low = jnp.where(i > 0, jnp.where(low_first, even, odd), 0.0)
    high = jnp.where(i < count - 1, jnp.where(low_first, odd, even), 0.0)
    return low, high


def x_halo_tiles(even, odd, t):
    ys = slice(t * 8, t * 8 + 8)
    pairs = {}
    for k, (n, i) in enumerate(LAYERS):
        low, high = halo_of("gx", N_GX, even[k, ys, :], odd[k, ys, :])
        count = 3 if n < 2 else 2
        spots = (SIDE - count + i, SIDE + HALF + count - 1 - i)
        for spot, tile in zip(spots, (low, high)):
            pairs.setdefault(spot, {})[n] = tile
            if i == 0 and n in SHARED:
                pairs[spot][SHARED[n]] = lroll(tile, -1)
    return pairs


EDGES = (1, 2, SIDE + HALF, SIDE + HALF + 1)


def edge_y_kernel(x_even, x_odd, even, odd):
    low = (lax.axis_index("gy") & 1) == 1
    near, far = x_halo_tiles(x_even, x_odd, 0), x_halo_tiles(x_even, x_odd, 3)
    for m in range(2):
        for w, (lo, hi) in enumerate(face_rows(*[(near[k], far[k]) for k in EDGES[2 * m : 2 * m + 2]])):
            even[7 * m + w] = jnp.where(low, lo, hi)
            odd[7 * m + w] = jnp.where(low, hi, lo)


PAD = (8, 8, 8, 0, 0, 0, 0)


def edge_z_kernel(home, x_even, x_odd, y_even, y_odd, e_even, e_odd, u1, b1, b0, f0, a0, f1, a1, edge):
    outs = (u1, b1, b0, f0, a0, f1, a1)

    def halo(even, odd, m, pairs):
        low_high = [halo_of("gy", N_GY, even[7 * m + w], odd[7 * m + w]) for w in range(7)]
        l3, h3 = low_high[6]
        for i, k in enumerate(pairs):
            (l0, h0), (l1, h1), (l2, h2) = low_high[3 * i : 3 * i + 3]
            lows = (sroll(l0, 3), sroll(l1, 3), sroll(l2, 4), l2, sroll(l3, 4) if i == 0 else l3, l0, l1)
            highs = (h0, h1, h2, sroll(h2, 4), h3 if i == 0 else sroll(h3, 4), sroll(h0, 3), sroll(h1, 3))
            for n in range(7):
                outs[n][k, PAD[n] : PAD[n] + 8, :] = lows[n]
                outs[n][k, PAD[n] + 40 : PAD[n] + 48, :] = highs[n]

    def tiles(k, t):
        return [outs[n][k, PAD[n] + t * 8 : PAD[n] + t * 8 + 8, :] for n in range(7)]

    def copy(m, carry):
        for i in range(2):
            for n in range(7):
                outs[n][2 * m + i + SIDE, PAD[n] + 8 : PAD[n] + 40, :] = home[n, 2 * m + i]
        halo(y_even, y_odd, m, (2 * m + SIDE, 2 * m + SIDE + 1))
        for i in range(2):
            k = 2 * m + i + SIDE
            edge[12 + 2 * m + i] = face_lanes(tiles(k, 0), tiles(k, 5))
        return carry

    lax.fori_loop(0, HALF // 2, copy, 0)
    for t in range(4):
        for k, fields in x_halo_tiles(x_even, x_odd, t).items():
            for n, tile in fields.items():
                outs[n][k, PAD[n] + 8 + t * 8 : PAD[n] + 16 + t * 8, :] = tile
    for m in range(2):
        halo(e_even, e_odd, m, EDGES[2 * m : 2 * m + 2])
    for i, k in enumerate(EDGES):
        for v in range(3):
            edge[3 * i + v] = face_lanes(tiles(k, 2 * v), tiles(k, 2 * v + 1))


def sweep_kernel(
    u1, b1, b0, f0, a0, f1, a1, z_even, z_odd, e_even, e_odd, sol, res, um0, um1, ua0, ua1, ba0, ba1, fax, co, dg
):
    lane = iota(1)
    first, last = lane == 0, lane == 127
    place = lane & 63
    is_odd = odd_cell()
    u = ((um0, ua0), (um1, ua1))
    b = ((b0, ba0), (b1, ba1))
    fa = (((f0, a0), (fax.at[0], fax.at[1])), ((f1, a1), (fax.at[2], fax.at[3])))
    starts = [2 * sum(WIDTH[:n]) for n in range(7)]
    high_part = functools.reduce(
        jnp.logical_or, [(place >= starts[n]) & (place < starts[n] + WIDTH[n]) for n in range(7)]
    )
    aux = (ua1, ba1, ba0, fax.at[0], fax.at[1], fax.at[2], fax.at[3])

    def unpack(k, even, odd, spots):
        low, high = halo_of("gz", N_GZ, even, odd)
        both = jnp.where(high_part, low, high)
        for w, t in enumerate(spots):
            for n in range(7):
                aux[n][k, PAD[n] + t * 8 : PAD[n] + t * 8 + 8, :] = lroll(both, -(64 * w + starts[n] + WIDTH[n]))

    def unpack_pair(j, carry):
        for v in range(2):
            unpack(j + SIDE, z_even[j, v], z_odd[j, v], (1 + 2 * v, 2 + 2 * v))
        unpack(j + SIDE, e_even[12 + j], e_odd[12 + j], (0, 5))
        return carry

    um1[...] = u1[...]
    lax.fori_loop(0, HALF, unpack_pair, 0, unroll=4)
    for i, k in enumerate(EDGES):
        for v in range(3):
            unpack(k, e_even[3 * i + v], e_odd[3 * i + v], (2 * v, 2 * v + 1))

    def around(c, field, k, t, spans):
        r = 8 + t * 8
        main, side = field[1 - c]
        m, a = main[k, r : r + 8, :], side[k, r : r + 8, :]
        m1, a1 = lroll(m, 1), lroll(a, 1)
        m2, a2 = lroll(m, 127), lroll(a, 127)
        below = (jnp.where(first, a1, m1), jnp.where(first, m1, a1))
        above = (jnp.where(last, a2, m2), jnp.where(last, m2, a2))
        out = []
        for s in spans:
            ref = (main, side)[s]
            back, ahead = ref[k - 1, r : r + 8, :], ref[k + 1, r : r + 8, :]
            beside = jnp.where(is_odd, back, ahead) if c else jnp.where(is_odd, ahead, back)
            out.append(((m, a)[s], beside, ref[k, r - 1 : r + 7, :], ref[k, r + 1 : r + 9, :], below[s], above[s]))
        return out

    def coefs(k, carry):
        for c in range(2):
            for t in range(6):
                rows = slice(t * 8, 8 + t * 8)
                near = around(c, b, k, t, (0, 1))
                for s in range(2):
                    mid = b[c][s][k, 8 + t * 8 : 16 + t * 8, :]
                    f, a = [ref[k, rows, :] for ref in fa[c][s]]
                    faces = [0.5 * (mid + v) for v in near[s]]
                    diag = a + (faces[0] + faces[1]) + (faces[2] + faces[3]) + (faces[4] + faces[5])
                    inverse = jnp.where(mid > 0, 1.0 / diag, 0.0)
                    for n in range(6):
                        co[c, s, n, k - 1, rows, :] = faces[n] * inverse
                    co[c, s, 6, k - 1, rows, :] = f * inverse
                    if s == 0:
                        dg[c, k - 1, rows, :] = diag
        return carry

    lax.fori_loop(1, PAIRS - 1, coefs, 0, unroll=4)

    def update(c, k, t, spans):
        rows = slice(t * 8, 8 + t * 8)
        new = []
        for s, v in zip(spans, around(c, u, k, t, spans)):
            w = [co[c, s, n, k - 1, rows, :] for n in range(7)]
            x = w[0] * v[0] + w[1] * v[1]
            y = w[2] * v[2] + w[3] * v[3]
            z = w[4] * v[4] + w[5] * v[5]
            new.append(w[6] + ((x + y) + z))
        return new

    for half in range(2 * SWEEPS):
        c = half % 2

        def sweep(k, carry):
            for t in range(6):
                for s, new in enumerate(update(c, k, t, (0, 1))):
                    u[c][s][k, 8 + t * 8 : 16 + t * 8, :] = new
            return carry

        out = half // 2
        lax.fori_loop(1 + out, PAIRS - 1 - out, sweep, 0, unroll=6 if out else 5)

    def finish(j, carry):
        k = j + SIDE
        for t in range(1, 5):
            ys = slice(t * 8 - 8, t * 8)
            rows = slice(t * 8, t * 8 + 8)
            now = [u[c][0][k, 8 + t * 8 : 16 + t * 8, :] for c in range(2)]
            rest = [dg[c, k - 1, rows, :] * (update(c, k, t, (0,))[0] - now[c]) for c in range(2)]
            for ref, (v0, v1) in ((sol, now), (res, rest)):
                ref[2 * j, ys, :] = jnp.where(is_odd, v1, v0)
                ref[2 * j + 1, ys, :] = jnp.where(is_odd, v0, v1)
        return carry

    lax.fori_loop(0, HALF, finish, 0, unroll=4)


def on_vmem(kernel, out_shape, scratch, name, limit, *args):
    vmem = pl.BlockSpec(memory_space=pltpu.VMEM)
    return pl.pallas_call(
        kernel,
        out_shape=out_shape,
        in_specs=[vmem] * len(args),
        out_specs=tuple([vmem] * len(out_shape)),
        scratch_shapes=scratch,
        compiler_params=pltpu.CompilerParams(vmem_limit_bytes=limit * MIB),
        name=name,
    )(*args)


def edge_y(x_even, x_odd):
    face = jax.ShapeDtypeStruct((14, 8, 128), F32)
    return on_vmem(edge_y_kernel, (face, face), [], "edge_y", 10, x_even, x_odd)


def edge_z(*args):
    grown = [jax.ShapeDtypeStruct((PAIRS, 48 + 2 * PAD[n], 128), F32) for n in range(7)]
    face = jax.ShapeDtypeStruct((12 + HALF, 8, 128), F32)
    return on_vmem(edge_z_kernel, (*grown, face), [], "edge_z", 16, *args)


def sweeps(grown, *faces):
    block = jax.ShapeDtypeStruct((BOX, BOX, 128), F32)
    padded = pltpu.VMEM((PAIRS, 64, 128), F32)
    scratch = [padded] * 6 + [
        pltpu.VMEM((4, PAIRS, 48, 128), F32),
        pltpu.VMEM((2, 2, 7, PAIRS - 2, 48, 128), F32),
        pltpu.VMEM((2, PAIRS - 2, 48, 128), F32),
    ]
    return on_vmem(sweep_kernel, (block, block), scratch, "sweeps", 40, *grown, *faces)


def exchange(axis, count, even, odd):
    pairs = []
    for start in (0, 1):
        step = []
        for i in range(start, count, 2):
            j = (i + 1) % count
            step += [(i, j), (j, i)]
        pairs.append(step)
    return lax.ppermute(even, axis, pairs[0]), lax.ppermute(odd, axis, pairs[1])


def per_device(solution_old, right_side, acoef, bcoef, corners):
    fields = (solution_old, right_side, acoef, bcoef)
    go0, go1, go2, plan, *pays = plan_and_pack(corners, fields)
    gots = [swap_round(go.reshape(()), pay) for go, pay in zip((go0, go1, go2), pays)]
    home, even, odd, near_even, near_odd, face = assemble(plan, fields, gots)
    x = exchange("gx", N_GX, even, odd)
    y = exchange("gy", N_GY, near_even, near_odd)
    z = exchange("gz", N_GZ, face, face)
    y_edges = exchange("gy", N_GY, *edge_y(*x))
    *grown, edge = edge_z(home, *x, *y, *y_edges)
    return sweeps(grown, *z, *exchange("gz", N_GZ, edge, edge))


def solution(mesh):
    boxes = P(("gx", "gy", "gz"), None, None)
    block = P("gx", "gy", "gz")
    return jax.shard_map(
        per_device,
        mesh=mesh,
        in_specs=(boxes, boxes, boxes, boxes, P()),
        out_specs=(block, block),
        check_vma=False,
    )
```

```python
import functools
import itertools

import jax
import jax.numpy as jnp
from jax import lax
from jax.experimental import pallas as pl
from jax.experimental.pallas import tpu as pltpu
from jax.sharding import PartitionSpec as P

BOX = 32
N_GX, N_GY, N_GZ = 4, 8, 8
PER_DEV = 4
ROUNDS = 3
HALF = BOX // 2
SIDE = 3
PAIRS = HALF + 2 * SIDE
SWEEPS = 2
F32 = jnp.float32
MIB = 1024 * 1024


def _colourings():
    table = {}
    for p1, p2 in itertools.combinations(range(1, 7), 2):
        codes = set()
        for cyc in itertools.product(range(3), repeat=7):
            if any(cyc[p] == cyc[p - 1] for p in range(7)):
                continue
            if [3 - cyc[p] - cyc[p - 1] for p in (0, p1, p2)] == [0, 1, 2]:
                codes.add(sum(c << (2 * i) for i, c in enumerate(list(cyc) + [0, 1, 2])))
        codes = sorted(codes)
        table[p1 * 7 + p2] = [codes[i % len(codes)] for i in range(CHOICES)]
    return table


CHOICES = 4
COLOURINGS = _colourings()
ORDERS = [sum(c << (2 * i) for i, c in enumerate(o)) for o in itertools.permutations(range(3))]


def _pick(flag, yes, no):
    return jnp.where(flag, jnp.int32(yes) if isinstance(yes, int) else yes, jnp.int32(no) if isinstance(no, int) else no)


def _chain(index, values):
    out = values[-1]
    for i in reversed(range(len(values) - 1)):
        out = jnp.where(index == i, values[i], out)
    return out


def _colour(code, edge):
    return lax.shift_right_logical(code, 2 * edge) & 3


def plan_kernel(
    table, f0, f1, f2, f3, go0, go1, go2, plan, pay0, pay1, pay2, corners, own, succ, swap, spot, boxes, rows8, sems, sem
):
    whole = pltpu.make_async_copy(table, corners, sem)
    whole.start()
    copies = [pltpu.make_async_copy(field, boxes.at[f], sems.at[f]) for f, field in enumerate((f1, f2, f3, f0))]
    for copy in copies:
        copy.start()
    whole.wait()
    gx, me, gz = lax.axis_index("gx"), lax.axis_index("gy"), lax.axis_index("gz")
    stride = N_GZ * PER_DEV
    bases = [gx * (N_GY * stride) + ((gz & 6) + c) * PER_DEV for c in range(2)]

    groups = []
    for c, base in enumerate(bases):
        hot = jnp.int32(0)
        rows = []
        for g in range(N_GY):
            row = [lax.shift_right_logical(corners[1, base + g * stride + s], 5) for s in range(PER_DEV)]
            rows.append(row)
            leaving = sum(_pick(o != g, 1, 0) for o in row)
            hot = hot + _pick(leaving == 3, g, 0)
            for s in range(PER_DEV):
                own[c * 32 + g * PER_DEV + s] = row[s]
        first = jnp.int32(0)
        for g in reversed(range(N_GY)):
            to_hot = jnp.int32(0)
            nxt = jnp.int32(0)
            for o in rows[g]:
                to_hot = to_hot + _pick(o == hot, 1, 0)
                nxt = nxt + _pick((o != g) & (o != hot), o, 0)
            is_swap = _pick(hot == g, 0, to_hot)
            succ[c * 8 + g] = nxt
            swap[c * 8 + g] = is_swap
            first = _pick(is_swap == 1, g, first)
        v = first
        p1 = jnp.int32(0)
        p2 = jnp.int32(0)
        mine = jnp.int32(-1)
        pred = jnp.int32(0)
        cycle = []
        for p in range(7):
            spot[c * 8 + p] = v
            cycle.append(v)
            if p:
                sw = swap[c * 8 + v] == 1
                p2 = _pick(sw & (p1 != 0), p, p2)
                p1 = _pick(sw & (p1 == 0), p, p1)
            mine = _pick(v == me, p, mine)
            nxt = succ[c * 8 + v]
            pred = _pick(nxt == me, v, pred)
            v = nxt
        key = p1 * 7 + p2
        codes = [jnp.int32(0)] * CHOICES
        for k, options in COLOURINGS.items():
            codes = [_pick(key == k, o, code) for o, code in zip(options, codes)]
        swaps = [cycle[0], spot[c * 8 + p1], spot[c * 8 + p2]]
        groups.append((hot, cycle, swaps, codes, mine, pred, p1))

    link, lane = iota(0), iota(1)
    order = _chain(lane & 7, ORDERS + ORDERS[:2])
    load = [jnp.zeros((8, 128), jnp.int32) for _ in range(2)]
    for c in range(2):
        hot, cycle, swaps, codes = groups[c][:4]
        code = _chain(lax.shift_right_logical(lane, 5 - 2 * c) & 3, codes)
        for e in range(10):
            colour = _colour(code, e)
            if c:
                colour = lax.shift_right_logical(order, 2 * colour) & 3
            unit = lax.shift_left(jnp.ones((8, 128), jnp.int32), 8 * colour)
            flows = [(cycle[e], cycle[(e + 1) % 7])] if e < 7 else [(hot, swaps[e - 7]), (swaps[e - 7], hot)]
            for i, j in flows:
                d = (j - i) & 7
                ahead = _pick(d <= 4, d, 0)
                back = _pick(d < 4, 0, 8 - d)
                load[0] = load[0] + jnp.where(((link - i) & 7) < ahead, unit * _pick(d == 4, 1, 2), 0)
                load[1] = load[1] + jnp.where(((i - link) & 7) < back, unit * _pick(d == 4, 1, 2), 0)
    cost = jnp.zeros((8, 128), F32)
    for r in range(ROUNDS):
        busiest = jnp.maximum(*[(lax.shift_right_logical(v, 8 * r) & 255).astype(F32) for v in load])
        for shift in (4, 2, 1):
            busiest = jnp.maximum(busiest, sroll(busiest, shift))
        cost = cost + busiest
    best = jnp.min(cost * 128.0 + lane.astype(F32)).astype(jnp.int32) & 127

    mine_second = (gz & 1) == 1

    def of_mine(values):
        return jnp.where(mine_second, values[1], values[0])

    code_a = _chain(lax.shift_right_logical(best, 5) & 3, groups[0][3])
    code_b = _chain(lax.shift_right_logical(best, 3) & 3, groups[1][3])
    order = jnp.where(mine_second, _chain(best & 7, [jnp.int32(o) for o in ORDERS + ORDERS[:2]]), ORDERS[0])
    code = of_mine((code_a, code_b))

    def round_of(edge):
        return lax.shift_right_logical(order, 2 * _colour(code, edge)) & 3

    hot = of_mine([g[0] for g in groups])
    spots = [of_mine([g[2][i] for g in groups]) for i in range(3)]
    mine, pred, p1 = [of_mine([g[i] for g in groups]) for i in (4, 5, 6)]
    c8, c32 = (gz & 1) * 8, (gz & 1) * 32
    base = of_mine(bases)

    def inner(g, s):
        return lax.shift_right_logical(corners[2, base + g * stride + s], 5) & 3

    star = [round_of(7 + i) for i in range(3)]
    is_hot = me == hot
    at = jnp.maximum(mine, 0)
    out_round = round_of(at)
    in_round = round_of(_pick(at == 0, 6, at - 1))
    my_succ = succ[c8 + me]
    swaps_here = jnp.logical_not(is_hot) & (swap[c8 + me] == 1)
    swap_at = _pick(swaps_here, _pick(at == 0, star[0], _pick(at == p1, star[1], star[2])), -1)
    places, arrives, slots = [], [], []
    for k in range(ROUNDS):
        hot_partner = sum(_pick(star[i] == k, spots[i], 0) for i in range(3))
        kind = _pick(swap_at == k, 3, _pick(out_round == k, 1, _pick(in_round == k, 2, 0)))
        partner = _pick(swap_at == k, hot, _pick(out_round == k, my_succ, pred))
        kind = _pick(is_hot, 3, kind)
        partner = _pick(is_hot, hot_partner, partner)
        way = me ^ partner
        up = ((kind == 1) & (me < partner)) | ((kind == 2) & (partner < me))
        (go0, go1, go2)[k][0] = _pick(kind == 0, 0, _pick(kind == 3, way, _pick(up, 7 + way, 14 + way)))
        slot = jnp.int32(0)
        place = jnp.int32(0)
        for s in range(PER_DEV):
            slot = slot + _pick(own[c32 + me * PER_DEV + s] == partner, s, 0)
            place = place + _pick(own[c32 + partner * PER_DEV + s] == me, inner(partner, s), 0)
        slots.append(jnp.minimum(slot, PER_DEV - 1))
        places.append(place)
        arrives.append((kind == 2) | (kind == 3))
    pays = (pay0, pay1, pay2)
    for q in range(PER_DEV):
        source = jnp.int32(0)
        for s in range(PER_DEV):
            source = source + _pick((own[c32 + me * PER_DEV + s] == me) & (inner(me, s) == q), s, 0)
        for k in range(ROUNDS):
            source = source + _pick(arrives[k] & (places[k] == q), 4 + k, 0)
        plan[q] = source
    for copy in copies:
        copy.wait()
    for k in range(ROUNDS):
        for f in range(3):
            pays[k][f * BOX : (f + 1) * BOX, :] = boxes[f, slots[k]]
        halve(boxes.at[3, slots[k]], rows8.at[k], pays[k].at[pl.ds(3 * BOX, HALF)])


def halve(box, tmp, out):
    lane = iota(1)
    is_odd = ((lax.shift_right_logical(lane, 5) + lane) & 1) == 1
    for j in range(8):
        tmp[j] = box[:, j * 128 : j * 128 + 128]
    for h in range(2):
        for j in range(8):
            lower = tmp[j, pl.ds(16 * h, 8, stride=2), :]
            upper = tmp[j, pl.ds(16 * h + 1, 8, stride=2), :]
            out[8 * h : 8 * h + 8, j * 128 : j * 128 + 128] = jnp.where(is_odd, lower, upper)


def plan_and_pack(corners, fields):
    hbm = pl.BlockSpec(memory_space=pltpu.HBM)
    smem = pl.BlockSpec(memory_space=pltpu.SMEM)
    vmem = pl.BlockSpec(memory_space=pltpu.VMEM)
    pay = jax.ShapeDtypeStruct((3 * BOX + HALF, BOX * BOX), F32)
    return pl.pallas_call(
        plan_kernel,
        out_shape=(*[jax.ShapeDtypeStruct((1,), jnp.int32)] * 3, jax.ShapeDtypeStruct((PER_DEV,), jnp.int32), pay, pay, pay),
        in_specs=[hbm] * 5,
        out_specs=(smem, smem, smem, smem, vmem, vmem, vmem),
        scratch_shapes=[
            pltpu.SMEM(corners.shape, jnp.int32),
            pltpu.SMEM((64,), jnp.int32),
            pltpu.SMEM((16,), jnp.int32),
            pltpu.SMEM((16,), jnp.int32),
            pltpu.SMEM((16,), jnp.int32),
            pltpu.VMEM((4, PER_DEV, BOX, BOX * BOX), F32),
            pltpu.VMEM((ROUNDS, 8, BOX, 128), F32),
            pltpu.SemaphoreType.DMA((4,)),
            pltpu.SemaphoreType.DMA,
        ],
        compiler_params=pltpu.CompilerParams(vmem_limit_bytes=60 * MIB),
        name="plan",
    )(corners, *fields)


def swap_round(branch, pay):
    def stay(x):
        return x

    def move(pairs, x):
        return lax.ppermute(x, "gy", pairs)

    branches = [stay]
    for r in range(1, 8):
        branches.append(functools.partial(move, [(i, i ^ r) for i in range(8)]))
    for r in range(1, 8):
        branches.append(functools.partial(move, [(i, i ^ r) for i in range(8) if i < i ^ r]))
    for r in range(1, 8):
        branches.append(functools.partial(move, [(i, i ^ r) for i in range(8) if i > i ^ r]))
    return lax.switch(branch, branches, pay)


def iota(dim):
    return lax.broadcasted_iota(jnp.int32, (8, 128), dim)


def lroll(v, shift):
    shift %= 128
    return pltpu.roll(v, shift, 1) if shift else v


def sroll(v, shift):
    shift %= 8
    return pltpu.roll(v, shift, 0) if shift else v


U1, B1, B0, F0, A0, F1, A1 = range(7)
WIDTH = (5, 5, 4, 4, 4, 3, 3)
LAYERS = [(U1, 0), (U1, 1), (U1, 2), (B1, 1), (B1, 2)]
LAYERS += [(n, i) for n in (B0, F0, A0) for i in range(2)] + [(F1, 0), (F1, 1), (A1, 1)]
SHARED = {U1: B1, F1: A1}


def odd_cell():
    return ((iota(0) + iota(1)) & 1) == 1


def face_rows(first, second):
    sub = iota(0)
    out = []
    for near, far in (first, second):
        out.append((jnp.where(sub < 5, near[U1], sroll(near[F1], 5)), jnp.where(sub < 5, sroll(far[U1], -3), far[F1])))
        out.append((jnp.where(sub < 5, near[B1], sroll(near[A1], 5)), jnp.where(sub < 5, sroll(far[B1], -3), far[A1])))
        out.append((jnp.where(sub < 4, near[B0], sroll(near[F0], 4)), jnp.where(sub < 4, sroll(far[B0], 4), far[F0])))
    (n0, f0), (n1, f1) = first, second
    lo = jnp.where(sub < 4, n0[A0], sroll(n1[A0], 4))
    hi = jnp.where(sub < 4, sroll(f0[A0], 4), f1[A0])
    return out + [(lo, hi)]


def face_lanes(first, second):
    lane = iota(1)
    place = lane & 63
    both = []
    for w, tiles in enumerate((first, second)):
        at = 0
        ends = []
        for n in range(7):
            ends.append((lroll(tiles[n], 64 * w + at + WIDTH[n]), at + 2 * WIDTH[n]))
            at += 2 * WIDTH[n]
        group = ends[-1][0]
        for tile, end in reversed(ends[:-1]):
            group = jnp.where(place < end, tile, group)
        both.append(group)
    return jnp.where(lane < 64, both[0], both[1])


def assemble_kernel(
    plan, f0, f1, f2, f3, r0, r1, r2, home, even, odd, y_even, y_odd, z_face, ubox, uhalf, rows8, raw, tmp, sems
):
    fields = (f1, f2, f3)
    gots = (r0, r1, r2)
    rows = pl.ds(3 * BOX, HALF)
    for q in range(PER_DEV):
        source = plan[q]

        @pl.when(source < 4)
        def _():
            box = jnp.minimum(source, 3)
            pltpu.make_async_copy(f0.at[box], ubox.at[q], sems.at[3, q]).start()
            for f in range(3):
                pltpu.make_async_copy(fields[f].at[box], raw.at[f, q], sems.at[f, q]).start()

        for k in range(ROUNDS):

            @pl.when(source == 4 + k)
            def _():
                pltpu.make_async_copy(gots[k].at[rows], uhalf.at[q], sems.at[3, q]).start()
                for f in range(3):
                    pltpu.make_async_copy(gots[k].at[pl.ds(f * BOX, BOX)], raw.at[f, q], sems.at[f, q]).start()

    lane = iota(1)
    m64 = (lane & 64) != 0
    m32 = (lane & 32) != 0
    is_odd = odd_cell()

    def relayout(load):
        for t in range(4):
            for jj in range(2):
                j = 2 * t + jj
                a = [load(k, slice(j * 128, (j + 1) * 128)) for k in range(4)]
                n02 = lroll(jnp.where(m64, a[0], a[2]), 64)
                n13 = lroll(jnp.where(m64, a[1], a[3]), 64)
                n0, n2 = jnp.where(m64, n02, a[0]), jnp.where(m64, a[2], n02)
                n1, n3 = jnp.where(m64, n13, a[1]), jnp.where(m64, a[3], n13)
                b = [
                    jnp.where(m32, lroll(n1, 32), n0),
                    jnp.where(m32, n1, lroll(n0, 96)),
                    jnp.where(m32, lroll(n3, 32), n2),
                    jnp.where(m32, n3, lroll(n2, 96)),
                ]
                for q in range(4):
                    y = jj * 4 + q
                    tmp[t, y * 8 : y * 8 + 8, :] = b[q]

    for f in range(3):
        for q in range(PER_DEV):
            pltpu.make_async_copy(f0.at[0], raw.at[f, q], sems.at[f, q]).wait()

        def step(i, carry):
            xt = pl.multiple_of(i * 8, 8)
            relayout(lambda k, lanes: raw[f, k, pl.ds(xt, 8), lanes])
            for t in range(4):
                ys = slice(t * 8, t * 8 + 8)
                for x in range(0, 8, 2):
                    lower = tmp[t, pl.ds(x, 8, stride=8), :]
                    upper = tmp[t, pl.ds(x + 1, 8, stride=8), :]
                    j = i * 4 + x // 2
                    home[(F1, A1, B1)[f], j, ys, :] = jnp.where(is_odd, lower, upper)
                    home[(F0, A0, B0)[f], j, ys, :] = jnp.where(is_odd, upper, lower)
            return carry

        lax.fori_loop(0, 4, step, 0, unroll=2)

    for q in range(PER_DEV):
        mine = plan[q] < 4

        @pl.when(mine)
        def _():
            pltpu.make_async_copy(f0.at[0], ubox.at[q], sems.at[3, q]).wait()
            halve(ubox.at[q], rows8.at[q], uhalf.at[q])

        @pl.when(jnp.logical_not(mine))
        def _():
            pltpu.make_async_copy(r0.at[rows], uhalf.at[q], sems.at[3, q]).wait()

    for i in range(2):
        relayout(lambda k, lanes: uhalf[k, 8 * i : 8 * i + 8, lanes])
        for t in range(4):
            for x in range(8):
                home[U1, i * 8 + x, t * 8 : t * 8 + 8, :] = tmp[t, pl.ds(x, 8, stride=8), :]

    low = (lax.axis_index("gx") & 1) == 1
    for k, (n, i) in enumerate(LAYERS):
        count = 3 if n < 2 else 2
        low_side, high_side = count - 1 - i, HALF - count + i
        for t in range(4):
            ys = slice(t * 8, t * 8 + 8)
            lo, hi = home[n, low_side, ys, :], home[n, high_side, ys, :]
            if i == 0 and n in SHARED:
                lo = jnp.where(is_odd, lo, lroll(home[SHARED[n], low_side, ys, :], 1))
                hi = jnp.where(is_odd, lroll(home[SHARED[n], high_side, ys, :], 1), hi)
            even[k, ys, :] = jnp.where(low, lo, hi)
            odd[k, ys, :] = jnp.where(low, hi, lo)

    low_y = (lax.axis_index("gy") & 1) == 1

    def faces(m, carry):
        tiles = [[[home[n, 2 * m + i, 8 * t : 8 * t + 8, :] for n in range(7)] for t in range(4)] for i in range(2)]
        for w, (lo, hi) in enumerate(face_rows(*[(tiles[i][0], tiles[i][3]) for i in range(2)])):
            y_even[7 * m + w] = jnp.where(low_y, lo, hi)
            y_odd[7 * m + w] = jnp.where(low_y, hi, lo)
        for i in range(2):
            for v in range(2):
                z_face[2 * m + i, v] = face_lanes(tiles[i][2 * v], tiles[i][2 * v + 1])
        return carry

    lax.fori_loop(0, HALF // 2, faces, 0)


def assemble(plan, fields, gots):
    any_spec = pl.BlockSpec(memory_space=pl.ANY)
    hbm = pl.BlockSpec(memory_space=pltpu.HBM)
    vmem = pl.BlockSpec(memory_space=pltpu.VMEM)
    face = jax.ShapeDtypeStruct((len(LAYERS), BOX, 128), F32)
    rows = jax.ShapeDtypeStruct((7 * HALF // 2, 8, 128), F32)
    return pl.pallas_call(
        assemble_kernel,
        out_shape=(
            jax.ShapeDtypeStruct((7, HALF, BOX, 128), F32),
            face,
            face,
            rows,
            rows,
            jax.ShapeDtypeStruct((HALF, 2, 8, 128), F32),
        ),
        in_specs=[pl.BlockSpec(memory_space=pltpu.SMEM)] + [hbm] * 4 + [any_spec] * 3,
        out_specs=(vmem,) * 6,
        scratch_shapes=[
            pltpu.VMEM((PER_DEV, BOX, BOX * BOX), F32),
            pltpu.VMEM((PER_DEV, HALF, BOX * BOX), F32),
            pltpu.VMEM((PER_DEV, 8, BOX, 128), F32),
            pltpu.VMEM((3, PER_DEV, BOX, BOX * BOX), F32),
            pltpu.VMEM((4, 64, 128), F32),
            pltpu.SemaphoreType.DMA((4, PER_DEV)),
        ],
        compiler_params=pltpu.CompilerParams(vmem_limit_bytes=12 * MIB),
        name="assemble",
    )(plan, *fields, *gots)


def halo_of(axis, count, even, odd):
    i = lax.axis_index(axis)
    low_first = (i & 1) == 1
    low = jnp.where(i > 0, jnp.where(low_first, even, odd), 0.0)
    high = jnp.where(i < count - 1, jnp.where(low_first, odd, even), 0.0)
    return low, high


def x_halo_tiles(even, odd, t):
    ys = slice(t * 8, t * 8 + 8)
    pairs = {}
    for k, (n, i) in enumerate(LAYERS):
        low, high = halo_of("gx", N_GX, even[k, ys, :], odd[k, ys, :])
        count = 3 if n < 2 else 2
        spots = (SIDE - count + i, SIDE + HALF + count - 1 - i)
        for spot, tile in zip(spots, (low, high)):
            pairs.setdefault(spot, {})[n] = tile
            if i == 0 and n in SHARED:
                pairs[spot][SHARED[n]] = lroll(tile, -1)
    return pairs


EDGES = (1, 2, SIDE + HALF, SIDE + HALF + 1)


def edge_y_kernel(x_even, x_odd, even, odd):
    low = (lax.axis_index("gy") & 1) == 1
    near, far = x_halo_tiles(x_even, x_odd, 0), x_halo_tiles(x_even, x_odd, 3)
    for m in range(2):
        for w, (lo, hi) in enumerate(face_rows(*[(near[k], far[k]) for k in EDGES[2 * m : 2 * m + 2]])):
            even[7 * m + w] = jnp.where(low, lo, hi)
            odd[7 * m + w] = jnp.where(low, hi, lo)


PAD = (8, 8, 8, 0, 0, 0, 0)


def edge_z_kernel(home, x_even, x_odd, y_even, y_odd, e_even, e_odd, u1, b1, b0, f0, a0, f1, a1, edge):
    outs = (u1, b1, b0, f0, a0, f1, a1)

    def halo(even, odd, m, pairs):
        low_high = [halo_of("gy", N_GY, even[7 * m + w], odd[7 * m + w]) for w in range(7)]
        l3, h3 = low_high[6]
        for i, k in enumerate(pairs):
            (l0, h0), (l1, h1), (l2, h2) = low_high[3 * i : 3 * i + 3]
            lows = (sroll(l0, 3), sroll(l1, 3), sroll(l2, 4), l2, sroll(l3, 4) if i == 0 else l3, l0, l1)
            highs = (h0, h1, h2, sroll(h2, 4), h3 if i == 0 else sroll(h3, 4), sroll(h0, 3), sroll(h1, 3))
            for n in range(7):
                outs[n][k, PAD[n] : PAD[n] + 8, :] = lows[n]
                outs[n][k, PAD[n] + 40 : PAD[n] + 48, :] = highs[n]

    def tiles(k, t):
        return [outs[n][k, PAD[n] + t * 8 : PAD[n] + t * 8 + 8, :] for n in range(7)]

    def copy(m, carry):
        for i in range(2):
            for n in range(7):
                outs[n][2 * m + i + SIDE, PAD[n] + 8 : PAD[n] + 40, :] = home[n, 2 * m + i]
        halo(y_even, y_odd, m, (2 * m + SIDE, 2 * m + SIDE + 1))
        for i in range(2):
            k = 2 * m + i + SIDE
            edge[12 + 2 * m + i] = face_lanes(tiles(k, 0), tiles(k, 5))
        return carry

    lax.fori_loop(0, HALF // 2, copy, 0)
    for t in range(4):
        for k, fields in x_halo_tiles(x_even, x_odd, t).items():
            for n, tile in fields.items():
                outs[n][k, PAD[n] + 8 + t * 8 : PAD[n] + 16 + t * 8, :] = tile
    for m in range(2):
        halo(e_even, e_odd, m, EDGES[2 * m : 2 * m + 2])
    for i, k in enumerate(EDGES):
        for v in range(3):
            edge[3 * i + v] = face_lanes(tiles(k, 2 * v), tiles(k, 2 * v + 1))


def sweep_kernel(
    u1, b1, b0, f0, a0, f1, a1, z_even, z_odd, e_even, e_odd, sol, res, um0, um1, ua0, ua1, ba0, ba1, fax, co, dg
):
    lane = iota(1)
    first, last = lane == 0, lane == 127
    place = lane & 63
    is_odd = odd_cell()
    u = ((um0, ua0), (um1, ua1))
    b = ((b0, ba0), (b1, ba1))
    fa = (((f0, a0), (fax.at[0], fax.at[1])), ((f1, a1), (fax.at[2], fax.at[3])))
    starts = [2 * sum(WIDTH[:n]) for n in range(7)]
    high_part = functools.reduce(
        jnp.logical_or, [(place >= starts[n]) & (place < starts[n] + WIDTH[n]) for n in range(7)]
    )
    aux = (ua1, ba1, ba0, fax.at[0], fax.at[1], fax.at[2], fax.at[3])

    def unpack(k, even, odd, spots):
        low, high = halo_of("gz", N_GZ, even, odd)
        both = jnp.where(high_part, low, high)
        for w, t in enumerate(spots):
            for n in range(7):
                aux[n][k, PAD[n] + t * 8 : PAD[n] + t * 8 + 8, :] = lroll(both, -(64 * w + starts[n] + WIDTH[n]))

    def unpack_pair(j, carry):
        for v in range(2):
            unpack(j + SIDE, z_even[j, v], z_odd[j, v], (1 + 2 * v, 2 + 2 * v))
        unpack(j + SIDE, e_even[12 + j], e_odd[12 + j], (0, 5))
        return carry

    um1[...] = u1[...]
    lax.fori_loop(0, HALF, unpack_pair, 0, unroll=4)
    for i, k in enumerate(EDGES):
        for v in range(3):
            unpack(k, e_even[3 * i + v], e_odd[3 * i + v], (2 * v, 2 * v + 1))

    def around(c, field, k, t, spans):
        r = 8 + t * 8
        main, side = field[1 - c]
        m, a = main[k, r : r + 8, :], side[k, r : r + 8, :]
        m1, a1 = lroll(m, 1), lroll(a, 1)
        m2, a2 = lroll(m, 127), lroll(a, 127)
        below = (jnp.where(first, a1, m1), jnp.where(first, m1, a1))
        above = (jnp.where(last, a2, m2), jnp.where(last, m2, a2))
        out = []
        for s in spans:
            ref = (main, side)[s]
            back, ahead = ref[k - 1, r : r + 8, :], ref[k + 1, r : r + 8, :]
            beside = jnp.where(is_odd, back, ahead) if c else jnp.where(is_odd, ahead, back)
            out.append(((m, a)[s], beside, ref[k, r - 1 : r + 7, :], ref[k, r + 1 : r + 9, :], below[s], above[s]))
        return out

    def coefs(k, carry):
        for c in range(2):
            for t in range(6):
                rows = slice(t * 8, 8 + t * 8)
                near = around(c, b, k, t, (0, 1))
                for s in range(2):
                    mid = b[c][s][k, 8 + t * 8 : 16 + t * 8, :]
                    f, a = [ref[k, rows, :] for ref in fa[c][s]]
                    faces = [0.5 * (mid + v) for v in near[s]]
                    diag = a + (faces[0] + faces[1]) + (faces[2] + faces[3]) + (faces[4] + faces[5])
                    inverse = jnp.where(mid > 0, 1.0 / diag, 0.0)
                    for n in range(6):
                        co[c, s, n, k - 1, rows, :] = faces[n] * inverse
                    co[c, s, 6, k - 1, rows, :] = f * inverse
                    if s == 0:
                        dg[c, k - 1, rows, :] = diag
        return carry

    lax.fori_loop(1, PAIRS - 1, coefs, 0, unroll=4)

    def update(c, k, t, spans):
        rows = slice(t * 8, 8 + t * 8)
        new = []
        for s, v in zip(spans, around(c, u, k, t, spans)):
            w = [co[c, s, n, k - 1, rows, :] for n in range(7)]
            x = w[0] * v[0] + w[1] * v[1]
            y = w[2] * v[2] + w[3] * v[3]
            z = w[4] * v[4] + w[5] * v[5]
            new.append(w[6] + ((x + y) + z))
        return new

    for half in range(2 * SWEEPS):
        c = half % 2

        def sweep(k, carry):
            for t in range(6):
                for s, new in enumerate(update(c, k, t, (0, 1))):
                    u[c][s][k, 8 + t * 8 : 16 + t * 8, :] = new
            return carry

        out = half // 2
        lax.fori_loop(1 + out, PAIRS - 1 - out, sweep, 0, unroll=6 if out else 5)

    def finish(j, carry):
        k = j + SIDE
        for t in range(1, 5):
            ys = slice(t * 8 - 8, t * 8)
            rows = slice(t * 8, t * 8 + 8)
            now = [u[c][0][k, 8 + t * 8 : 16 + t * 8, :] for c in range(2)]
            rest = [dg[c, k - 1, rows, :] * (update(c, k, t, (0,))[0] - now[c]) for c in range(2)]
            for ref, (v0, v1) in ((sol, now), (res, rest)):
                ref[2 * j, ys, :] = jnp.where(is_odd, v1, v0)
                ref[2 * j + 1, ys, :] = jnp.where(is_odd, v0, v1)
        return carry

    lax.fori_loop(0, HALF, finish, 0, unroll=4)


def on_vmem(kernel, out_shape, scratch, name, limit, *args):
    vmem = pl.BlockSpec(memory_space=pltpu.VMEM)
    return pl.pallas_call(
        kernel,
        out_shape=out_shape,
        in_specs=[vmem] * len(args),
        out_specs=tuple([vmem] * len(out_shape)),
        scratch_shapes=scratch,
        compiler_params=pltpu.CompilerParams(vmem_limit_bytes=limit * MIB),
        name=name,
    )(*args)


def edge_y(x_even, x_odd):
    face = jax.ShapeDtypeStruct((14, 8, 128), F32)
    return on_vmem(edge_y_kernel, (face, face), [], "edge_y", 10, x_even, x_odd)


def edge_z(*args):
    grown = [jax.ShapeDtypeStruct((PAIRS, 48 + 2 * PAD[n], 128), F32) for n in range(7)]
    face = jax.ShapeDtypeStruct((12 + HALF, 8, 128), F32)
    return on_vmem(edge_z_kernel, (*grown, face), [], "edge_z", 16, *args)


def sweeps(grown, *faces):
    block = jax.ShapeDtypeStruct((BOX, BOX, 128), F32)
    padded = pltpu.VMEM((PAIRS, 64, 128), F32)
    scratch = [padded] * 6 + [
        pltpu.VMEM((4, PAIRS, 48, 128), F32),
        pltpu.VMEM((2, 2, 7, PAIRS - 2, 48, 128), F32),
        pltpu.VMEM((2, PAIRS - 2, 48, 128), F32),
    ]
    return on_vmem(sweep_kernel, (block, block), scratch, "sweeps", 40, *grown, *faces)


def exchange(axis, count, even, odd):
    pairs = []
    for start in (0, 1):
        step = []
        for i in range(start, count, 2):
            j = (i + 1) % count
            step += [(i, j), (j, i)]
        pairs.append(step)
    return lax.ppermute(even, axis, pairs[0]), lax.ppermute(odd, axis, pairs[1])


def per_device(solution_old, right_side, acoef, bcoef, corners):
    fields = (solution_old, right_side, acoef, bcoef)
    go0, go1, go2, plan, *pays = plan_and_pack(corners, fields)
    gots = [swap_round(go.reshape(()), pay) for go, pay in zip((go0, go1, go2), pays)]
    home, even, odd, near_even, near_odd, face = assemble(plan, fields, gots)
    x = exchange("gx", N_GX, even, odd)
    y = exchange("gy", N_GY, near_even, near_odd)
    z = exchange("gz", N_GZ, face, face)
    y_edges = exchange("gy", N_GY, *edge_y(*x))
    *grown, edge = edge_z(home, *x, *y, *y_edges)
    return sweeps(grown, *z, *exchange("gz", N_GZ, edge, edge))


def solution(mesh):
    boxes = P(("gx", "gy", "gz"), None, None)
    block = P("gx", "gy", "gz")
    return jax.shard_map(
        per_device,
        mesh=mesh,
        in_specs=(boxes, boxes, boxes, boxes, P()),
        out_specs=(block, block),
        check_vma=False,
    )
```
